32 devices in a mesh: ctx: 16 (over z, y, x), tp: 2 (over core).
Axes of the slice: x: 2, y: 2, z: 4, core: 2. Of those that a mesh axis runs over, the one named last changes fastest.
Arguments:
- tokens: bfloat16 [8192, 5120], P('ctx', 'tp'), may hold values from -6 to 6
- norm_gain: float32 [5120], replicated, may hold values from 0.1 to 1.9
- w_query: bfloat16 [5120, 5120], P('ctx', 'tp'), may hold values from -0.078125 to 0.078125
- cache_keys: bfloat16 [8192, 1024], P('ctx', 'tp'), may hold values from -100 to 100
- cache_values: bfloat16 [8192, 1024], P('ctx', 'tp'), may hold values from -6 to 6
- doc_start: int32 [8192], P('ctx'), may hold values from 0 to 8191, as said below
- tile_mask: int32 [64, 64], P('ctx'), may hold values from 0 to 1, as said below
Outputs:
- attended: bfloat16 [8192, 5120], P('ctx', 'tp')
The draws below stay inside these ranges and needn't reach their ends.
Inputs may be any that keep to these rules, and one draw needn't show every extreme that they name: Documents are contiguous: doc_start is the same within a document and i - 2048 < doc_start[i] <= i; some document has exactly 2048 tokens. `tile_mask`: every diagonal tile is 1.
All inputs are finite; a program needn't handle non-finite values.
Results may differ from the reference program's by a relative error of at most 0.012.
The reference program's roundings to bfloat16 on the way (of `normed`, `queries` and `probs`) count: a program that leaves them out, or rounds other values in their place, can miss the bound.
Values may be sent and summed in bfloat16 or wider, within the bound.
No kernel may reach another device: no remote copies, remote signals or barrier semaphores. Data moves between devices by JAX's collectives and lax.ppermute only.
A program may use at most 256 MiB of HBM per device.

```python
import jax
import jax.numpy as jnp
from jax import lax

D = 5120
H = 40
KVH = 8
HD = 128
TOK_DEV = 512
TILE = 128
MAXDOC = 2048
REACH = 4
SEQ = 8192
TILES = 64


def draw_cache_keys(key, part):
    drawn = jnp.clip(jax.random.normal(key, (SEQ, KVH * HD), jnp.float32), -6.0, 6.0)
    return drawn.astype(jnp.bfloat16)


def draw_doc_start(key, part):
    length_key = jax.random.fold_in(key, 21)
    place_key = jax.random.fold_in(key, 22)
    lengths = jax.random.randint(length_key, (SEQ,), 1, MAXDOC + 1, jnp.int32)
    forced = jax.random.randint(place_key, (), 0, 2, jnp.int32)
    lengths = jnp.where(jnp.arange(SEQ, dtype=jnp.int32) == forced, MAXDOC, lengths).astype(jnp.int32)
    ends = jnp.cumsum(lengths).astype(jnp.int32)
    starts = ends - lengths
    position = jnp.arange(SEQ, dtype=jnp.int32)
    doc_index = jnp.searchsorted(ends, position, side='right').astype(jnp.int32)
    return starts[doc_index].astype(jnp.int32)


def draw_tile_mask(key, part):
    drawn = (jax.random.randint(jax.random.fold_in(key, 31), (TILES, TILES), 0, 4, jnp.int32) > 0).astype(jnp.int32)
    diagonal = jnp.arange(TILES, dtype=jnp.int32)
    return jnp.where(diagonal[:, None] == diagonal[None, :], 1, drawn).astype(jnp.int32)


def shard_levels(rng, shape, split, smallest, high):
    level, own = 1.0, jax.random.fold_in(rng, 6)
    for axis_at, parts in split:
        heights = jnp.exp(jax.random.uniform(jax.random.fold_in(own, axis_at), (parts,), jnp.float32, smallest / len(split), high / len(split)))
        level = level * jnp.repeat(heights, shape[axis_at] // parts).reshape([-1 if axis == axis_at else 1 for axis in range(len(shape))])
    return level


def gaussian(rng, dims, scale, limit, cuts=(), kind=jnp.bfloat16):
    entries = jax.random.normal(rng, dims, jnp.float32) * scale
    if len(cuts) > 0:
        entries = shard_levels(rng, dims, cuts, -0.22, 0.18) * entries
    return jnp.clip(entries, min=-limit, max=limit).astype(kind)


def setup_inputs(seed: int = 0) -> dict:
    splits = jax.random.split(jax.random.key(seed), 8)
    tokens = gaussian(splits[0], (SEQ, D), 1.0, 6.0, ((0, 16), (1, 2)))
    norm_gain = jnp.clip(1.0 + 0.18 * jax.random.normal(splits[1], (D,), jnp.float32), 0.1, 1.9)
    w_query = gaussian(splits[2], (D, H * HD), D ** -0.5, 0.078125, ((0, 16), (1, 2)))
    cache_keys = draw_cache_keys(jax.random.fold_in(splits[7], 71), 0)
    cache_values = gaussian(splits[4], (SEQ, KVH * HD), 1.0, 6.0, ((0, 16), (1, 2)))
    doc_start = draw_doc_start(jax.random.fold_in(splits[7], 71), 0)
    tile_mask = draw_tile_mask(jax.random.fold_in(splits[7], 71), 0)
    return {"tokens": tokens, "norm_gain": norm_gain, "w_query": w_query, "cache_keys": cache_keys, "cache_values": cache_values, "doc_start": doc_start, "tile_mask": tile_mask}


epsilon = 1e-05

def reference(tokens, norm_gain, w_query, cache_keys, cache_values, doc_start, tile_mask):
    float_tokens = tokens.astype(jnp.float32)
    inverse = lax.rsqrt(lax.optimization_barrier(jnp.mean(float_tokens * float_tokens, axis=-1, keepdims=True)) + epsilon)
    normed = (float_tokens * inverse * norm_gain).astype(jnp.bfloat16)
    queries = jnp.dot(normed, w_query, preferred_element_type=jnp.float32).astype(jnp.bfloat16)
    group_size = H // KVH
    pad_rows = REACH * TOK_DEV
    window = (REACH + 1) * TOK_DEV
    tiles_dev = TOK_DEV // TILE
    key_pad = jnp.concatenate([jnp.zeros((pad_rows, KVH * HD), jnp.bfloat16), cache_keys], axis=0)
    value_pad = jnp.concatenate([jnp.zeros((pad_rows, KVH * HD), jnp.bfloat16), cache_values], axis=0)
    mask_pad = jnp.concatenate([jnp.zeros((TILES, REACH * tiles_dev), jnp.int32), tile_mask], axis=1)
    score_scale = 1.0 / HD ** 0.5

    def one_block(block_index):
        first = (block_index * TOK_DEV).astype(jnp.int32)
        query_blk = lax.dynamic_slice_in_dim(queries, first, TOK_DEV, 0)
        query_blk = query_blk.reshape(TOK_DEV, KVH, group_size, HD).astype(jnp.float32)
        key_win = lax.dynamic_slice_in_dim(key_pad, first, window, 0).reshape(window, KVH, HD).astype(jnp.float32)
        value_win = lax.dynamic_slice_in_dim(value_pad, first, window, 0).reshape(window, KVH, HD).astype(jnp.float32)
        query_start = lax.dynamic_slice_in_dim(doc_start, first, TOK_DEV, 0)
        tile_rows = lax.dynamic_slice_in_dim(mask_pad, (block_index * tiles_dev).astype(jnp.int32), tiles_dev, 0)
        tile_block = lax.dynamic_slice_in_dim(tile_rows, (block_index * tiles_dev).astype(jnp.int32), (REACH + 1) * tiles_dev, 1)
        expanded = jnp.repeat(jnp.repeat(tile_block, TILE, axis=0), TILE, axis=1)
        query_pos = first + jnp.arange(TOK_DEV, dtype=jnp.int32)
        key_pos = first - pad_rows + jnp.arange(window, dtype=jnp.int32)
        visible = (key_pos[None, :] <= query_pos[:, None]) & (key_pos[None, :] >= query_start[:, None]) & (expanded == 1)
        scores = jnp.einsum('qkgd,pkd->kgqp', query_blk, key_win) * score_scale
        masked = jnp.where(visible, scores, -1e+30)
        row_max = lax.optimization_barrier(jnp.max(masked, axis=-1, keepdims=True))
        weights = jnp.where(visible, jnp.exp(masked - row_max), 0.0)
        weight_sum = lax.optimization_barrier(jnp.sum(weights, axis=-1))
        probs = lax.optimization_barrier(weights.astype(jnp.bfloat16)).astype(jnp.float32)
        summed = jnp.einsum('kgqp,pkd->qkgd', probs, value_win)
        normal = jnp.transpose(weight_sum, (2, 0, 1))[..., None]
        return (summed / normal).reshape(TOK_DEV, H * HD).astype(jnp.bfloat16)
    blocks = lax.map(one_block, jnp.arange(SEQ // TOK_DEV, dtype=jnp.int32))
    return blocks.reshape(SEQ, H * HD)
```

```python
import functools
import math

import jax
import jax.numpy as jnp
from jax import lax
from jax.experimental import pallas as pl
from jax.experimental.pallas import tpu as pltpu
from jax.sharding import PartitionSpec as P

HD = 128
TILE = 128
MAXDOC = 2048
KEYS = 256
MASKED = -1e30


epsilon = 1e-05
exp2_scale = math.log2(math.e) / HD**0.5


def block_kernel(
    info,
    parts,
    source_rows,
    depth,
    shard_rows,
    *refs,
):
    (doc_smem, tile_smem) = refs[:2]
    token_refs = refs[2 : 2 + parts]
    w_hbm, kv_ref, doc_ref, out_ref, w_ref, query_ref, acc_ref, max_ref, sum_ref, sem = refs[2 + parts :]
    rows = out_ref.shape[0]
    heads = out_ref.shape[1] // HD
    blocks = w_hbm.shape[0]
    swap = info[3]
    group = info[4]

    def fetch(at):
        canonical = (at // group) * group + lax.bitwise_xor(lax.rem(at, group), swap)
        first = pl.multiple_of(canonical * source_rows, 16)
        return pltpu.make_async_copy(w_hbm.at[at], w_ref.at[pl.ds(first, source_rows)], sem.at[at])

    for at in range(blocks):
        fetch(at).start()
    for at in range(blocks):
        fetch(at).wait()

    step = 256
    for first in range(0, rows, step):
        total = None
        for part in range(parts):
            half = lax.bitwise_xor(info[5], part)
            piece = jnp.dot(
                token_refs[part][first : first + step, :],
                w_ref[pl.ds(pl.multiple_of(half * depth, 16), depth), :],
                preferred_element_type=jnp.float32,
            )
            total = piece if total is None else total + piece
        rounded = total.astype(jnp.bfloat16)
        for tile in range(first // TILE, (first + step) // TILE):
            for head in range(heads):
                at = (tile * heads + head) * TILE
                query_ref[at : at + TILE, :] = rounded[
                    tile * TILE - first : (tile + 1) * TILE - first, head * HD : (head + 1) * HD
                ]

    stacked = heads * TILE
    tiles_shard = shard_rows // TILE

    def one_tile(tile, carry):
        query = query_ref[pl.ds(pl.multiple_of(tile * stacked, stacked), stacked), :]
        row_in_window = info[0] + tile * TILE
        row_first = info[1] + row_in_window
        docs_first = doc_smem[tile * TILE]
        docs_last = doc_smem[tile * TILE + TILE - 1]
        docs = doc_ref[pl.ds(pl.multiple_of(tile * TILE, TILE), TILE), :]
        last = row_in_window // KEYS
        first = lax.max(docs_first - info[1], 0) // KEYS

        def scores_of(block):
            shard = (block * KEYS) // shard_rows
            slot = (shard // group) * group + lax.bitwise_xor(lax.rem(shard, group), swap)
            at = pl.multiple_of(lax.rem(block * KEYS, shard_rows), KEYS)
            keys = kv_ref[slot, 0, pl.ds(at, KEYS), :]
            values = kv_ref[slot, 1, pl.ds(at, KEYS), :]
            scores = lax.dot_general(query, keys, (((1,), (1,)), ((), ())), preferred_element_type=jnp.float32)
            return scores, values

        def mask_of(scores, block, bits):
            lane = lax.broadcasted_iota(jnp.int32, (TILE, KEYS), 1)
            key_pos = info[1] + block * KEYS + lane
            query_pos = row_first + lax.broadcasted_iota(jnp.int32, (TILE, KEYS), 0)
            open_tile = jnp.zeros((TILE, KEYS), jnp.int32)
            for k in range(KEYS // TILE):
                open_tile = jnp.where(lane >= k * TILE, bits[k], open_tile)
            visible = (key_pos <= query_pos) & (key_pos >= docs) & (open_tile == 1)
            return jnp.where(visible[None], scores.reshape(heads, TILE, KEYS), MASKED).reshape(stacked, KEYS)

        def fold(weights):
            total = weights[:, :TILE]
            for k in range(1, KEYS // TILE):
                total = total + weights[:, k * TILE : (k + 1) * TILE]
            return total

        def update(scores, values):
            old = max_ref[...]
            new = jnp.maximum(old, jnp.max(scores, axis=1, keepdims=True))
            alpha = jnp.exp2((old - new) * exp2_scale)
            shift = jnp.concatenate([new * exp2_scale] * (KEYS // HD), axis=1)
            weights = jnp.exp2(scores * exp2_scale - shift)
            max_ref[...] = new
            sum_ref[...] = sum_ref[...] * alpha + fold(weights)
            product = jnp.dot(weights.astype(jnp.bfloat16), values, preferred_element_type=jnp.float32)
            acc_ref[...] = acc_ref[...] * alpha + product

        def bits_of(block):
            first_tile = info[1] // TILE + block * (KEYS // TILE)
            width = tile_smem.shape[1]
            bits = []
            for k in range(KEYS // TILE):
                at = lax.min(lax.max(first_tile + k, 0), width - 1)
                bits.append(tile_smem[tile, at])
            return bits

        max_ref[...] = jnp.full(max_ref.shape, MASKED, jnp.float32)
        sum_ref[...] = jnp.zeros(sum_ref.shape, jnp.float32)
        acc_ref[...] = jnp.zeros(acc_ref.shape, jnp.float32)

        def one_block(back, carry):
            block = last - back
            bits = bits_of(block)
            some, every = bits[0], bits[0]
            for bit in bits[1:]:
                some, every = lax.max(some, bit), lax.min(every, bit)
            key_first = info[1] + block * KEYS
            whole = (every == 1) & (key_first + KEYS - 1 <= row_first) & (key_first >= docs_last)

            @pl.when((some == 1) & whole)
            def _():
                scores, values = scores_of(block)
                update(scores, values)

            @pl.when((some == 1) & jnp.logical_not(whole))
            def _():
                scores, values = scores_of(block)
                update(mask_of(scores, block, bits), values)

            return carry

        lax.fori_loop(0, last - first + 1, one_block, 0)
        result = acc_ref[...] / jnp.sum(sum_ref[...], axis=1, keepdims=True)
        for head in range(heads):
            out_ref[pl.ds(pl.multiple_of(tile * TILE, TILE), TILE), head * HD : (head + 1) * HD] = result[
                head * TILE : (head + 1) * TILE
            ].astype(out_ref.dtype)
        return carry

    lax.fori_loop(0, rows // TILE, one_tile, 0)


def attend(info, docs, tiles, token_parts, w_blocks, kv_window, shard_rows):
    rows = token_parts[0].shape[0]
    depth = token_parts[0].shape[1]
    columns = w_blocks.shape[2]
    heads = columns // HD
    parts = len(token_parts)
    vmem = pl.BlockSpec(memory_space=pltpu.VMEM)
    smem = pl.BlockSpec(memory_space=pltpu.SMEM)

    def kernel(info_ref, *refs):
        block_kernel(info_ref, parts, w_blocks.shape[1], depth, shard_rows, *refs)

    return pl.pallas_call(
        kernel,
        out_shape=jax.ShapeDtypeStruct((rows, columns), jnp.bfloat16),
        in_specs=[smem, smem, smem] + [vmem] * parts + [pl.BlockSpec(memory_space=pl.ANY), vmem, vmem],
        out_specs=vmem,
        scratch_shapes=[
            pltpu.VMEM((w_blocks.shape[0] * w_blocks.shape[1], columns), jnp.bfloat16),
            pltpu.VMEM((rows * heads, HD), jnp.bfloat16),
            pltpu.VMEM((heads * TILE, HD), jnp.float32),
            pltpu.VMEM((heads * TILE, HD), jnp.float32),
            pltpu.VMEM((heads * TILE, HD), jnp.float32),
            pltpu.SemaphoreType.DMA((w_blocks.shape[0],)),
        ],
        compiler_params=pltpu.CompilerParams(vmem_limit_bytes=44 << 20),
        cost_estimate=pl.CostEstimate(
            flops=2 * rows * depth * parts * columns + 4 * rows * columns * 1024,
            bytes_accessed=2 * (rows * depth * parts + w_blocks.size + kv_window.size + rows * columns),
            transcendentals=rows * heads * 1024,
        ),
    )(info, docs, tiles, *token_parts, w_blocks, kv_window, docs.reshape(rows, 1))


def planar(tokens, norm_gain, w_query, cache_keys, cache_values, doc_start, tile_mask, group):
    devices = lax.axis_size("ctx")
    index = lax.axis_index("ctx")
    core = lax.axis_index("tp")
    place = lax.rem(index, group)
    tok_rows, width = tokens.shape
    w_rows, columns = w_query.shape
    kv_width = cache_keys.shape[1] // group
    q_width = columns // group
    rows = group * tok_rows
    groups = [[first + k for k in range(group)] for first in range(0, devices, group)]
    lines = [[first + k for first in range(0, devices, group)] for k in range(group)]

    def swapped(block, distance):
        return lax.ppermute(block, "ctx", [(i, i ^ distance) for i in range(devices)])

    def other_core(block):
        return lax.ppermute(block, "tp", [(0, 1), (1, 0)])

    def columns_for(array, distance, size):
        return lax.dynamic_slice_in_dim(array, lax.bitwise_xor(place, distance) * size, size, 1)

    w_plane = [columns_for(w_query, 0, q_width)]
    for distance in range(1, group):
        w_plane.append(swapped(columns_for(w_query, distance, q_width), distance))
    w_blocks = lax.all_gather(jnp.stack(w_plane), "ctx", axis=0, tiled=True, axis_index_groups=lines)

    float_tokens = tokens.astype(jnp.float32)
    squares = jnp.sum(float_tokens * float_tokens, axis=-1)
    squares = squares + other_core(squares)
    inverse = lax.rsqrt(squares / (2 * width) + epsilon)
    gain = lax.dynamic_slice_in_dim(norm_gain, core * width, width, 0)
    normed = (float_tokens * inverse[:, None] * gain).astype(jnp.bfloat16)

    half = width // 2
    from_x, from_y = swapped(normed, 1), swapped(normed, 2)
    token_halves = {
        0: normed,
        1: from_x,
        2: from_y,
        3: jnp.concatenate([swapped(from_y[:, :half], 1), swapped(from_x[:, half:], 2)], axis=1),
    }

    def kv_for(distance):
        return jnp.stack([columns_for(cache_keys, distance, kv_width), columns_for(cache_values, distance, kv_width)])

    kv_own = jnp.stack([kv_for(0)] + [swapped(kv_for(distance), distance) for distance in range(1, group)])
    kv_before = lax.ppermute(kv_own, "ctx", [(i, i + group) for i in range(devices - group)])
    kv_window = jnp.concatenate([kv_before, kv_own])

    tile_rows, tile_columns = tile_mask.shape
    marks = lax.all_gather(
        jnp.concatenate([doc_start, tile_mask.reshape(-1)]), "ctx", axis=0, axis_index_groups=groups
    )
    window_first = (index // group - 1) * rows

    outs = {}
    for distance in (3, 2, 1, 0):
        source = lax.bitwise_xor(place, distance)
        mark = lax.dynamic_index_in_dim(marks, source, 0, keepdims=False)
        docs, tiles = mark[:tok_rows], mark[tok_rows:].reshape(tile_rows, tile_columns)
        info = jnp.stack(
            [rows + source * tok_rows, window_first, jnp.int32(0), place, jnp.int32(group), core]
        ).astype(jnp.int32)
        mine = token_halves[distance]
        block = attend(info, docs, tiles, [mine, other_core(mine)], w_blocks, kv_window, tok_rows)
        outs[distance] = swapped(block, distance) if distance else block
    ordered = []
    for k in range(group):
        distance = lax.bitwise_xor(place, k)
        chosen = outs[0]
        for other in range(1, group):
            chosen = jnp.where(distance == other, outs[other], chosen)
        ordered.append(chosen)
    return jnp.concatenate(ordered, axis=1)


def plain(tokens, norm_gain, w_query, cache_keys, cache_values, doc_start, tile_mask):
    devices = lax.axis_size("ctx")
    index = lax.axis_index("ctx")
    tok_rows = tokens.shape[0]
    float_tokens = lax.all_gather(tokens, "tp", axis=1, tiled=True).astype(jnp.float32)
    inverse = lax.rsqrt(jnp.mean(float_tokens * float_tokens, axis=-1, keepdims=True) + epsilon)
    normed = (float_tokens * inverse * norm_gain).astype(jnp.bfloat16)
    kv_heads = cache_keys.shape[1] // HD
    q_width = w_query.shape[1] // kv_heads
    w_blocks = lax.all_gather(w_query, "ctx", axis=0)
    reach = (MAXDOC + tok_rows - 2) // tok_rows
    kv_own = jnp.stack([cache_keys, cache_values])
    shards = [
        lax.ppermute(kv_own, "ctx", [(i, i + distance) for i in range(devices - distance)])
        for distance in range(reach, 0, -1)
    ]
    kv_window = jnp.stack(shards + [kv_own])
    zero = jnp.int32(0)
    info = jnp.stack(
        [jnp.int32(reach * tok_rows), (index - reach) * tok_rows, zero, zero, jnp.int32(1), zero]
    ).astype(jnp.int32)
    outs = [
        attend(
            info,
            doc_start,
            tile_mask,
            [normed],
            w_blocks[:, :, head * q_width : (head + 1) * q_width],
            kv_window[:, :, :, head * HD : (head + 1) * HD],
            tok_rows,
        )
        for head in range(kv_heads)
    ]
    return outs[0] if kv_heads == 1 else jnp.concatenate(outs, axis=1)


def on_device(*arrays):
    kv_heads = arrays[3].shape[1] // HD
    group = 4
    rows = group * arrays[0].shape[0]
    if kv_heads == group and lax.axis_size("ctx") % group == 0 and lax.axis_size("tp") == 2 and rows >= MAXDOC - 1:
        return planar(*arrays, group)
    return plain(*arrays)


def solution(mesh):
    return jax.shard_map(
        on_device,
        mesh=mesh,
        in_specs=(
            P("ctx", "tp"),
            P(),
            P("ctx", "tp"),
            P("ctx", "tp"),
            P("ctx", "tp"),
            P("ctx"),
            P("ctx", None),
        ),
        out_specs=P("ctx", "tp"),
        check_vma=False,
    )
```

```python
import math

import jax
import jax.numpy as jnp
from jax import lax
from jax.experimental import pallas as pl
from jax.experimental.pallas import tpu as pltpu
from jax.sharding import PartitionSpec as P

HD = 128
TILE = 128
MAXDOC = 2048
KEYS = 256
CHUNKS = 4
MASKED = -1e30


epsilon = 1e-05
exp2_scale = math.log2(math.e) / HD**0.5


def block_kernel(counts, source_rows, shard_rows, info, doc_smem, tile_smem, doc_ref, *refs):
    parts, w_count, kv_count, deltas = counts
    token_hbm, w_hbm, kv_hbm = refs[:parts], refs[parts : parts + w_count], refs[parts + w_count :][:kv_count]
    out_ref, token_ref, w_ref, kv_ref, total_ref, query_ref, doc_full, acc_ref, max_ref, sum_ref = refs[
        parts + w_count + kv_count :
    ][:10]
    token_sem, w_sem, kv_sem = refs[-3:]
    rows = out_ref.shape[0]
    heads = out_ref.shape[1] // HD
    depth = w_ref.shape[0]
    group = w_hbm[0].shape[0]
    blocks = depth // source_rows
    halves = kv_hbm[0].shape[0]
    swap = info[3]
    chunk = depth // CHUNKS
    chunks_part = CHUNKS // parts

    def token_copy(part, at, place):
        target = pl.ds(pl.multiple_of(place * chunk, 128), chunk)
        return pltpu.make_async_copy(
            token_hbm[part].at[:, at * chunk : (at + 1) * chunk], token_ref.at[:, target], token_sem.at[place]
        )

    def w_copy(ref, at, place):
        target = pl.ds(pl.multiple_of(place * source_rows, 16), source_rows)
        return pltpu.make_async_copy(ref.at[at], w_ref.at[target], w_sem.at[place])

    def kv_copy(ref, half, place):
        return pltpu.make_async_copy(ref.at[half], kv_ref.at[place], kv_sem.at[place])

    for part in range(parts):
        for at in range(chunks_part):
            token_copy(part, at, lax.bitwise_xor(info[4], part) * chunks_part + at).start()
    for ref, delta in zip(w_hbm, deltas):
        place = info[2] + delta

        @pl.when((place >= 0) & (place < blocks // group))
        def _():
            for at in range(group):
                w_copy(ref, at, place * group + lax.bitwise_xor(swap, at)).start()

    for at in range(kv_count):
        for half in range(halves):
            kv_copy(kv_hbm[at], half, half * kv_count + lax.bitwise_xor(swap, at)).start()

    for k in range(CHUNKS):
        token_copy(0, 0, k).wait()
        for place in range(k * (blocks // CHUNKS), (k + 1) * (blocks // CHUNKS)):
            w_copy(w_hbm[0], 0, place).wait()
        piece = jnp.dot(
            token_ref[:, k * chunk : (k + 1) * chunk],
            w_ref[k * chunk : (k + 1) * chunk, :],
            preferred_element_type=jnp.float32,
        )
        if k == 0:
            total_ref[...] = piece
        else:
            total_ref[...] += piece
    for tile in range(rows // TILE):
        for head in range(heads):
            at = (tile * heads + head) * TILE
            query_ref[at : at + TILE, :] = total_ref[
                tile * TILE : (tile + 1) * TILE, head * HD : (head + 1) * HD
            ].astype(jnp.bfloat16)
    for at in range(kv_count * halves):
        kv_copy(kv_hbm[0], 0, at).wait()

    stacked = heads * TILE

    def one_tile(tile, carry):
        query = query_ref[pl.ds(pl.multiple_of(tile * stacked, stacked), stacked), :]
        row_in_window = info[0] + tile * TILE
        row_first = info[1] + row_in_window
        docs_first = doc_smem[tile, 0]
        docs_last = doc_smem[tile, TILE - 1]
        docs_row = doc_ref[pl.ds(tile, 1), :].astype(jnp.float32)
        doc_full[...] = jnp.transpose(jnp.broadcast_to(docs_row, (TILE, TILE))).astype(jnp.int32)
        last = row_in_window // KEYS
        first = lax.max(docs_first - info[1], 0) // KEYS

        def scores_of(block):
            slot = (block * KEYS) // shard_rows
            at = pl.multiple_of(lax.rem(block * KEYS, shard_rows), KEYS)
            keys = kv_ref[slot, 0, pl.ds(at, KEYS), :]
            values = kv_ref[slot, 1, pl.ds(at, KEYS), :]
            scores = lax.dot_general(query, keys, (((1,), (1,)), ((), ())), preferred_element_type=jnp.float32)
            return scores, values

        def mask_of(scores, block, bits):
            lane = lax.broadcasted_iota(jnp.int32, (TILE, KEYS), 1)
            key_pos = info[1] + block * KEYS + lane
            query_pos = row_first + lax.broadcasted_iota(jnp.int32, (TILE, KEYS), 0)
            docs = jnp.concatenate([doc_full[...]] * (KEYS // TILE), axis=1)
            open_tile = jnp.zeros((TILE, KEYS), jnp.int32)
            for k in range(KEYS // TILE):
                open_tile = jnp.where(lane >= k * TILE, bits[k], open_tile)
            visible = (key_pos <= query_pos) & (key_pos >= docs) & (open_tile == 1)
            return jnp.where(visible[None], scores.reshape(heads, TILE, KEYS), MASKED).reshape(stacked, KEYS)

        def fold(weights):
            total = weights[:, :TILE]
            for k in range(1, KEYS // TILE):
                total = total + weights[:, k * TILE : (k + 1) * TILE]
            return total

        def update(scores, values):
            old = max_ref[...]
            new = jnp.maximum(old, jnp.max(scores, axis=1, keepdims=True))
            alpha = jnp.exp2((old - new) * exp2_scale)
            shift = jnp.concatenate([new * exp2_scale] * (KEYS // HD), axis=1)
            weights = jnp.exp2(scores * exp2_scale - shift)
            max_ref[...] = new
            sum_ref[...] = sum_ref[...] * alpha + fold(weights)
            product = jnp.dot(weights.astype(jnp.bfloat16), values, preferred_element_type=jnp.float32)
            acc_ref[...] = acc_ref[...] * alpha + product

        def bits_of(block):
            first_tile = info[1] // TILE + block * (KEYS // TILE)
            width = tile_smem.shape[1]
            bits = []
            for k in range(KEYS // TILE):
                at = lax.min(lax.max(first_tile + k, 0), width - 1)
                bits.append(tile_smem[tile, at])
            return bits

        max_ref[...] = jnp.full(max_ref.shape, MASKED, jnp.float32)
        sum_ref[...] = jnp.zeros(sum_ref.shape, jnp.float32)
        acc_ref[...] = jnp.zeros(acc_ref.shape, jnp.float32)

        def one_block(back, carry):
            block = last - back
            bits = bits_of(block)
            some, every = bits[0], bits[0]
            for bit in bits[1:]:
                some, every = lax.max(some, bit), lax.min(every, bit)
            key_first = info[1] + block * KEYS
            whole = (every == 1) & (key_first + KEYS - 1 <= row_first) & (key_first >= docs_last)

            @pl.when((some == 1) & whole)
            def _():
                scores, values = scores_of(block)
                update(scores, values)

            @pl.when((some == 1) & jnp.logical_not(whole))
            def _():
                scores, values = scores_of(block)
                update(mask_of(scores, block, bits), values)

            return carry

        lax.fori_loop(0, last - first + 1, one_block, 0)
        result = acc_ref[...] / jnp.sum(sum_ref[...], axis=1, keepdims=True)
        for head in range(heads):
            out_ref[pl.ds(pl.multiple_of(tile * TILE, TILE), TILE), head * HD : (head + 1) * HD] = result[
                head * TILE : (head + 1) * TILE
            ].astype(out_ref.dtype)
        return carry

    lax.fori_loop(0, rows // TILE, one_tile, 0)


def attend(info, docs, tiles, token_parts, w_parts, deltas, kv_parts):
    rows = token_parts[0].shape[0]
    depth = token_parts[0].shape[1] * len(token_parts)
    source_rows, columns = w_parts[0].shape[1:]
    heads = columns // HD
    shard_rows = kv_parts[0].shape[2]
    shards = len(kv_parts) * kv_parts[0].shape[0]
    blocks = depth // source_rows
    vmem = pl.BlockSpec(memory_space=pltpu.VMEM)
    smem = pl.BlockSpec(memory_space=pltpu.SMEM)
    leave = pl.BlockSpec(memory_space=pl.ANY)
    docs = docs.reshape(rows // TILE, TILE)
    arrays = [*token_parts, *w_parts, *kv_parts]
    counts = (len(token_parts), len(w_parts), len(kv_parts), tuple(deltas))

    def kernel(*refs):
        block_kernel(counts, source_rows, shard_rows, *refs)

    return pl.pallas_call(
        kernel,
        out_shape=jax.ShapeDtypeStruct((rows, columns), jnp.bfloat16),
        in_specs=[smem, smem, smem, vmem] + [leave] * len(arrays),
        out_specs=vmem,
        scratch_shapes=[
            pltpu.VMEM((rows, depth), jnp.bfloat16),
            pltpu.VMEM((depth, columns), jnp.bfloat16),
            pltpu.VMEM((shards, 2, shard_rows, HD), jnp.bfloat16),
            pltpu.VMEM((rows, columns), jnp.float32),
            pltpu.VMEM((rows * heads, HD), jnp.bfloat16),
            pltpu.VMEM((TILE, TILE), jnp.int32),
            pltpu.VMEM((heads * TILE, HD), jnp.float32),
            pltpu.VMEM((heads * TILE, HD), jnp.float32),
            pltpu.VMEM((heads * TILE, HD), jnp.float32),
            pltpu.SemaphoreType.DMA((CHUNKS,)),
            pltpu.SemaphoreType.DMA((blocks,)),
            pltpu.SemaphoreType.DMA((shards,)),
        ],
        compiler_params=pltpu.CompilerParams(vmem_limit_bytes=40 << 20),
        cost_estimate=pl.CostEstimate(
            flops=2 * rows * depth * columns + 4 * rows * columns * 1024,
            bytes_accessed=2 * (rows * depth + depth * columns + shards * 2 * shard_rows * HD + rows * columns),
            transcendentals=rows * heads * 1024,
        ),
    )(info, docs, tiles, docs, *arrays)


def planar(tokens, norm_gain, w_query, cache_keys, cache_values, doc_start, tile_mask, group):
    devices = lax.axis_size("ctx")
    index = lax.axis_index("ctx")
    core = lax.axis_index("tp")
    place = lax.rem(index, group)
    tok_rows, width = tokens.shape
    kv_width = cache_keys.shape[1] // group
    q_width = w_query.shape[1] // group
    rows = group * tok_rows
    lines = devices // group

    def swapped(block, distance):
        return lax.ppermute(block, "ctx", [(i, i ^ distance) for i in range(devices)])

    def along(block, step):
        route = [(i, i + step * group) for i in range(devices) if 0 <= i + step * group < devices]
        return lax.ppermute(block, "ctx", route)

    def other_core(block):
        return lax.ppermute(block, "tp", [(0, 1), (1, 0)])

    def columns_for(array, distance, size, axis):
        return lax.dynamic_slice_in_dim(array, lax.bitwise_xor(place, distance) * size, size, axis)

    kv_own = jnp.stack([cache_keys, cache_values])
    kv_two = jnp.stack([along(kv_own, 1), kv_own])

    w_plane = [columns_for(w_query, 0, q_width, 1)]
    for distance in range(1, group):
        w_plane.append(swapped(columns_for(w_query, distance, q_width, 1), distance))

    float_tokens = tokens.astype(jnp.float32)
    squares = jnp.sum(float_tokens * float_tokens, axis=-1)
    squares = squares + other_core(squares)
    inverse = lax.rsqrt(squares / (2 * width) + epsilon)
    gain = lax.dynamic_slice_in_dim(norm_gain, core * width, width, 0)
    normed = (float_tokens * inverse[:, None] * gain).astype(jnp.bfloat16)

    marks = [jnp.concatenate([doc_start, tile_mask.reshape(-1)])]
    for distance in range(1, group):
        marks.append(swapped(marks[0], distance))

    half = width // 2
    from_x, from_y = swapped(normed, 1), swapped(normed, 2)
    mine = [
        normed,
        from_x,
        from_y,
        jnp.concatenate([swapped(from_y[:, :half], 1), swapped(from_x[:, half:], 2)], axis=1),
    ]
    token_parts = [[part, other_core(part)] for part in mine]

    kv_parts = [columns_for(kv_two, 0, kv_width, 3)]
    for distance in range(1, group):
        kv_parts.append(swapped(columns_for(kv_two, distance, kv_width, 3), distance))

    first_columns = (q_width // HD + 1) // 2 * HD
    w_chunks = []
    for low, high in ((0, first_columns), (first_columns, q_width)):
        own = jnp.stack([block[:, low:high] for block in w_plane])
        chunk, deltas = [own], [0]
        above, below = own, own
        for step in range(1, lines):
            above, below = along(above, 1), along(below, -1)
            chunk += [above, below]
            deltas += [-step, step]
        w_chunks.append((chunk, deltas))

    window_first = (index // group - 1) * rows
    pieces = []
    for number, (chunk, deltas) in enumerate(w_chunks):
        outs = [None] * group
        for distance in (0, 1, 2, 3) if number == 0 else (3, 2, 1, 0):
            source = lax.bitwise_xor(place, distance)
            docs, tiles = marks[distance][:tok_rows], marks[distance][tok_rows:].reshape(tile_mask.shape)
            info = jnp.stack([rows + source * tok_rows, window_first, index // group, place, core]).astype(jnp.int32)
            block = attend(info, docs, tiles, token_parts[distance], chunk, deltas, kv_parts)
            outs[distance] = swapped(block, distance) if distance else block
        pieces.append(outs)
    joined = [jnp.concatenate([outs[distance] for outs in pieces], axis=1) for distance in range(group)]
    ordered = []
    for k in range(group):
        distance = lax.bitwise_xor(place, k)
        chosen = joined[0]
        for other in range(1, group):
            chosen = jnp.where(distance == other, joined[other], chosen)
        ordered.append(chosen)
    return jnp.concatenate(ordered, axis=1)


def plain(tokens, norm_gain, w_query, cache_keys, cache_values, doc_start, tile_mask):
    devices = lax.axis_size("ctx")
    index = lax.axis_index("ctx")
    tok_rows = tokens.shape[0]
    float_tokens = lax.all_gather(tokens, "tp", axis=1, tiled=True).astype(jnp.float32)
    inverse = lax.rsqrt(jnp.mean(float_tokens * float_tokens, axis=-1, keepdims=True) + epsilon)
    normed = (float_tokens * inverse * norm_gain).astype(jnp.bfloat16)
    kv_heads = cache_keys.shape[1] // HD
    q_width = w_query.shape[1] // kv_heads
    w_blocks = lax.all_gather(w_query, "ctx", axis=0)
    reach = (MAXDOC + tok_rows - 2) // tok_rows
    kv_own = jnp.stack([cache_keys, cache_values])
    shards = [
        lax.ppermute(kv_own, "ctx", [(i, i + distance) for i in range(devices - distance)])
        for distance in range(reach, 0, -1)
    ]
    kv_window = jnp.stack(shards + [kv_own])
    zero = jnp.int32(0)
    info = jnp.stack([jnp.int32(reach * tok_rows), (index - reach) * tok_rows, zero, zero, zero]).astype(jnp.int32)
    outs = [
        attend(
            info,
            doc_start,
            tile_mask,
            [normed],
            [w_blocks[:, :, head * q_width : (head + 1) * q_width]],
            [0],
            [kv_window[:, :, :, head * HD : (head + 1) * HD]],
        )
        for head in range(kv_heads)
    ]
    return outs[0] if kv_heads == 1 else jnp.concatenate(outs, axis=1)


def on_device(*arrays):
    kv_heads = arrays[3].shape[1] // HD
    group = 4
    rows = group * arrays[0].shape[0]
    if kv_heads == group and lax.axis_size("ctx") % group == 0 and lax.axis_size("tp") == 2 and rows >= MAXDOC - 1:
        return planar(*arrays, group)
    return plain(*arrays)


def solution(mesh):
    return jax.shard_map(
        on_device,
        mesh=mesh,
        in_specs=(
            P("ctx", "tp"),
            P(),
            P("ctx", "tp"),
            P("ctx", "tp"),
            P("ctx", "tp"),
            P("ctx"),
            P("ctx", None),
        ),
        out_specs=P("ctx", "tp"),
        check_vma=False,
    )
```

```python
import math

import jax
import jax.numpy as jnp
from jax import lax
from jax.experimental import pallas as pl
from jax.experimental.pallas import tpu as pltpu
from jax.sharding import PartitionSpec as P

HD = 128
TILE = 128
MAXDOC = 2048
KEYS = 512
QUERIES = 256
CHUNKS = 4
FAR = 1 << 30
MASKED = -1e30


epsilon = 1e-05
exp2_scale = math.log2(math.e) / HD**0.5


def rows_kernel(counts, distances, shapes, info, marks_smem, marks_ref, *refs):
    parts, kv_count, mask_width = counts
    tok_rows, shard_rows, source_rows = shapes
    n = len(distances)
    token_hbm = [refs[k * parts : (k + 1) * parts] for k in range(n)]
    w_hbm = refs[n * parts]
    kv_hbm = refs[n * parts + 1 :][:kv_count]
    out_hbm = refs[n * parts + 1 + kv_count :][:n]
    scratch = refs[n * parts + 1 + kv_count + n :]
    token_ref, w_ref, key_ref, value_ref, total_ref, query_ref, doc_full, acc_ref, max_ref, sum_ref, out_ref = scratch[:11]
    token_sem, w_sem, kv_sem, out_sem = scratch[11:]
    columns = w_ref.shape[1]
    heads = columns // HD
    depth = w_ref.shape[0]
    blocks = depth // source_rows
    halves = kv_hbm[0].shape[0]
    swap = info[1]
    chunk = depth // CHUNKS
    chunks_part = CHUNKS // parts
    doc_rows = tok_rows // TILE
    window_rows = halves * kv_count * shard_rows
    base = window_rows - kv_count * shard_rows

    def token_copy(ref, at, place, slot):
        target = pl.ds(pl.multiple_of(place * chunk, 128), chunk)
        return pltpu.make_async_copy(
            ref.at[:, at * chunk : (at + 1) * chunk], token_ref.at[slot, :, target], token_sem.at[slot, place]
        )

    def fetch_tokens(k):
        for part in range(parts):
            for at in range(chunks_part):
                token_copy(token_hbm[k][part], at, lax.bitwise_xor(info[2], part) * chunks_part + at, k % 2).start()

    def w_copy(at, place):
        target = pl.ds(pl.multiple_of(place * source_rows, 16), source_rows)
        return pltpu.make_async_copy(w_hbm.at[at], w_ref.at[target], w_sem.at[place])

    def kv_copy(ref, half, which, place):
        target = pl.ds(pl.multiple_of(KEYS + place * shard_rows, 16), shard_rows)
        return pltpu.make_async_copy(
            ref.at[half, which], (key_ref, value_ref)[which].at[target], kv_sem.at[place, which]
        )

    def out_copy(k, slot):
        return pltpu.make_async_copy(out_ref.at[slot], out_hbm[k], out_sem.at[slot])

    fetch_tokens(0)
    for at in range(blocks):
        w_copy(at, lax.bitwise_xor(swap, at)).start()
    for at in range(kv_count):
        for half in range(halves):
            for which in range(2):
                kv_copy(kv_hbm[at], half, which, half * kv_count + lax.bitwise_xor(swap, at)).start()
    key_ref[0:KEYS, :] = jnp.zeros((KEYS, HD), jnp.bfloat16)
    value_ref[0:KEYS, :] = jnp.zeros((KEYS, HD), jnp.bfloat16)

    stacked = heads * QUERIES
    subs = QUERIES // TILE

    def one_rows(k, carry):
        slot = lax.rem(k, 2)
        for ahead in range(1, n):

            @pl.when(k == ahead - 1)
            def _():
                fetch_tokens(ahead)

        for c in range(CHUNKS):
            token_copy(token_hbm[0][0], 0, c, slot).wait()

            @pl.when(k == 0)
            def _():
                for place in range(c * (blocks // CHUNKS), (c + 1) * (blocks // CHUNKS)):
                    w_copy(0, place).wait()

            piece = jnp.dot(
                token_ref[slot, :, c * chunk : (c + 1) * chunk],
                w_ref[c * chunk : (c + 1) * chunk, :],
                preferred_element_type=jnp.float32,
            )
            if c == 0:
                total_ref[...] = piece
            else:
                total_ref[...] += piece
        for tile in range(tok_rows // QUERIES):
            for head in range(heads):
                at = (tile * heads + head) * QUERIES
                query_ref[at : at + QUERIES, :] = total_ref[
                    tile * QUERIES : (tile + 1) * QUERIES, head * HD : (head + 1) * HD
                ].astype(jnp.bfloat16)

        @pl.when(k == 0)
        def _():
            for place in range(kv_count * halves):
                for which in range(2):
                    kv_copy(kv_hbm[0], 0, which, place).wait()

        @pl.when(k >= 2)
        def _():
            out_copy(0, slot).wait()

        distance = jnp.int32(distances[0])
        for other in range(1, n):
            distance = jnp.where(k == other, distances[other], distance)
        rows_first = base + lax.bitwise_xor(swap, distance) * tok_rows

        def one_tile(tile, carry):
            query = query_ref[pl.ds(pl.multiple_of(tile * stacked, stacked), stacked), :]
            row_first = rows_first + tile * QUERIES
            end = row_first + QUERIES
            for sub in range(subs):
                docs_row = marks_ref[k, pl.ds(tile * subs + sub, 1), :].astype(jnp.float32)
                doc_full[sub] = jnp.transpose(jnp.broadcast_to(docs_row, (TILE, TILE))).astype(jnp.int32)
            first_key = marks_smem[k, tile * subs, 0] - info[0]
            count = (end - first_key + KEYS - 1) // KEYS

            def one_block(back, carry):
                start = end - (back + 1) * KEYS
                at = pl.multiple_of(start + KEYS, TILE)
                keys = key_ref[pl.ds(at, KEYS), :]
                values = value_ref[pl.ds(at, KEYS), :]
                scores = lax.dot_general(query, keys, (((1,), (1,)), ((), ())), preferred_element_type=jnp.float32)
                key_tile = (info[0] + start) // TILE
                lane = lax.broadcasted_iota(jnp.int32, (TILE, TILE), 1)
                row = lax.broadcasted_iota(jnp.int32, (TILE, TILE), 0)
                masks = []
                for sub in range(subs):
                    causal = row + (row_first + sub * TILE - start)
                    docs = doc_full[sub] - (info[0] + start)
                    pieces = []
                    for m in range(KEYS // TILE):
                        column = lax.min(lax.max(key_tile + m, 0), mask_width - 1)
                        flat = (tile * subs + sub) * mask_width + column
                        shut = jnp.where(marks_smem[k, doc_rows + flat // TILE, lax.rem(flat, TILE)] == 1, 0, FAR)
                        pieces.append((lane <= causal - m * TILE) & (lane >= docs + (shut - m * TILE)))
                    masks.append(jnp.concatenate(pieces, axis=1))
                visible = jnp.concatenate(masks, axis=0)
                scores = jnp.where(visible[None], scores.reshape(heads, QUERIES, KEYS), MASKED).reshape(stacked, KEYS)
                old = max_ref[...]
                new = jnp.maximum(old, jnp.max(scores, axis=1, keepdims=True))
                alpha = jnp.exp2((old - new) * exp2_scale)
                shift = jnp.concatenate([new * exp2_scale] * (KEYS // HD), axis=1)
                weights = jnp.exp2(scores * exp2_scale - shift)
                max_ref[...] = new
                folded = weights[:, :HD]
                for m in range(1, KEYS // HD):
                    folded = folded + weights[:, m * HD : (m + 1) * HD]
                sum_ref[...] = sum_ref[...] * alpha + folded
                product = jnp.dot(weights.astype(jnp.bfloat16), values, preferred_element_type=jnp.float32)
                acc_ref[...] = acc_ref[...] * alpha + product
                return carry

            max_ref[...] = jnp.full(max_ref.shape, MASKED, jnp.float32)
            sum_ref[...] = jnp.zeros(sum_ref.shape, jnp.float32)
            acc_ref[...] = jnp.zeros(acc_ref.shape, jnp.float32)
            lax.fori_loop(0, count, one_block, 0)
            result = acc_ref[...] / jnp.sum(sum_ref[...], axis=1, keepdims=True)
            for head in range(heads):
                out_ref[slot, pl.ds(pl.multiple_of(tile * QUERIES, QUERIES), QUERIES), head * HD : (head + 1) * HD] = (
                    result[head * QUERIES : (head + 1) * QUERIES].astype(out_ref.dtype)
                )
            return carry

        lax.fori_loop(0, tok_rows // QUERIES, one_tile, 0)
        for at in range(n):

            @pl.when(k == at)
            def _():
                out_copy(at, at % 2).start()

        return carry

    lax.fori_loop(0, n, one_rows, 0)
    for k in range(max(n - 2, 0), n):
        out_copy(k, k % 2).wait()


def attend(info, marks, distances, token_parts, w_blocks, kv_parts, mask_width):
    n = len(distances)
    parts = len(token_parts[0])
    rows = token_parts[0][0].shape[0]
    source_rows, columns = w_blocks.shape[1:]
    depth = w_blocks.shape[0] * source_rows
    heads = columns // HD
    shard_rows = kv_parts[0].shape[2]
    shards = len(kv_parts) * kv_parts[0].shape[0]
    vmem = pl.BlockSpec(memory_space=pltpu.VMEM)
    smem = pl.BlockSpec(memory_space=pltpu.SMEM)
    leave = pl.BlockSpec(memory_space=pl.ANY)
    arrays = [part for block in token_parts for part in block] + [w_blocks] + list(kv_parts)
    counts = (parts, len(kv_parts), mask_width)
    tile_rows = heads * QUERIES

    def kernel(*refs):
        rows_kernel(counts, distances, (rows, shard_rows, source_rows), *refs)

    return pl.pallas_call(
        kernel,
        out_shape=[jax.ShapeDtypeStruct((rows, columns), jnp.bfloat16)] * n,
        in_specs=[smem, smem, vmem] + [leave] * len(arrays),
        out_specs=[leave] * n,
        scratch_shapes=[
            pltpu.VMEM((2, rows, depth), jnp.bfloat16),
            pltpu.VMEM((depth, columns), jnp.bfloat16),
            pltpu.VMEM((KEYS + shards * shard_rows, HD), jnp.bfloat16),
            pltpu.VMEM((KEYS + shards * shard_rows, HD), jnp.bfloat16),
            pltpu.VMEM((rows, columns), jnp.float32),
            pltpu.VMEM((rows * heads, HD), jnp.bfloat16),
            pltpu.VMEM((QUERIES // TILE, TILE, TILE), jnp.int32),
            pltpu.VMEM((tile_rows, HD), jnp.float32),
            pltpu.VMEM((tile_rows, HD), jnp.float32),
            pltpu.VMEM((tile_rows, HD), jnp.float32),
            pltpu.VMEM((2, rows, columns), jnp.bfloat16),
            pltpu.SemaphoreType.DMA((2, CHUNKS)),
            pltpu.SemaphoreType.DMA((w_blocks.shape[0],)),
            pltpu.SemaphoreType.DMA((shards, 2)),
            pltpu.SemaphoreType.DMA((2,)),
        ],
        compiler_params=pltpu.CompilerParams(vmem_limit_bytes=60 << 20),
        cost_estimate=pl.CostEstimate(
            flops=n * (2 * rows * depth * columns + 4 * rows * columns * 1024),
            bytes_accessed=2 * (n * rows * depth + depth * columns + shards * 2 * shard_rows * HD + n * rows * columns),
            transcendentals=n * rows * heads * 1024,
        ),
    )(info, marks, marks, *arrays)


def marks_of(doc_start, tile_mask):
    return jnp.concatenate([doc_start.reshape(-1, TILE), tile_mask.reshape(-1, TILE)])


def planar(tokens, norm_gain, w_query, cache_keys, cache_values, doc_start, tile_mask, group):
    devices = lax.axis_size("ctx")
    index = lax.axis_index("ctx")
    core = lax.axis_index("tp")
    place = lax.rem(index, group)
    tok_rows, width = tokens.shape
    kv_width = cache_keys.shape[1] // group
    q_width = w_query.shape[1] // group
    rows = group * tok_rows
    lines = [[first + k for first in range(0, devices, group)] for k in range(group)]
    far = range(1, group)

    def swapped(block, distance):
        return lax.ppermute(block, "ctx", [(i, i ^ distance) for i in range(devices)])

    def other_core(block):
        return lax.ppermute(block, "tp", [(0, 1), (1, 0)])

    def columns_for(array, distance, first, size, of, axis):
        at = lax.bitwise_xor(place, distance) * of + first
        return lax.dynamic_slice_in_dim(array, at, size, axis)

    def after(values, *earlier):
        flat = lax.optimization_barrier((tuple(values), tuple(earlier)))
        return list(flat[0])

    kv_own = jnp.stack([cache_keys, cache_values])
    first_columns = (q_width // HD + 1) // 2 * HD
    cuts = ((0, first_columns), (first_columns, q_width))

    marks_own = marks_of(doc_start, tile_mask)
    w_first = [columns_for(w_query, d, cuts[0][0], cuts[0][1] - cuts[0][0], q_width, 1) for d in range(group)]
    marks = [marks_own] + [swapped(marks_own, d) for d in far]
    w_first = w_first[:1] + [swapped(w_first[d], d) for d in far]
    kv_before = lax.ppermute(kv_own, "ctx", [(i, i + group) for i in range(devices - group)])

    float_tokens = tokens.astype(jnp.float32)
    squares = jnp.sum(float_tokens * float_tokens, axis=-1)
    squares = squares + other_core(squares)
    inverse = lax.rsqrt(squares / (2 * width) + epsilon)
    gain = lax.dynamic_slice_in_dim(norm_gain, core * width, width, 0)
    normed = (float_tokens * inverse[:, None] * gain).astype(jnp.bfloat16)

    w_stack = jnp.stack(w_first)
    w_chunks = [lax.all_gather(w_stack, "ctx", axis=0, tiled=True, axis_index_groups=lines)]
    w_second = [columns_for(w_query, d, cuts[1][0], cuts[1][1] - cuts[1][0], q_width, 1) for d in range(group)]
    w_second = after(w_second, w_stack, *marks)
    w_second = w_second[:1] + [swapped(w_second[d], d) for d in far]
    w_stack = jnp.stack(w_second)
    (w_after,) = after([w_stack], w_chunks[0])
    w_chunks.append(lax.all_gather(w_after, "ctx", axis=0, tiled=True, axis_index_groups=lines))

    kv_two = jnp.stack([kv_before, kv_own])
    kv_cut = after([columns_for(kv_two, d, 0, kv_width, kv_width, 3) for d in range(group)], w_stack)
    (normed,) = after([normed], w_stack, kv_before)
    kv_parts = kv_cut[:1] + [swapped(kv_cut[d], d) for d in far]
    from_x, from_y = swapped(normed, 1), swapped(normed, 2)
    mine_other = other_core(normed)

    half = width // 2
    relay_y, relay_x = after([from_y[:, :half], from_x[:, half:]], *kv_parts)
    corner_a, corner_b = swapped(relay_y, 1), swapped(relay_x, 2)
    corner = jnp.concatenate([corner_a, corner_b], axis=1)
    mine = [normed, from_x, from_y, corner]
    token_parts = [[normed, mine_other]] + [[mine[d], other_core(mine[d])] for d in far]

    info = jnp.stack([(index // group - 1) * rows, place, core]).astype(jnp.int32)
    width_mask = tile_mask.shape[1]

    def call(distances, chunk, *earlier):
        chosen = [token_parts[d] for d in distances]
        (start,) = after([info], *earlier)
        picked = jnp.stack([marks[d] for d in distances])
        return attend(start, picked, distances, chosen, chunk, kv_parts, width_mask)

    outs = dict(zip((3, 2, 1, 0), call((3, 2, 1, 0), w_chunks[0])))
    pieces = {(d, 0): swapped(out, d) if d else out for d, out in outs.items()}
    outs = dict(zip((3, 2, 1), call((3, 2, 1), w_chunks[1], outs[0])))
    pieces.update({(d, 1): swapped(out, d) for d, out in outs.items()})
    pieces[0, 1] = call((0,), w_chunks[1], outs[1])[0]
    return joined(info, pieces, q_width, [low for low, _ in cuts], group * q_width)


def joined(info, pieces, q_width, lows, columns):
    keys = sorted(pieces)
    rows = pieces[keys[0]].shape[0]
    leave = pl.BlockSpec(memory_space=pl.ANY)

    def kernel(info_ref, *refs):
        out_hbm, sem = refs[-2:]

        def copy(k):
            distance, chunk = keys[k]
            at = pl.multiple_of(lax.bitwise_xor(info_ref[1], distance) * q_width + lows[chunk], HD)
            target = out_hbm.at[:, pl.ds(at, refs[k].shape[1])]
            return pltpu.make_async_copy(refs[k], target, sem.at[k])

        for k in range(len(keys)):
            copy(k).start()
        for k in range(len(keys)):
            copy(k).wait()

    return pl.pallas_call(
        kernel,
        out_shape=jax.ShapeDtypeStruct((rows, columns), jnp.bfloat16),
        in_specs=[pl.BlockSpec(memory_space=pltpu.SMEM)] + [leave] * len(keys),
        out_specs=leave,
        scratch_shapes=[pltpu.SemaphoreType.DMA((len(keys),))],
        cost_estimate=pl.CostEstimate(flops=0, bytes_accessed=4 * rows * columns, transcendentals=0),
    )(info, *[pieces[key] for key in keys])


def plain(tokens, norm_gain, w_query, cache_keys, cache_values, doc_start, tile_mask):
    devices = lax.axis_size("ctx")
    index = lax.axis_index("ctx")
    tok_rows = tokens.shape[0]
    float_tokens = lax.all_gather(tokens, "tp", axis=1, tiled=True).astype(jnp.float32)
    inverse = lax.rsqrt(jnp.mean(float_tokens * float_tokens, axis=-1, keepdims=True) + epsilon)
    normed = (float_tokens * inverse * norm_gain).astype(jnp.bfloat16)
    kv_heads = cache_keys.shape[1] // HD
    q_width = w_query.shape[1] // kv_heads
    w_blocks = lax.all_gather(w_query, "ctx", axis=0)
    reach = (MAXDOC + tok_rows - 2) // tok_rows
    kv_own = jnp.stack([cache_keys, cache_values])
    shards = [
        lax.ppermute(kv_own, "ctx", [(i, i + distance) for i in range(devices - distance)])
        for distance in range(reach, 0, -1)
    ]
    kv_window = jnp.stack(shards + [kv_own])
    info = jnp.stack([(index - reach) * tok_rows, jnp.int32(0), jnp.int32(0)]).astype(jnp.int32)
    marks = marks_of(doc_start, tile_mask)[None]
    outs = [
        attend(
            info,
            marks,
            (0,),
            [[normed]],
            w_blocks[:, :, head * q_width : (head + 1) * q_width],
            [kv_window[:, :, :, head * HD : (head + 1) * HD]],
            tile_mask.shape[1],
        )[0]
        for head in range(kv_heads)
    ]
    return outs[0] if kv_heads == 1 else jnp.concatenate(outs, axis=1)


def on_device(*arrays):
    kv_heads = arrays[3].shape[1] // HD
    group = 4
    rows = group * arrays[0].shape[0]
    if kv_heads == group and lax.axis_size("ctx") % group == 0 and lax.axis_size("tp") == 2 and rows >= MAXDOC - 1:
        return planar(*arrays, group)
    return plain(*arrays)


def solution(mesh):
    return jax.shard_map(
        on_device,
        mesh=mesh,
        in_specs=(
            P("ctx", "tp"),
            P(),
            P("ctx", "tp"),
            P("ctx", "tp"),
            P("ctx", "tp"),
            P("ctx"),
            P("ctx", None),
        ),
        out_specs=P("ctx", "tp"),
        check_vma=False,
    )
```

```python
import math

import jax
import jax.numpy as jnp
from jax import lax
from jax.experimental import pallas as pl
from jax.experimental.pallas import tpu as pltpu
from jax.sharding import PartitionSpec as P

HD = 128
TILE = 128
MAXDOC = 2048
KEYS = 512
QUERIES = 256
CHUNKS = 4
FAR = 1 << 30
MASKED = -1e30


epsilon = 1e-05
exp2_scale = math.log2(math.e) / HD**0.5


def rows_kernel(counts, distances, shapes, info, marks_smem, marks_ref, *refs):
    parts, kv_count, mask_width = counts
    tok_rows, shard_rows, source_rows = shapes
    n = len(distances)
    token_hbm = [refs[k * parts : (k + 1) * parts] for k in range(n)]
    w_hbm = refs[n * parts]
    kv_hbm = refs[n * parts + 1 :][:kv_count]
    out_hbm = refs[n * parts + 1 + kv_count :][:n]
    scratch = refs[n * parts + 1 + kv_count + n :]
    token_ref, w_ref, key_ref, value_ref, total_ref, query_ref, doc_full, acc_ref, max_ref, sum_ref, out_ref = scratch[:11]
    token_sem, w_sem, kv_sem, out_sem = scratch[11:]
    columns = w_ref.shape[1]
    heads = columns // HD
    depth = w_ref.shape[0]
    blocks = depth // source_rows
    halves = kv_hbm[0].shape[0]
    swap = info[1]
    chunk = depth // CHUNKS
    chunks_part = CHUNKS // parts
    doc_rows = tok_rows // TILE
    window_rows = halves * kv_count * shard_rows
    base = window_rows - kv_count * shard_rows

    def token_copy(ref, at, place, slot):
        target = pl.ds(pl.multiple_of(place * chunk, 128), chunk)
        return pltpu.make_async_copy(
            ref.at[:, at * chunk : (at + 1) * chunk], token_ref.at[slot, :, target], token_sem.at[slot, place]
        )

    def fetch_tokens(k):
        for part in range(parts):
            for at in range(chunks_part):
                token_copy(token_hbm[k][part], at, lax.bitwise_xor(info[2], part) * chunks_part + at, k % 2).start()

    def w_copy(at, place):
        target = pl.ds(pl.multiple_of(place * source_rows, 16), source_rows)
        return pltpu.make_async_copy(w_hbm.at[at], w_ref.at[target], w_sem.at[place])

    def kv_copy(ref, half, which, place):
        target = pl.ds(pl.multiple_of(KEYS + place * shard_rows, 16), shard_rows)
        return pltpu.make_async_copy(
            ref.at[half, which], (key_ref, value_ref)[which].at[target], kv_sem.at[place, which]
        )

    def out_copy(k, slot):
        return pltpu.make_async_copy(out_ref.at[slot], out_hbm[k], out_sem.at[slot])

    fetch_tokens(0)
    for at in range(blocks):
        w_copy(at, lax.bitwise_xor(swap, at)).start()
    for at in range(kv_count):
        for half in range(halves):
            for which in range(2):
                kv_copy(kv_hbm[at], half, which, half * kv_count + lax.bitwise_xor(swap, at)).start()
    key_ref[0:KEYS, :] = jnp.zeros((KEYS, HD), jnp.bfloat16)
    value_ref[0:KEYS, :] = jnp.zeros((KEYS, HD), jnp.bfloat16)

    stacked = heads * QUERIES
    subs = QUERIES // TILE

    def one_rows(k, carry):
        slot = lax.rem(k, 2)
        for ahead in range(1, n):

            @pl.when(k == ahead - 1)
            def _():
                fetch_tokens(ahead)

        for c in range(CHUNKS):
            token_copy(token_hbm[0][0], 0, c, slot).wait()

            @pl.when(k == 0)
            def _():
                for place in range(c * (blocks // CHUNKS), (c + 1) * (blocks // CHUNKS)):
                    w_copy(0, place).wait()

            for first in range(0, tok_rows, QUERIES):
                piece = jnp.dot(
                    token_ref[slot, first : first + QUERIES, c * chunk : (c + 1) * chunk],
                    w_ref[c * chunk : (c + 1) * chunk, :],
                    preferred_element_type=jnp.float32,
                )
                if c == 0:
                    total_ref[first : first + QUERIES, :] = piece
                else:
                    total_ref[first : first + QUERIES, :] += piece
        for tile in range(tok_rows // QUERIES):
            for head in range(heads):
                at = (tile * heads + head) * QUERIES
                query_ref[at : at + QUERIES, :] = total_ref[
                    tile * QUERIES : (tile + 1) * QUERIES, head * HD : (head + 1) * HD
                ].astype(jnp.bfloat16)

        @pl.when(k == 0)
        def _():
            for place in range(kv_count * halves):
                for which in range(2):
                    kv_copy(kv_hbm[0], 0, which, place).wait()

        @pl.when(k >= 2)
        def _():
            out_copy(0, slot).wait()

        distance = jnp.int32(distances[0])
        for other in range(1, n):
            distance = jnp.where(k == other, distances[other], distance)
        rows_first = base + lax.bitwise_xor(swap, distance) * tok_rows

        def one_tile(tile, carry):
            query = query_ref[pl.ds(pl.multiple_of(tile * stacked, stacked), stacked), :]
            row_first = rows_first + tile * QUERIES
            end = row_first + QUERIES
            for sub in range(subs):
                docs_row = marks_ref[k, pl.ds(tile * subs + sub, 1), :].astype(jnp.float32)
                doc_full[sub] = jnp.transpose(jnp.broadcast_to(docs_row, (TILE, TILE))).astype(jnp.int32)
            first_key = marks_smem[k, tile * subs, 0] - info[0]
            count = (end - first_key + KEYS - 1) // KEYS

            def one_block(back, carry):
                start = end - (back + 1) * KEYS
                at = pl.multiple_of(start + KEYS, TILE)
                keys = key_ref[pl.ds(at, KEYS), :]
                values = value_ref[pl.ds(at, KEYS), :]
                scores = lax.dot_general(query, keys, (((1,), (1,)), ((), ())), preferred_element_type=jnp.float32)
                key_tile = (info[0] + start) // TILE
                lane = lax.broadcasted_iota(jnp.int32, (TILE, TILE), 1)
                row = lax.broadcasted_iota(jnp.int32, (TILE, TILE), 0)
                masks = []
                for sub in range(subs):
                    causal = row + (row_first + sub * TILE - start)
                    docs = doc_full[sub] - (info[0] + start)
                    pieces = []
                    for m in range(KEYS // TILE):
                        column = lax.min(lax.max(key_tile + m, 0), mask_width - 1)
                        flat = (tile * subs + sub) * mask_width + column
                        shut = jnp.where(marks_smem[k, doc_rows + flat // TILE, lax.rem(flat, TILE)] == 1, 0, FAR)
                        pieces.append((lane <= causal - m * TILE) & (lane >= docs + (shut - m * TILE)))
                    masks.append(jnp.concatenate(pieces, axis=1))
                visible = jnp.concatenate(masks, axis=0)
                scores = jnp.where(visible[None], scores.reshape(heads, QUERIES, KEYS), MASKED).reshape(stacked, KEYS)
                old = max_ref[...]
                new = jnp.maximum(old, jnp.max(scores, axis=1, keepdims=True))
                alpha = jnp.exp2((old - new) * exp2_scale)
                shift = jnp.concatenate([new * exp2_scale] * (KEYS // HD), axis=1)
                weights = jnp.exp2(scores * exp2_scale - shift)
                max_ref[...] = new
                folded = weights[:, :HD]
                for m in range(1, KEYS // HD):
                    folded = folded + weights[:, m * HD : (m + 1) * HD]
                sum_ref[...] = sum_ref[...] * alpha + folded
                product = jnp.dot(weights.astype(jnp.bfloat16), values, preferred_element_type=jnp.float32)
                acc_ref[...] = acc_ref[...] * alpha + product
                return carry

            max_ref[...] = jnp.full(max_ref.shape, MASKED, jnp.float32)
            sum_ref[...] = jnp.zeros(sum_ref.shape, jnp.float32)
            acc_ref[...] = jnp.zeros(acc_ref.shape, jnp.float32)
            lax.fori_loop(0, count, one_block, 0)
            result = acc_ref[...] / jnp.sum(sum_ref[...], axis=1, keepdims=True)
            for head in range(heads):
                out_ref[slot, pl.ds(pl.multiple_of(tile * QUERIES, QUERIES), QUERIES), head * HD : (head + 1) * HD] = (
                    result[head * QUERIES : (head + 1) * QUERIES].astype(out_ref.dtype)
                )
            return carry

        lax.fori_loop(0, tok_rows // QUERIES, one_tile, 0)
        for at in range(n):

            @pl.when(k == at)
            def _():
                out_copy(at, at % 2).start()

        return carry

    lax.fori_loop(0, n, one_rows, 0)
    for k in range(max(n - 2, 0), n):
        out_copy(k, k % 2).wait()


def attend(info, marks, distances, token_parts, w_blocks, kv_parts, mask_width):
    n = len(distances)
    parts = len(token_parts[0])
    rows = token_parts[0][0].shape[0]
    source_rows, columns = w_blocks.shape[1:]
    depth = w_blocks.shape[0] * source_rows
    heads = columns // HD
    shard_rows = kv_parts[0].shape[2]
    shards = len(kv_parts) * kv_parts[0].shape[0]
    vmem = pl.BlockSpec(memory_space=pltpu.VMEM)
    smem = pl.BlockSpec(memory_space=pltpu.SMEM)
    leave = pl.BlockSpec(memory_space=pl.ANY)
    arrays = [part for block in token_parts for part in block] + [w_blocks] + list(kv_parts)
    counts = (parts, len(kv_parts), mask_width)
    tile_rows = heads * QUERIES

    def kernel(*refs):
        rows_kernel(counts, distances, (rows, shard_rows, source_rows), *refs)

    return pl.pallas_call(
        kernel,
        out_shape=[jax.ShapeDtypeStruct((rows, columns), jnp.bfloat16)] * n,
        in_specs=[smem, smem, vmem] + [leave] * len(arrays),
        out_specs=[leave] * n,
        scratch_shapes=[
            pltpu.VMEM((2, rows, depth), jnp.bfloat16),
            pltpu.VMEM((depth, columns), jnp.bfloat16),
            pltpu.VMEM((KEYS + shards * shard_rows, HD), jnp.bfloat16),
            pltpu.VMEM((KEYS + shards * shard_rows, HD), jnp.bfloat16),
            pltpu.VMEM((rows, columns), jnp.float32),
            pltpu.VMEM((rows * heads, HD), jnp.bfloat16),
            pltpu.VMEM((QUERIES // TILE, TILE, TILE), jnp.int32),
            pltpu.VMEM((tile_rows, HD), jnp.float32),
            pltpu.VMEM((tile_rows, HD), jnp.float32),
            pltpu.VMEM((tile_rows, HD), jnp.float32),
            pltpu.VMEM((2, rows, columns), jnp.bfloat16),
            pltpu.SemaphoreType.DMA((2, CHUNKS)),
            pltpu.SemaphoreType.DMA((w_blocks.shape[0],)),
            pltpu.SemaphoreType.DMA((shards, 2)),
            pltpu.SemaphoreType.DMA((2,)),
        ],
        compiler_params=pltpu.CompilerParams(vmem_limit_bytes=60 << 20),
        cost_estimate=pl.CostEstimate(
            flops=n * (2 * rows * depth * columns + 4 * rows * columns * 1024),
            bytes_accessed=2 * (n * rows * depth + depth * columns + shards * 2 * shard_rows * HD + n * rows * columns),
            transcendentals=n * rows * heads * 1024,
        ),
    )(info, marks, marks, *arrays)


def marks_of(doc_start, tile_mask):
    return jnp.concatenate([doc_start.reshape(-1, TILE), tile_mask.reshape(-1, TILE)])


def planar(tokens, norm_gain, w_query, cache_keys, cache_values, doc_start, tile_mask, group):
    devices = lax.axis_size("ctx")
    index = lax.axis_index("ctx")
    core = lax.axis_index("tp")
    place = lax.rem(index, group)
    tok_rows, width = tokens.shape
    kv_width = cache_keys.shape[1] // group
    q_width = w_query.shape[1] // group
    rows = group * tok_rows
    lines = [[first + k for first in range(0, devices, group)] for k in range(group)]
    far = range(1, group)

    def swapped(block, distance):
        return lax.ppermute(block, "ctx", [(i, i ^ distance) for i in range(devices)])

    def other_core(block):
        return lax.ppermute(block, "tp", [(0, 1), (1, 0)])

    def columns_for(array, distance, first, size, of, axis):
        at = lax.bitwise_xor(place, distance) * of + first
        return lax.dynamic_slice_in_dim(array, at, size, axis)

    def after(values, *earlier):
        flat = lax.optimization_barrier((tuple(values), tuple(earlier)))
        return list(flat[0])

    first_columns = (q_width // HD + 1) // 2 * HD
    cuts = ((0, first_columns), (first_columns, q_width))

    marks_own = marks_of(doc_start, tile_mask)
    w_first = [columns_for(w_query, d, cuts[0][0], cuts[0][1] - cuts[0][0], q_width, 1) for d in range(group)]
    w_first = w_first[:1] + [swapped(w_first[d], d) for d in far]
    hop = [(i, i + group) for i in range(devices - group)]
    kv_before = [lax.ppermute(array, "ctx", hop) for array in (cache_keys, cache_values)]
    (marks_sent,) = after([marks_own], *w_first)
    marks = [marks_own] + [swapped(marks_sent, d) for d in far]

    float_tokens = tokens.astype(jnp.float32)
    squares = jnp.sum(float_tokens * float_tokens, axis=-1)
    squares = squares + other_core(squares)
    inverse = lax.rsqrt(squares / (2 * width) + epsilon)
    gain = lax.dynamic_slice_in_dim(norm_gain, core * width, width, 0)
    normed = (float_tokens * inverse[:, None] * gain).astype(jnp.bfloat16)

    w_first = after(w_first, *kv_before)
    w_chunks = [lax.all_gather(jnp.stack(w_first), "ctx", axis=0, tiled=True, axis_index_groups=lines)]

    def kv_for(d):
        arrays = (*kv_before, cache_keys, cache_values)
        return jnp.stack([columns_for(array, d, 0, kv_width, kv_width, 1) for array in arrays]).reshape(
            2, 2, tok_rows, kv_width
        )

    w_second = [columns_for(w_query, d, cuts[1][0], cuts[1][1] - cuts[1][0], q_width, 1) for d in range(group)]
    w_second = after(w_second, *marks)
    w_second = w_second[:1] + [swapped(w_second[d], d) for d in far]
    from_x, from_y = swapped(normed, 1), swapped(normed, 2)
    mine_other = other_core(normed)
    kv_cut = [kv_for(d) for d in range(group)]
    kv_parts = kv_cut[:1] + [swapped(kv_cut[d], d) for d in far]
    (w_after,) = after([jnp.stack(w_second)], *kv_parts)
    w_chunks.append(lax.all_gather(w_after, "ctx", axis=0, tiled=True, axis_index_groups=lines))

    half = width // 2
    relay_y, relay_x = after([from_y, from_x], w_after)
    corner_a, corner_b = swapped(relay_y[:, :half], 1), swapped(relay_x[:, half:], 2)
    corner = jnp.concatenate([corner_a, corner_b], axis=1)
    mine = [normed, from_x, from_y, corner]
    token_parts = [[normed, mine_other]] + [[mine[d], other_core(mine[d])] for d in far]

    info = jnp.stack([(index // group - 1) * rows, place, core]).astype(jnp.int32)
    width_mask = tile_mask.shape[1]

    def call(distances, chunk, *earlier):
        chosen = [token_parts[d] for d in distances]
        (start,) = after([info], *earlier)
        picked = jnp.stack([marks[d] for d in distances])
        return attend(start, picked, distances, chosen, chunk, kv_parts, width_mask)

    pieces, last = {}, ()
    for chunk, distances in ((0, (2, 1, 0)), (0, (3,)), (1, (3, 2, 1)), (1, (0,))):
        outs = call(distances, w_chunks[chunk], *last)
        last = outs[:1]
        pieces.update({(d, chunk): swapped(out, d) if d else out for d, out in zip(distances, outs)})
    return joined(info, pieces, q_width, [low for low, _ in cuts], group * q_width)


def joined(info, pieces, q_width, lows, columns):
    keys = sorted(pieces)
    rows = pieces[keys[0]].shape[0]
    vmem = pl.BlockSpec(memory_space=pltpu.VMEM)

    def kernel(info_ref, *refs):
        out_ref = refs[-1]
        for k, (distance, chunk) in enumerate(keys):
            at = pl.multiple_of(lax.bitwise_xor(info_ref[1], distance) * q_width + lows[chunk], HD)
            out_ref[:, pl.ds(at, refs[k].shape[1])] = refs[k][...]

    return pl.pallas_call(
        kernel,
        out_shape=jax.ShapeDtypeStruct((rows, columns), jnp.bfloat16),
        in_specs=[pl.BlockSpec(memory_space=pltpu.SMEM)] + [vmem] * len(keys),
        out_specs=vmem,
        cost_estimate=pl.CostEstimate(flops=0, bytes_accessed=4 * rows * columns, transcendentals=0),
    )(info, *[pieces[key] for key in keys])


def plain(tokens, norm_gain, w_query, cache_keys, cache_values, doc_start, tile_mask):
    devices = lax.axis_size("ctx")
    index = lax.axis_index("ctx")
    tok_rows = tokens.shape[0]
    float_tokens = lax.all_gather(tokens, "tp", axis=1, tiled=True).astype(jnp.float32)
    inverse = lax.rsqrt(jnp.mean(float_tokens * float_tokens, axis=-1, keepdims=True) + epsilon)
    normed = (float_tokens * inverse * norm_gain).astype(jnp.bfloat16)
    kv_heads = cache_keys.shape[1] // HD
    q_width = w_query.shape[1] // kv_heads
    w_blocks = lax.all_gather(w_query, "ctx", axis=0)
    reach = (MAXDOC + tok_rows - 2) // tok_rows
    kv_own = jnp.stack([cache_keys, cache_values])
    shards = [
        lax.ppermute(kv_own, "ctx", [(i, i + distance) for i in range(devices - distance)])
        for distance in range(reach, 0, -1)
    ]
    kv_window = jnp.stack(shards + [kv_own])
    info = jnp.stack([(index - reach) * tok_rows, jnp.int32(0), jnp.int32(0)]).astype(jnp.int32)
    marks = marks_of(doc_start, tile_mask)[None]
    outs = [
        attend(
            info,
            marks,
            (0,),
            [[normed]],
            w_blocks[:, :, head * q_width : (head + 1) * q_width],
            [kv_window[:, :, :, head * HD : (head + 1) * HD]],
            tile_mask.shape[1],
        )[0]
        for head in range(kv_heads)
    ]
    return outs[0] if kv_heads == 1 else jnp.concatenate(outs, axis=1)


def on_device(*arrays):
    kv_heads = arrays[3].shape[1] // HD
    group = 4
    rows = group * arrays[0].shape[0]
    if kv_heads == group and lax.axis_size("ctx") % group == 0 and lax.axis_size("tp") == 2 and rows >= MAXDOC - 1:
        return planar(*arrays, group)
    return plain(*arrays)


def solution(mesh):
    return jax.shard_map(
        on_device,
        mesh=mesh,
        in_specs=(
            P("ctx", "tp"),
            P(),
            P("ctx", "tp"),
            P("ctx", "tp"),
            P("ctx", "tp"),
            P("ctx"),
            P("ctx", None),
        ),
        out_specs=P("ctx", "tp"),
        check_vma=False,
    )
```

```python
import math

import jax
import jax.numpy as jnp
from jax import lax
from jax.experimental import pallas as pl
from jax.experimental.pallas import tpu as pltpu
from jax.sharding import PartitionSpec as P

HD = 128
TILE = 128
MAXDOC = 2048
KEYS = 512
QUERIES = 256
CHUNKS = 4
FAR = 1 << 30
MASKED = -1e30


epsilon = 1e-05
exp2_scale = math.log2(math.e) / HD**0.5


def rows_kernel(counts, distances, shapes, info, marks_smem, marks_ref, *refs):
    parts, kv_count, mask_width = counts
    tok_rows, shard_rows, source_rows = shapes
    n = len(distances)
    token_hbm = [refs[k * parts : (k + 1) * parts] for k in range(n)]
    w_hbm = refs[n * parts]
    kv_hbm = refs[n * parts + 1 :][:kv_count]
    out_hbm = refs[n * parts + 1 + kv_count :][:n]
    scratch = refs[n * parts + 1 + kv_count + n :]
    token_ref, w_ref, key_ref, value_ref, total_ref, query_ref, doc_full, acc_ref, max_ref, sum_ref, out_ref = scratch[:11]
    token_sem, w_sem, kv_sem, out_sem = scratch[11:]
    columns = w_ref.shape[1]
    heads = columns // HD
    depth = w_ref.shape[0]
    blocks = depth // source_rows
    halves = kv_hbm[0].shape[0]
    swap = info[1]
    chunk = depth // CHUNKS
    chunks_part = CHUNKS // parts
    doc_rows = tok_rows // TILE
    window_rows = halves * kv_count * shard_rows
    base = window_rows - kv_count * shard_rows

    def token_copy(ref, at, c, slot):
        return pltpu.make_async_copy(
            ref.at[:, at * chunk : (at + 1) * chunk],
            token_ref.at[slot, :, c * chunk : (c + 1) * chunk],
            token_sem.at[slot, c],
        )

    def fetch_tokens(k, c):
        token_copy(token_hbm[k][c // chunks_part], c % chunks_part, c, k % 2).start()

    def rows_of(c):
        return lax.bitwise_xor(info[2], c // chunks_part) * chunks_part + c % chunks_part

    def w_copy(at, place):
        target = pl.ds(pl.multiple_of(place * source_rows, 16), source_rows)
        return pltpu.make_async_copy(w_hbm.at[at], w_ref.at[target], w_sem.at[place])

    blocks_chunk = blocks // CHUNKS

    def kv_copy(ref, half, which, place):
        target = pl.ds(pl.multiple_of(KEYS + place * shard_rows, 16), shard_rows)
        return pltpu.make_async_copy(
            ref.at[half, which], (key_ref, value_ref)[which].at[target], kv_sem.at[place, which]
        )

    def out_copy(k, slot):
        return pltpu.make_async_copy(out_ref.at[slot], out_hbm[k], out_sem.at[slot])

    for c in range(CHUNKS):
        fetch_tokens(0, c)
        for at in range(blocks_chunk):
            place = rows_of(c) * blocks_chunk + at
            w_copy(lax.bitwise_xor(swap, place), place).start()
    for at in range(kv_count):
        for half in range(halves):
            for which in range(2):
                kv_copy(kv_hbm[at], half, which, half * kv_count + lax.bitwise_xor(swap, at)).start()
    key_ref[0:KEYS, :] = jnp.zeros((KEYS, HD), jnp.bfloat16)
    value_ref[0:KEYS, :] = jnp.zeros((KEYS, HD), jnp.bfloat16)

    stacked = heads * QUERIES
    subs = QUERIES // TILE

    def one_rows(k, carry):
        slot = lax.rem(k, 2)
        for ahead in range(1, n):

            @pl.when(k == ahead - 1)
            def _():
                for c in range(CHUNKS):
                    fetch_tokens(ahead, c)

        for c in range(CHUNKS):
            token_copy(token_hbm[0][0], 0, c, slot).wait()

            @pl.when(k == 0)
            def _():
                for at in range(blocks_chunk):
                    w_copy(0, rows_of(c) * blocks_chunk + at).wait()

            for first in range(0, tok_rows, QUERIES):
                piece = jnp.dot(
                    token_ref[slot, first : first + QUERIES, c * chunk : (c + 1) * chunk],
                    w_ref[pl.ds(pl.multiple_of(rows_of(c) * chunk, 16), chunk), :],
                    preferred_element_type=jnp.float32,
                )
                if c == 0:
                    total_ref[first : first + QUERIES, :] = piece
                else:
                    total_ref[first : first + QUERIES, :] += piece
        for tile in range(tok_rows // QUERIES):
            for head in range(heads):
                at = (tile * heads + head) * QUERIES
                query_ref[at : at + QUERIES, :] = total_ref[
                    tile * QUERIES : (tile + 1) * QUERIES, head * HD : (head + 1) * HD
                ].astype(jnp.bfloat16)

        @pl.when(k == 0)
        def _():
            for place in range(kv_count * halves):
                for which in range(2):
                    kv_copy(kv_hbm[0], 0, which, place).wait()

        @pl.when(k >= 2)
        def _():
            out_copy(0, slot).wait()

        distance = jnp.int32(distances[0])
        for other in range(1, n):
            distance = jnp.where(k == other, distances[other], distance)
        rows_first = base + lax.bitwise_xor(swap, distance) * tok_rows

        def one_tile(tile, carry):
            query = query_ref[pl.ds(pl.multiple_of(tile * stacked, stacked), stacked), :]
            row_first = rows_first + tile * QUERIES
            end = row_first + QUERIES
            for sub in range(subs):
                docs_row = marks_ref[k, pl.ds(tile * subs + sub, 1), :].astype(jnp.float32)
                doc_full[sub] = jnp.transpose(jnp.broadcast_to(docs_row, (TILE, TILE))).astype(jnp.int32)
            first_key = marks_smem[k, tile * subs, 0] - info[0]
            count = (end - first_key + KEYS - 1) // KEYS

            def one_block(back, carry):
                start = end - (back + 1) * KEYS
                at = pl.multiple_of(start + KEYS, TILE)
                keys = key_ref[pl.ds(at, KEYS), :]
                values = value_ref[pl.ds(at, KEYS), :]
                scores = lax.dot_general(query, keys, (((1,), (1,)), ((), ())), preferred_element_type=jnp.float32)
                key_tile = (info[0] + start) // TILE
                lane = lax.broadcasted_iota(jnp.int32, (TILE, TILE), 1)
                row = lax.broadcasted_iota(jnp.int32, (TILE, TILE), 0)
                masks = []
                for sub in range(subs):
                    causal = row + (row_first + sub * TILE - start)
                    docs = doc_full[sub] - (info[0] + start)
                    pieces = []
                    for m in range(KEYS // TILE):
                        column = lax.min(lax.max(key_tile + m, 0), mask_width - 1)
                        flat = (tile * subs + sub) * mask_width + column
                        shut = jnp.where(marks_smem[k, doc_rows + flat // TILE, lax.rem(flat, TILE)] == 1, 0, FAR)
                        pieces.append((lane <= causal - m * TILE) & (lane >= docs + (shut - m * TILE)))
                    masks.append(jnp.concatenate(pieces, axis=1))
                visible = jnp.concatenate(masks, axis=0)
                scores = jnp.where(visible[None], scores.reshape(heads, QUERIES, KEYS), MASKED).reshape(stacked, KEYS)
                old = max_ref[...]
                new = jnp.maximum(old, jnp.max(scores, axis=1, keepdims=True))
                alpha = jnp.exp2((old - new) * exp2_scale)
                shift = jnp.concatenate([new * exp2_scale] * (KEYS // HD), axis=1)
                weights = jnp.exp2(scores * exp2_scale - shift)
                max_ref[...] = new
                folded = weights[:, :HD]
                for m in range(1, KEYS // HD):
                    folded = folded + weights[:, m * HD : (m + 1) * HD]
                sum_ref[...] = sum_ref[...] * alpha + folded
                product = jnp.dot(weights.astype(jnp.bfloat16), values, preferred_element_type=jnp.float32)
                acc_ref[...] = acc_ref[...] * alpha + product
                return carry

            max_ref[...] = jnp.full(max_ref.shape, MASKED, jnp.float32)
            sum_ref[...] = jnp.zeros(sum_ref.shape, jnp.float32)
            acc_ref[...] = jnp.zeros(acc_ref.shape, jnp.float32)
            lax.fori_loop(0, count, one_block, 0)
            result = acc_ref[...] / jnp.sum(sum_ref[...], axis=1, keepdims=True)
            for head in range(heads):
                out_ref[slot, pl.ds(pl.multiple_of(tile * QUERIES, QUERIES), QUERIES), head * HD : (head + 1) * HD] = (
                    result[head * QUERIES : (head + 1) * QUERIES].astype(out_ref.dtype)
                )
            return carry

        lax.fori_loop(0, tok_rows // QUERIES, one_tile, 0)
        for at in range(n):

            @pl.when(k == at)
            def _():
                out_copy(at, at % 2).start()

        return carry

    lax.fori_loop(0, n, one_rows, 0)
    for k in range(max(n - 2, 0), n):
        out_copy(k, k % 2).wait()


def attend(info, marks, distances, token_parts, w_blocks, kv_parts, mask_width):
    n = len(distances)
    parts = len(token_parts[0])
    rows = token_parts[0][0].shape[0]
    source_rows, columns = w_blocks.shape[1:]
    depth = w_blocks.shape[0] * source_rows
    heads = columns // HD
    shard_rows = kv_parts[0].shape[2]
    shards = len(kv_parts) * kv_parts[0].shape[0]
    vmem = pl.BlockSpec(memory_space=pltpu.VMEM)
    smem = pl.BlockSpec(memory_space=pltpu.SMEM)
    leave = pl.BlockSpec(memory_space=pl.ANY)
    arrays = [part for block in token_parts for part in block] + [w_blocks] + list(kv_parts)
    counts = (parts, len(kv_parts), mask_width)
    tile_rows = heads * QUERIES

    def kernel(*refs):
        rows_kernel(counts, distances, (rows, shard_rows, source_rows), *refs)

    return pl.pallas_call(
        kernel,
        out_shape=[jax.ShapeDtypeStruct((rows, columns), jnp.bfloat16)] * n,
        in_specs=[smem, smem, vmem] + [leave] * len(arrays),
        out_specs=[leave] * n,
        scratch_shapes=[
            pltpu.VMEM((2, rows, depth), jnp.bfloat16),
            pltpu.VMEM((depth, columns), jnp.bfloat16),
            pltpu.VMEM((KEYS + shards * shard_rows, HD), jnp.bfloat16),
            pltpu.VMEM((KEYS + shards * shard_rows, HD), jnp.bfloat16),
            pltpu.VMEM((rows, columns), jnp.float32),
            pltpu.VMEM((rows * heads, HD), jnp.bfloat16),
            pltpu.VMEM((QUERIES // TILE, TILE, TILE), jnp.int32),
            pltpu.VMEM((tile_rows, HD), jnp.float32),
            pltpu.VMEM((tile_rows, HD), jnp.float32),
            pltpu.VMEM((tile_rows, HD), jnp.float32),
            pltpu.VMEM((2, rows, columns), jnp.bfloat16),
            pltpu.SemaphoreType.DMA((2, CHUNKS)),
            pltpu.SemaphoreType.DMA((w_blocks.shape[0],)),
            pltpu.SemaphoreType.DMA((shards, 2)),
            pltpu.SemaphoreType.DMA((2,)),
        ],
        compiler_params=pltpu.CompilerParams(vmem_limit_bytes=60 << 20),
        cost_estimate=pl.CostEstimate(
            flops=n * (2 * rows * depth * columns + 4 * rows * columns * 1024),
            bytes_accessed=2 * (n * rows * depth + depth * columns + shards * 2 * shard_rows * HD + n * rows * columns),
            transcendentals=n * rows * heads * 1024,
        ),
    )(info, marks, marks, *arrays)


def marks_of(doc_start, tile_mask):
    return jnp.concatenate([doc_start.reshape(-1, TILE), tile_mask.reshape(-1, TILE)])


def planar(tokens, norm_gain, w_query, cache_keys, cache_values, doc_start, tile_mask, group):
    devices = lax.axis_size("ctx")
    index = lax.axis_index("ctx")
    core = lax.axis_index("tp")
    place = lax.rem(index, group)
    tok_rows, width = tokens.shape
    kv_width = cache_keys.shape[1] // group
    q_width = w_query.shape[1] // group
    rows = group * tok_rows
    lines = [[first + k for first in range(0, devices, group)] for k in range(group)]
    far = range(1, group)

    def swapped(block, distance):
        return lax.ppermute(block, "ctx", [(i, i ^ distance) for i in range(devices)])

    def other_core(block):
        return lax.ppermute(block, "tp", [(0, 1), (1, 0)])

    def columns_for(array, distance, first, size, of, axis):
        at = lax.bitwise_xor(place, distance) * of + first
        return lax.dynamic_slice_in_dim(array, at, size, axis)

    def after(values, *earlier):
        flat = lax.optimization_barrier((tuple(values), tuple(earlier)))
        return list(flat[0])

    first_columns = (q_width // HD + 1) // 2 * HD
    cuts = ((0, first_columns), (first_columns, q_width))

    marks_own = marks_of(doc_start, tile_mask)
    w_first = [columns_for(w_query, d, cuts[0][0], cuts[0][1] - cuts[0][0], q_width, 1) for d in range(group)]
    w_first = w_first[:1] + [swapped(w_first[d], d) for d in far]
    hop = [(i, i + group) for i in range(devices - group)]
    kv_before = [lax.ppermute(array, "ctx", hop) for array in (cache_keys, cache_values)]
    (marks_sent,) = after([marks_own], *w_first)
    marks = [marks_own] + [swapped(marks_sent, d) for d in far]

    float_tokens = tokens.astype(jnp.float32)
    squares = jnp.sum(float_tokens * float_tokens, axis=-1)
    squares = squares + other_core(squares)
    inverse = lax.rsqrt(squares / (2 * width) + epsilon)
    gain = lax.dynamic_slice_in_dim(norm_gain, core * width, width, 0)
    normed = (float_tokens * inverse[:, None] * gain).astype(jnp.bfloat16)

    w_first = after(w_first, *kv_before)
    w_chunks = [lax.all_gather(jnp.stack(w_first), "ctx", axis=0, tiled=True, axis_index_groups=lines)]

    def kv_for(d):
        arrays = (*kv_before, cache_keys, cache_values)
        return jnp.stack([columns_for(array, d, 0, kv_width, kv_width, 1) for array in arrays]).reshape(
            2, 2, tok_rows, kv_width
        )

    w_second = [columns_for(w_query, d, cuts[1][0], cuts[1][1] - cuts[1][0], q_width, 1) for d in range(group)]
    (normed,) = after([normed], *marks)
    w_second = after(w_second, *marks)
    from_x, from_y = swapped(normed, 1), swapped(normed, 2)
    w_second = w_second[:1] + [swapped(w_second[d], d) for d in far]
    mine_other = other_core(normed)
    kv_cut = [kv_for(d) for d in range(group)]
    kv_parts = kv_cut[:1] + [swapped(kv_cut[d], d) for d in far]
    (w_after,) = after([jnp.stack(w_second)], *kv_parts)
    w_chunks.append(lax.all_gather(w_after, "ctx", axis=0, tiled=True, axis_index_groups=lines))

    half = width // 2
    from_x, from_y = after([from_x, from_y], w_after)
    corner_a, corner_b = swapped(from_y[:, :half], 1), swapped(from_x[:, half:], 2)
    token_parts = [[normed, mine_other]] + [[from_x, other_core(from_x)], [from_y, other_core(from_y)]]

    info = jnp.stack([(index // group - 1) * rows, place, core]).astype(jnp.int32)
    width_mask = tile_mask.shape[1]

    def call(distances, chunk, *earlier):
        chosen = [token_parts[d] for d in distances]
        (start,) = after([info], *earlier)
        picked = jnp.stack([marks[d] for d in distances])
        return attend(start, picked, distances, chosen, chunk, kv_parts, width_mask)

    pieces, last = {}, ()
    for chunk, distances in ((0, (2, 1, 0)), (0, (3,)), (1, (3, 2, 1)), (1, (0,))):
        if distances == (3,):
            corner = jnp.concatenate(after([corner_a, corner_b], *last), axis=1)
            token_parts.append([corner, other_core(corner)])
        outs = call(distances, w_chunks[chunk], *last)
        last = outs[:1]
        pieces.update({(d, chunk): swapped(out, d) if d else out for d, out in zip(distances, outs)})
    return joined(info, pieces, q_width, [low for low, _ in cuts], group * q_width)


def joined(info, pieces, q_width, lows, columns):
    keys = sorted(pieces)
    rows = pieces[keys[0]].shape[0]
    vmem = pl.BlockSpec(memory_space=pltpu.VMEM)

    def kernel(info_ref, *refs):
        out_ref = refs[-1]
        for k, (distance, chunk) in enumerate(keys):
            at = pl.multiple_of(lax.bitwise_xor(info_ref[1], distance) * q_width + lows[chunk], HD)
            out_ref[:, pl.ds(at, refs[k].shape[1])] = refs[k][...]

    return pl.pallas_call(
        kernel,
        out_shape=jax.ShapeDtypeStruct((rows, columns), jnp.bfloat16),
        in_specs=[pl.BlockSpec(memory_space=pltpu.SMEM)] + [vmem] * len(keys),
        out_specs=vmem,
        cost_estimate=pl.CostEstimate(flops=0, bytes_accessed=4 * rows * columns, transcendentals=0),
    )(info, *[pieces[key] for key in keys])


def plain(tokens, norm_gain, w_query, cache_keys, cache_values, doc_start, tile_mask):
    devices = lax.axis_size("ctx")
    index = lax.axis_index("ctx")
    tok_rows = tokens.shape[0]
    float_tokens = lax.all_gather(tokens, "tp", axis=1, tiled=True).astype(jnp.float32)
    inverse = lax.rsqrt(jnp.mean(float_tokens * float_tokens, axis=-1, keepdims=True) + epsilon)
    normed = (float_tokens * inverse * norm_gain).astype(jnp.bfloat16)
    kv_heads = cache_keys.shape[1] // HD
    q_width = w_query.shape[1] // kv_heads
    w_blocks = lax.all_gather(w_query, "ctx", axis=0)
    reach = (MAXDOC + tok_rows - 2) // tok_rows
    kv_own = jnp.stack([cache_keys, cache_values])
    shards = [
        lax.ppermute(kv_own, "ctx", [(i, i + distance) for i in range(devices - distance)])
        for distance in range(reach, 0, -1)
    ]
    kv_window = jnp.stack(shards + [kv_own])
    info = jnp.stack([(index - reach) * tok_rows, jnp.int32(0), jnp.int32(0)]).astype(jnp.int32)
    marks = marks_of(doc_start, tile_mask)[None]
    outs = [
        attend(
            info,
            marks,
            (0,),
            [[normed]],
            w_blocks[:, :, head * q_width : (head + 1) * q_width],
            [kv_window[:, :, :, head * HD : (head + 1) * HD]],
            tile_mask.shape[1],
        )[0]
        for head in range(kv_heads)
    ]
    return outs[0] if kv_heads == 1 else jnp.concatenate(outs, axis=1)


def on_device(*arrays):
    kv_heads = arrays[3].shape[1] // HD
    group = 4
    rows = group * arrays[0].shape[0]
    if kv_heads == group and lax.axis_size("ctx") % group == 0 and lax.axis_size("tp") == 2 and rows >= MAXDOC - 1:
        return planar(*arrays, group)
    return plain(*arrays)


def solution(mesh):
    return jax.shard_map(
        on_device,
        mesh=mesh,
        in_specs=(
            P("ctx", "tp"),
            P(),
            P("ctx", "tp"),
            P("ctx", "tp"),
            P("ctx", "tp"),
            P("ctx"),
            P("ctx", None),
        ),
        out_specs=P("ctx", "tp"),
        check_vma=False,
    )
```

```python
import math

import jax
import jax.numpy as jnp
from jax import lax
from jax.experimental import pallas as pl
from jax.experimental.pallas import tpu as pltpu
from jax.sharding import PartitionSpec as P

HD = 128
TILE = 128
MAXDOC = 2048
KEYS = 512
QUERIES = 256
CHUNKS = 4
FAR = 1 << 30
MASKED = -1e30


epsilon = 1e-05
exp2_scale = math.log2(math.e) / HD**0.5


def rows_kernel(counts, distances, shapes, info, marks_smem, marks_ref, *refs):
    parts, kv_count, mask_width = counts
    tok_rows, shard_rows, source_rows = shapes
    n = len(distances)
    token_hbm = [refs[k * parts : (k + 1) * parts] for k in range(n)]
    w_hbm = refs[n * parts]
    kv_hbm = refs[n * parts + 1 :][:kv_count]
    out_hbm = refs[n * parts + 1 + kv_count :][:n]
    scratch = refs[n * parts + 1 + kv_count + n :]
    token_ref, w_ref, key_ref, value_ref, total_ref, query_ref, doc_full, acc_ref, max_ref, sum_ref, out_ref = scratch[:11]
    token_sem, w_sem, kv_sem, out_sem = scratch[11:]
    columns = w_ref.shape[1]
    heads = columns // HD
    depth = w_ref.shape[0]
    blocks = depth // source_rows
    halves = kv_hbm[0].shape[0]
    swap = info[1]
    chunk = depth // CHUNKS
    chunks_part = CHUNKS // parts
    doc_rows = tok_rows // TILE
    window_rows = halves * kv_count * shard_rows
    base = window_rows - kv_count * shard_rows

    def token_copy(ref, at, c, slot):
        return pltpu.make_async_copy(
            ref.at[:, at * chunk : (at + 1) * chunk],
            token_ref.at[slot, :, c * chunk : (c + 1) * chunk],
            token_sem.at[slot, c],
        )

    def fetch_tokens(k, c):
        token_copy(token_hbm[k][c // chunks_part], c % chunks_part, c, k % 2).start()

    def rows_of(c):
        return lax.bitwise_xor(info[2], c // chunks_part) * chunks_part + c % chunks_part

    def w_copy(at, place):
        target = pl.ds(pl.multiple_of(place * source_rows, 16), source_rows)
        return pltpu.make_async_copy(w_hbm.at[at], w_ref.at[target], w_sem.at[place])

    blocks_chunk = blocks // CHUNKS

    def kv_copy(ref, half, which, place):
        target = pl.ds(pl.multiple_of(KEYS + place * shard_rows, 16), shard_rows)
        return pltpu.make_async_copy(
            ref.at[half, which], (key_ref, value_ref)[which].at[target], kv_sem.at[place, which]
        )

    def out_copy(k, slot):
        return pltpu.make_async_copy(out_ref.at[slot], out_hbm[k], out_sem.at[slot])

    for c in range(CHUNKS):
        fetch_tokens(0, c)
        for at in range(blocks_chunk):
            place = rows_of(c) * blocks_chunk + at
            w_copy(lax.bitwise_xor(swap, place), place).start()
    for at in range(kv_count):
        for half in range(halves):
            for which in range(2):
                kv_copy(kv_hbm[at], half, which, half * kv_count + lax.bitwise_xor(swap, at)).start()
    key_ref[0:KEYS, :] = jnp.zeros((KEYS, HD), jnp.bfloat16)
    value_ref[0:KEYS, :] = jnp.zeros((KEYS, HD), jnp.bfloat16)

    stacked = heads * QUERIES
    subs = QUERIES // TILE

    def one_rows(k, carry):
        slot = lax.rem(k, 2)
        for ahead in range(1, n):

            @pl.when(k == ahead - 1)
            def _():
                for c in range(CHUNKS):
                    fetch_tokens(ahead, c)

        for c in range(CHUNKS):
            token_copy(token_hbm[0][0], 0, c, slot).wait()

            @pl.when(k == 0)
            def _():
                for at in range(blocks_chunk):
                    w_copy(0, rows_of(c) * blocks_chunk + at).wait()

            for first in range(0, tok_rows, QUERIES):
                piece = jnp.dot(
                    token_ref[slot, first : first + QUERIES, c * chunk : (c + 1) * chunk],
                    w_ref[pl.ds(pl.multiple_of(rows_of(c) * chunk, 16), chunk), :],
                    preferred_element_type=jnp.float32,
                )
                if c == 0:
                    total_ref[first : first + QUERIES, :] = piece
                else:
                    total_ref[first : first + QUERIES, :] += piece
        for tile in range(tok_rows // QUERIES):
            for head in range(heads):
                at = (tile * heads + head) * QUERIES
                query_ref[at : at + QUERIES, :] = total_ref[
                    tile * QUERIES : (tile + 1) * QUERIES, head * HD : (head + 1) * HD
                ].astype(jnp.bfloat16)

        @pl.when(k == 0)
        def _():
            for place in range(kv_count * halves):
                for which in range(2):
                    kv_copy(kv_hbm[0], 0, which, place).wait()

        @pl.when(k >= 2)
        def _():
            out_copy(0, slot).wait()

        distance = jnp.int32(distances[0])
        for other in range(1, n):
            distance = jnp.where(k == other, distances[other], distance)
        rows_first = base + lax.bitwise_xor(swap, distance) * tok_rows

        def one_tile(tile, carry):
            query = query_ref[pl.ds(pl.multiple_of(tile * stacked, stacked), stacked), :]
            row_first = rows_first + tile * QUERIES
            end = row_first + QUERIES
            for sub in range(subs):
                docs_row = marks_ref[k, pl.ds(tile * subs + sub, 1), :].astype(jnp.float32)
                doc_full[sub] = jnp.transpose(jnp.broadcast_to(docs_row, (TILE, TILE))).astype(jnp.int32)
            first_key = marks_smem[k, tile * subs, 0] - info[0]
            count = (end - first_key + KEYS - 1) // KEYS

            def one_block(back, carry):
                start = end - (back + 1) * KEYS
                at = pl.multiple_of(start + KEYS, TILE)
                keys = key_ref[pl.ds(at, KEYS), :]
                values = value_ref[pl.ds(at, KEYS), :]
                scores = lax.dot_general(query, keys, (((1,), (1,)), ((), ())), preferred_element_type=jnp.float32)
                key_tile = (info[0] + start) // TILE
                lane = lax.broadcasted_iota(jnp.int32, (TILE, TILE), 1)
                row = lax.broadcasted_iota(jnp.int32, (TILE, TILE), 0)
                masks = []
                for sub in range(subs):
                    causal = row + (row_first + sub * TILE - start)
                    docs = doc_full[sub] - (info[0] + start)
                    pieces = []
                    for m in range(KEYS // TILE):
                        column = lax.min(lax.max(key_tile + m, 0), mask_width - 1)
                        flat = (tile * subs + sub) * mask_width + column
                        shut = jnp.where(marks_smem[k, doc_rows + flat // TILE, lax.rem(flat, TILE)] == 1, 0, FAR)
                        pieces.append((lane <= causal - m * TILE) & (lane >= docs + (shut - m * TILE)))
                    masks.append(jnp.concatenate(pieces, axis=1))
                visible = jnp.concatenate(masks, axis=0)
                scores = jnp.where(visible[None], scores.reshape(heads, QUERIES, KEYS), MASKED).reshape(stacked, KEYS)
                old = max_ref[...]
                new = jnp.maximum(old, jnp.max(scores, axis=1, keepdims=True))
                alpha = jnp.exp2((old - new) * exp2_scale)
                shift = jnp.concatenate([new * exp2_scale] * (KEYS // HD), axis=1)
                weights = jnp.exp2(scores * exp2_scale - shift)
                max_ref[...] = new
                folded = weights[:, :HD]
                for m in range(1, KEYS // HD):
                    folded = folded + weights[:, m * HD : (m + 1) * HD]
                sum_ref[...] = sum_ref[...] * alpha + folded
                product = jnp.dot(weights.astype(jnp.bfloat16), values, preferred_element_type=jnp.float32)
                acc_ref[...] = acc_ref[...] * alpha + product
                return carry

            max_ref[...] = jnp.full(max_ref.shape, MASKED, jnp.float32)
            sum_ref[...] = jnp.zeros(sum_ref.shape, jnp.float32)
            acc_ref[...] = jnp.zeros(acc_ref.shape, jnp.float32)
            lax.fori_loop(0, count, one_block, 0)
            result = acc_ref[...] / jnp.sum(sum_ref[...], axis=1, keepdims=True)
            for head in range(heads):
                out_ref[slot, pl.ds(pl.multiple_of(tile * QUERIES, QUERIES), QUERIES), head * HD : (head + 1) * HD] = (
                    result[head * QUERIES : (head + 1) * QUERIES].astype(out_ref.dtype)
                )
            return carry

        lax.fori_loop(0, tok_rows // QUERIES, one_tile, 0)
        for at in range(n):

            @pl.when(k == at)
            def _():
                out_copy(at, at % 2).start()

        return carry

    lax.fori_loop(0, n, one_rows, 0)
    for k in range(max(n - 2, 0), n):
        out_copy(k, k % 2).wait()


def attend(info, marks, distances, token_parts, w_blocks, kv_parts, mask_width):
    n = len(distances)
    parts = len(token_parts[0])
    rows = token_parts[0][0].shape[0]
    source_rows, columns = w_blocks.shape[1:]
    depth = w_blocks.shape[0] * source_rows
    heads = columns // HD
    shard_rows = kv_parts[0].shape[2]
    shards = len(kv_parts) * kv_parts[0].shape[0]
    vmem = pl.BlockSpec(memory_space=pltpu.VMEM)
    smem = pl.BlockSpec(memory_space=pltpu.SMEM)
    leave = pl.BlockSpec(memory_space=pl.ANY)
    arrays = [part for block in token_parts for part in block] + [w_blocks] + list(kv_parts)
    counts = (parts, len(kv_parts), mask_width)
    tile_rows = heads * QUERIES

    def kernel(*refs):
        rows_kernel(counts, distances, (rows, shard_rows, source_rows), *refs)

    return pl.pallas_call(
        kernel,
        out_shape=[jax.ShapeDtypeStruct((rows, columns), jnp.bfloat16)] * n,
        in_specs=[smem, smem, vmem] + [leave] * len(arrays),
        out_specs=[leave] * n,
        scratch_shapes=[
            pltpu.VMEM((2, rows, depth), jnp.bfloat16),
            pltpu.VMEM((depth, columns), jnp.bfloat16),
            pltpu.VMEM((KEYS + shards * shard_rows, HD), jnp.bfloat16),
            pltpu.VMEM((KEYS + shards * shard_rows, HD), jnp.bfloat16),
            pltpu.VMEM((rows, columns), jnp.float32),
            pltpu.VMEM((rows * heads, HD), jnp.bfloat16),
            pltpu.VMEM((QUERIES // TILE, TILE, TILE), jnp.int32),
            pltpu.VMEM((tile_rows, HD), jnp.float32),
            pltpu.VMEM((tile_rows, HD), jnp.float32),
            pltpu.VMEM((tile_rows, HD), jnp.float32),
            pltpu.VMEM((2, rows, columns), jnp.bfloat16),
            pltpu.SemaphoreType.DMA((2, CHUNKS)),
            pltpu.SemaphoreType.DMA((w_blocks.shape[0],)),
            pltpu.SemaphoreType.DMA((shards, 2)),
            pltpu.SemaphoreType.DMA((2,)),
        ],
        compiler_params=pltpu.CompilerParams(vmem_limit_bytes=60 << 20),
        cost_estimate=pl.CostEstimate(
            flops=n * (2 * rows * depth * columns + 4 * rows * columns * 1024),
            bytes_accessed=2 * (n * rows * depth + depth * columns + shards * 2 * shard_rows * HD + n * rows * columns),
            transcendentals=n * rows * heads * 1024,
        ),
    )(info, marks, marks, *arrays)


def marks_of(doc_start, tile_mask):
    return jnp.concatenate([doc_start.reshape(-1, TILE), tile_mask.reshape(-1, TILE)])


def planar(tokens, norm_gain, w_query, cache_keys, cache_values, doc_start, tile_mask, group):
    devices = lax.axis_size("ctx")
    index = lax.axis_index("ctx")
    core = lax.axis_index("tp")
    place = lax.rem(index, group)
    tok_rows, width = tokens.shape
    kv_width = cache_keys.shape[1] // group
    q_width = w_query.shape[1] // group
    rows = group * tok_rows
    lines = [[first + k for first in range(0, devices, group)] for k in range(group)]
    far = range(1, group)

    def swapped(block, distance):
        return lax.ppermute(block, "ctx", [(i, i ^ distance) for i in range(devices)])

    def other_core(block):
        return lax.ppermute(block, "tp", [(0, 1), (1, 0)])

    def columns_for(array, distance, first, size, of, axis):
        at = lax.bitwise_xor(place, distance) * of + first
        return lax.dynamic_slice_in_dim(array, at, size, axis)

    def after(values, *earlier):
        flat = lax.optimization_barrier((tuple(values), tuple(earlier)))
        return list(flat[0])

    first_columns = (q_width // HD + 1) // 2 * HD
    cuts = ((0, first_columns), (first_columns, q_width))

    marks_own = marks_of(doc_start, tile_mask)
    w_first = [columns_for(w_query, d, cuts[0][0], cuts[0][1] - cuts[0][0], q_width, 1) for d in range(group)]
    kv_own = after([cache_keys, cache_values], *w_first)
    w_first = w_first[:1] + [swapped(w_first[d], d) for d in far]
    hop = [(i, i + group) for i in range(devices - group)]
    kv_before = [lax.ppermute(array, "ctx", hop) for array in kv_own]

    float_tokens = tokens.astype(jnp.float32)
    squares = jnp.sum(float_tokens * float_tokens, axis=-1)
    squares = squares + other_core(squares)
    inverse = lax.rsqrt(squares / (2 * width) + epsilon)
    gain = lax.dynamic_slice_in_dim(norm_gain, core * width, width, 0)
    normed = (float_tokens * inverse[:, None] * gain).astype(jnp.bfloat16)

    w_second = [columns_for(w_query, d, cuts[1][0], cuts[1][1] - cuts[1][0], q_width, 1) for d in range(group)]
    w_second = after(w_second, *w_first)
    w_second = w_second[:1] + [swapped(w_second[d], d) for d in far]
    w_stack = jnp.stack(after(w_first, *kv_before))
    w_chunks = [lax.all_gather(w_stack, "ctx", axis=0, tiled=True, axis_index_groups=lines)]
    (marks_sent,) = after([marks_own], w_stack)
    marks = [marks_own] + [swapped(marks_sent, d) for d in far]

    def kv_for(d):
        arrays = (*kv_before, cache_keys, cache_values)
        return jnp.stack([columns_for(array, d, 0, kv_width, kv_width, 1) for array in arrays]).reshape(
            2, 2, tok_rows, kv_width
        )

    kv_cut = [kv_for(d) for d in range(group)]
    kv_parts = kv_cut[:1] + [swapped(kv_cut[d], d) for d in far]
    (normed,) = after([normed], *marks, *kv_cut, *w_second)
    from_x, from_y = swapped(normed, 1), swapped(normed, 2)
    mine_other = other_core(normed)
    (w_after,) = after([jnp.stack(w_second)], *kv_parts)
    w_chunks.append(lax.all_gather(w_after, "ctx", axis=0, tiled=True, axis_index_groups=lines))

    half = width // 2
    from_x, from_y = after([from_x, from_y], w_after)
    corner_a, corner_b = swapped(from_y[:, :half], 1), swapped(from_x[:, half:], 2)
    token_parts = [[normed, mine_other]] + [[from_x, other_core(from_x)], [from_y, other_core(from_y)]]

    info = jnp.stack([(index // group - 1) * rows, place, core]).astype(jnp.int32)
    width_mask = tile_mask.shape[1]

    def call(distances, chunk, *earlier):
        chosen = [token_parts[d] for d in distances]
        (start,) = after([info], *earlier)
        picked = jnp.stack([marks[d] for d in distances])
        return attend(start, picked, distances, chosen, chunk, kv_parts, width_mask)

    pieces, last = {}, ()
    for chunk, distances in ((0, (2, 1, 0)), (0, (3,)), (1, (3, 2, 1)), (1, (0,))):
        if distances == (3,):
            corner = jnp.concatenate(after([corner_a, corner_b], *last), axis=1)
            token_parts.append([corner, other_core(corner)])
        outs = call(distances, w_chunks[chunk], *last)
        last = outs[:1]
        pieces.update({(d, chunk): swapped(out, d) if d else out for d, out in zip(distances, outs)})
    return joined(info, pieces, q_width, [low for low, _ in cuts], group * q_width)


def joined(info, pieces, q_width, lows, columns):
    keys = sorted(pieces)
    rows = pieces[keys[0]].shape[0]
    vmem = pl.BlockSpec(memory_space=pltpu.VMEM)

    def kernel(info_ref, *refs):
        out_ref = refs[-1]
        for k, (distance, chunk) in enumerate(keys):
            at = pl.multiple_of(lax.bitwise_xor(info_ref[1], distance) * q_width + lows[chunk], HD)
            out_ref[:, pl.ds(at, refs[k].shape[1])] = refs[k][...]

    return pl.pallas_call(
        kernel,
        out_shape=jax.ShapeDtypeStruct((rows, columns), jnp.bfloat16),
        in_specs=[pl.BlockSpec(memory_space=pltpu.SMEM)] + [vmem] * len(keys),
        out_specs=vmem,
        cost_estimate=pl.CostEstimate(flops=0, bytes_accessed=4 * rows * columns, transcendentals=0),
    )(info, *[pieces[key] for key in keys])


def plain(tokens, norm_gain, w_query, cache_keys, cache_values, doc_start, tile_mask):
    devices = lax.axis_size("ctx")
    index = lax.axis_index("ctx")
    tok_rows = tokens.shape[0]
    float_tokens = lax.all_gather(tokens, "tp", axis=1, tiled=True).astype(jnp.float32)
    inverse = lax.rsqrt(jnp.mean(float_tokens * float_tokens, axis=-1, keepdims=True) + epsilon)
    normed = (float_tokens * inverse * norm_gain).astype(jnp.bfloat16)
    kv_heads = cache_keys.shape[1] // HD
    q_width = w_query.shape[1] // kv_heads
    w_blocks = lax.all_gather(w_query, "ctx", axis=0)
    reach = (MAXDOC + tok_rows - 2) // tok_rows
    kv_own = jnp.stack([cache_keys, cache_values])
    shards = [
        lax.ppermute(kv_own, "ctx", [(i, i + distance) for i in range(devices - distance)])
        for distance in range(reach, 0, -1)
    ]
    kv_window = jnp.stack(shards + [kv_own])
    info = jnp.stack([(index - reach) * tok_rows, jnp.int32(0), jnp.int32(0)]).astype(jnp.int32)
    marks = marks_of(doc_start, tile_mask)[None]
    outs = [
        attend(
            info,
            marks,
            (0,),
            [[normed]],
            w_blocks[:, :, head * q_width : (head + 1) * q_width],
            [kv_window[:, :, :, head * HD : (head + 1) * HD]],
            tile_mask.shape[1],
        )[0]
        for head in range(kv_heads)
    ]
    return outs[0] if kv_heads == 1 else jnp.concatenate(outs, axis=1)


def on_device(*arrays):
    kv_heads = arrays[3].shape[1] // HD
    group = 4
    rows = group * arrays[0].shape[0]
    if kv_heads == group and lax.axis_size("ctx") % group == 0 and lax.axis_size("tp") == 2 and rows >= MAXDOC - 1:
        return planar(*arrays, group)
    return plain(*arrays)


def solution(mesh):
    return jax.shard_map(
        on_device,
        mesh=mesh,
        in_specs=(
            P("ctx", "tp"),
            P(),
            P("ctx", "tp"),
            P("ctx", "tp"),
            P("ctx", "tp"),
            P("ctx"),
            P("ctx", None),
        ),
        out_specs=P("ctx", "tp"),
        check_vma=False,
    )
```

```python
import math

import jax
import jax.numpy as jnp
from jax import lax
from jax.experimental import pallas as pl
from jax.experimental.pallas import tpu as pltpu
from jax.sharding import PartitionSpec as P

HD = 128
TILE = 128
MAXDOC = 2048
KEYS = 512
QUERIES = 256
CHUNKS = 4
FAR = 1 << 30
MASKED = -1e30


epsilon = 1e-05
exp2_scale = math.log2(math.e) / HD**0.5


def rows_kernel(counts, distances, shapes, info, marks_smem, marks_ref, *refs):
    parts, kv_count, halves, mask_width = counts
    tok_rows, shard_rows, source_rows = shapes
    n = len(distances)
    token_hbm = [refs[k * parts : (k + 1) * parts] for k in range(n)]
    w_hbm = refs[n * parts]
    kv_hbm = refs[n * parts + 1 :][:kv_count]
    out_hbm = refs[n * parts + 1 + kv_count :][:n]
    scratch = refs[n * parts + 1 + kv_count + n :]
    token_ref, w_ref, key_ref, value_ref, total_ref, query_ref, doc_full, acc_ref, max_ref, sum_ref, out_ref = scratch[:11]
    token_sem, w_sem, kv_sem, out_sem = scratch[11:]
    columns = w_ref.shape[1]
    heads = columns // HD
    depth = w_ref.shape[0]
    blocks = depth // source_rows
    swap = info[1]
    chunk = depth // CHUNKS
    chunks_part = CHUNKS // parts
    doc_rows = tok_rows // TILE
    window_rows = halves * kv_count * shard_rows
    base = window_rows - kv_count * shard_rows

    def token_copy(ref, at, c, slot):
        return pltpu.make_async_copy(
            ref.at[:, at * chunk : (at + 1) * chunk],
            token_ref.at[slot, :, c * chunk : (c + 1) * chunk],
            token_sem.at[slot, c],
        )

    def fetch_tokens(k, c):
        token_copy(token_hbm[k][c // chunks_part], c % chunks_part, c, k % 2).start()

    def rows_of(c):
        return lax.bitwise_xor(info[2], c // chunks_part) * chunks_part + c % chunks_part

    def w_copy(at, place):
        target = pl.ds(pl.multiple_of(place * source_rows, 16), source_rows)
        return pltpu.make_async_copy(w_hbm.at[at], w_ref.at[target], w_sem.at[place])

    blocks_chunk = blocks // CHUNKS

    def kv_copy(ref, half, which, place):
        target = pl.ds(pl.multiple_of(KEYS + place * shard_rows, 16), shard_rows)
        return pltpu.make_async_copy(
            ref.at[pl.ds((half * 2 + which) * shard_rows, shard_rows), :],
            (key_ref, value_ref)[which].at[target],
            kv_sem.at[place, which],
        )

    def out_copy(k, slot):
        return pltpu.make_async_copy(out_ref.at[slot], out_hbm[k], out_sem.at[slot])

    for c in range(CHUNKS):
        fetch_tokens(0, c)
        for at in range(blocks_chunk):
            place = rows_of(c) * blocks_chunk + at
            w_copy(lax.bitwise_xor(swap, place), place).start()
    for at in range(kv_count):
        for half in range(halves):
            for which in range(2):
                kv_copy(kv_hbm[at], half, which, half * kv_count + lax.bitwise_xor(swap, at)).start()
    key_ref[0:KEYS, :] = jnp.zeros((KEYS, HD), jnp.bfloat16)
    value_ref[0:KEYS, :] = jnp.zeros((KEYS, HD), jnp.bfloat16)

    stacked = heads * QUERIES
    subs = QUERIES // TILE

    def one_rows(k, carry):
        slot = lax.rem(k, 2)
        for ahead in range(1, n):

            @pl.when(k == ahead - 1)
            def _():
                for c in range(CHUNKS):
                    fetch_tokens(ahead, c)

        for c in range(CHUNKS):
            token_copy(token_hbm[0][0], 0, c, slot).wait()

            @pl.when(k == 0)
            def _():
                for at in range(blocks_chunk):
                    w_copy(0, rows_of(c) * blocks_chunk + at).wait()

            for first in range(0, tok_rows, QUERIES):
                piece = jnp.dot(
                    token_ref[slot, first : first + QUERIES, c * chunk : (c + 1) * chunk],
                    w_ref[pl.ds(pl.multiple_of(rows_of(c) * chunk, 16), chunk), :],
                    preferred_element_type=jnp.float32,
                )
                if c == 0:
                    total_ref[first : first + QUERIES, :] = piece
                else:
                    total_ref[first : first + QUERIES, :] += piece
        for tile in range(tok_rows // QUERIES):
            for head in range(heads):
                at = (tile * heads + head) * QUERIES
                query_ref[at : at + QUERIES, :] = total_ref[
                    tile * QUERIES : (tile + 1) * QUERIES, head * HD : (head + 1) * HD
                ].astype(jnp.bfloat16)

        @pl.when(k == 0)
        def _():
            for place in range(kv_count * halves):
                for which in range(2):
                    kv_copy(kv_hbm[0], 0, which, place).wait()

        @pl.when(k >= 2)
        def _():
            out_copy(0, slot).wait()

        distance = jnp.int32(distances[0])
        for other in range(1, n):
            distance = jnp.where(k == other, distances[other], distance)
        rows_first = base + lax.bitwise_xor(swap, distance) * tok_rows

        def one_tile(tile, carry):
            query = query_ref[pl.ds(pl.multiple_of(tile * stacked, stacked), stacked), :]
            row_first = rows_first + tile * QUERIES
            end = row_first + QUERIES
            for sub in range(subs):
                docs_row = marks_ref[distance, pl.ds(tile * subs + sub, 1), :].astype(jnp.float32)
                doc_full[sub] = jnp.transpose(jnp.broadcast_to(docs_row, (TILE, TILE))).astype(jnp.int32)
            first_key = marks_smem[distance, tile * subs, 0] - info[0]
            count = (end - first_key + KEYS - 1) // KEYS

            def one_block(back, carry):
                start = end - (back + 1) * KEYS
                at = pl.multiple_of(start + KEYS, TILE)
                keys = key_ref[pl.ds(at, KEYS), :]
                values = value_ref[pl.ds(at, KEYS), :]
                scores = lax.dot_general(query, keys, (((1,), (1,)), ((), ())), preferred_element_type=jnp.float32)
                key_tile = (info[0] + start) // TILE
                lane = lax.broadcasted_iota(jnp.int32, (TILE, TILE), 1)
                row = lax.broadcasted_iota(jnp.int32, (TILE, TILE), 0)
                masks = []
                for sub in range(subs):
                    causal = row + (row_first + sub * TILE - start)
                    docs = doc_full[sub] - (info[0] + start)
                    pieces = []
                    for m in range(KEYS // TILE):
                        column = lax.min(lax.max(key_tile + m, 0), mask_width - 1)
                        flat = (tile * subs + sub) * mask_width + column
                        shut = jnp.where(marks_smem[distance, doc_rows + flat // TILE, lax.rem(flat, TILE)] == 1, 0, FAR)
                        pieces.append((lane <= causal - m * TILE) & (lane >= docs + (shut - m * TILE)))
                    masks.append(jnp.concatenate(pieces, axis=1))
                visible = jnp.concatenate(masks, axis=0)
                scores = jnp.where(visible[None], scores.reshape(heads, QUERIES, KEYS), MASKED).reshape(stacked, KEYS)
                old = max_ref[...]
                new = jnp.maximum(old, jnp.max(scores, axis=1, keepdims=True))
                alpha = jnp.exp2((old - new) * exp2_scale)
                shift = jnp.concatenate([new * exp2_scale] * (KEYS // HD), axis=1)
                weights = jnp.exp2(scores * exp2_scale - shift)
                max_ref[...] = new
                folded = weights[:, :HD]
                for m in range(1, KEYS // HD):
                    folded = folded + weights[:, m * HD : (m + 1) * HD]
                sum_ref[...] = sum_ref[...] * alpha + folded
                product = jnp.dot(weights.astype(jnp.bfloat16), values, preferred_element_type=jnp.float32)
                acc_ref[...] = acc_ref[...] * alpha + product
                return carry

            max_ref[...] = jnp.full(max_ref.shape, MASKED, jnp.float32)
            sum_ref[...] = jnp.zeros(sum_ref.shape, jnp.float32)
            acc_ref[...] = jnp.zeros(acc_ref.shape, jnp.float32)
            lax.fori_loop(0, count, one_block, 0)
            result = acc_ref[...] / jnp.sum(sum_ref[...], axis=1, keepdims=True)
            for head in range(heads):
                out_ref[slot, pl.ds(pl.multiple_of(tile * QUERIES, QUERIES), QUERIES), head * HD : (head + 1) * HD] = (
                    result[head * QUERIES : (head + 1) * QUERIES].astype(out_ref.dtype)
                )
            return carry

        lax.fori_loop(0, tok_rows // QUERIES, one_tile, 0)
        for at in range(n):

            @pl.when(k == at)
            def _():
                out_copy(at, at % 2).start()

        return carry

    lax.fori_loop(0, n, one_rows, 0)
    for k in range(max(n - 2, 0), n):
        out_copy(k, k % 2).wait()


def attend(info, marks, distances, token_parts, w_blocks, kv_parts, halves, mask_width):
    n = len(distances)
    parts = len(token_parts[0])
    rows = token_parts[0][0].shape[0]
    source_rows, columns = w_blocks.shape[1:]
    depth = w_blocks.shape[0] * source_rows
    heads = columns // HD
    shard_rows = kv_parts[0].shape[0] // (2 * halves) // TILE * TILE
    shards = len(kv_parts) * halves
    vmem = pl.BlockSpec(memory_space=pltpu.VMEM)
    smem = pl.BlockSpec(memory_space=pltpu.SMEM)
    leave = pl.BlockSpec(memory_space=pl.ANY)
    arrays = [part for block in token_parts for part in block] + [w_blocks] + list(kv_parts)
    counts = (parts, len(kv_parts), halves, mask_width)
    tile_rows = heads * QUERIES

    def kernel(*refs):
        rows_kernel(counts, distances, (rows, shard_rows, source_rows), *refs)

    return pl.pallas_call(
        kernel,
        out_shape=[jax.ShapeDtypeStruct((rows, columns), jnp.bfloat16)] * n,
        in_specs=[smem, smem, vmem] + [leave] * len(arrays),
        out_specs=[leave] * n,
        scratch_shapes=[
            pltpu.VMEM((2, rows, depth), jnp.bfloat16),
            pltpu.VMEM((depth, columns), jnp.bfloat16),
            pltpu.VMEM((KEYS + shards * shard_rows, HD), jnp.bfloat16),
            pltpu.VMEM((KEYS + shards * shard_rows, HD), jnp.bfloat16),
            pltpu.VMEM((rows, columns), jnp.float32),
            pltpu.VMEM((rows * heads, HD), jnp.bfloat16),
            pltpu.VMEM((QUERIES // TILE, TILE, TILE), jnp.int32),
            pltpu.VMEM((tile_rows, HD), jnp.float32),
            pltpu.VMEM((tile_rows, HD), jnp.float32),
            pltpu.VMEM((tile_rows, HD), jnp.float32),
            pltpu.VMEM((2, rows, columns), jnp.bfloat16),
            pltpu.SemaphoreType.DMA((2, CHUNKS)),
            pltpu.SemaphoreType.DMA((w_blocks.shape[0],)),
            pltpu.SemaphoreType.DMA((shards, 2)),
            pltpu.SemaphoreType.DMA((2,)),
        ],
        compiler_params=pltpu.CompilerParams(vmem_limit_bytes=60 << 20),
        cost_estimate=pl.CostEstimate(
            flops=n * (2 * rows * depth * columns + 4 * rows * columns * 1024),
            bytes_accessed=2 * (n * rows * depth + depth * columns + shards * 2 * shard_rows * HD + n * rows * columns),
            transcendentals=n * rows * heads * 1024,
        ),
    )(info, marks, marks, *arrays)


def marks_of(doc_start, tile_mask):
    return jnp.concatenate([doc_start.reshape(-1, TILE), tile_mask.reshape(-1, TILE)])


def planar(tokens, norm_gain, w_query, cache_keys, cache_values, doc_start, tile_mask, group):
    devices = lax.axis_size("ctx")
    index = lax.axis_index("ctx")
    core = lax.axis_index("tp")
    place = lax.rem(index, group)
    tok_rows, width = tokens.shape
    kv_width = cache_keys.shape[1] // group
    q_width = w_query.shape[1] // group
    rows = group * tok_rows
    lines = [[first + k for first in range(0, devices, group)] for k in range(group)]
    far = range(1, group)

    def swapped(block, distance):
        return lax.ppermute(block, "ctx", [(i, i ^ distance) for i in range(devices)])

    def other_core(block):
        return lax.ppermute(block, "tp", [(0, 1), (1, 0)])

    def columns_for(array, distance, first, size, of, axis):
        at = lax.bitwise_xor(place, distance) * of + first
        return lax.dynamic_slice_in_dim(array, at, size, axis)

    def after(values, *earlier):
        flat = lax.optimization_barrier((tuple(values), tuple(earlier)))
        return list(flat[0])

    first_columns = (q_width // HD + 1) // 2 * HD
    cuts = ((0, first_columns), (first_columns, q_width))

    kv_own = jnp.stack([cache_keys, cache_values])
    w_first = [columns_for(w_query, d, cuts[0][0], cuts[0][1] - cuts[0][0], q_width, 1) for d in range(group)]
    w_first = after(w_first, kv_own)
    w_first = w_first[:1] + [swapped(w_first[d], d) for d in far]
    kv_before = lax.ppermute(kv_own, "ctx", [(i, i + group) for i in range(devices - group)])

    float_tokens = tokens.astype(jnp.float32)
    squares = jnp.sum(float_tokens * float_tokens, axis=-1)
    squares = squares + other_core(squares)
    inverse = lax.rsqrt(squares / (2 * width) + epsilon)
    gain = lax.dynamic_slice_in_dim(norm_gain, core * width, width, 0)
    normed = (float_tokens * inverse[:, None] * gain).astype(jnp.bfloat16)

    w_second = [columns_for(w_query, d, cuts[1][0], cuts[1][1] - cuts[1][0], q_width, 1) for d in range(group)]
    w_second = after(w_second, *w_first)
    w_second = w_second[:1] + [swapped(w_second[d], d) for d in far]
    w_stack = jnp.stack(after(w_first, kv_before))
    w_chunks = [lax.all_gather(w_stack, "ctx", axis=0, tiled=True, axis_index_groups=lines)]

    marks_own = marks_of(doc_start, tile_mask)
    marks_rows = marks_own.shape[0]
    bytes_own = jnp.concatenate([marks_own >> 16, (marks_own >> 8) & 255, marks_own & 255]).astype(jnp.bfloat16)
    bytes_own = jnp.pad(bytes_own, ((0, -bytes_own.shape[0] % 16), (0, 0)))

    def kv_for(d):
        cut = [columns_for(array, d, 0, kv_width, kv_width, 2).reshape(-1, kv_width) for array in (kv_before, kv_own)]
        return jnp.concatenate(cut + [bytes_own])

    kv_parts = [kv_for(0)] + [swapped(kv_for(d), d) for d in far]

    sent = jnp.stack([part[4 * tok_rows :] for part in kv_parts]).astype(jnp.int32)
    marks = sent[:, :marks_rows] * 65536 + sent[:, marks_rows : 2 * marks_rows] * 256
    marks = marks + sent[:, 2 * marks_rows : 3 * marks_rows]
    from_x, from_y = swapped(normed, 1), swapped(normed, 2)
    mine_other = other_core(normed)
    (w_after,) = after([jnp.stack(w_second)], *kv_parts)
    w_chunks.append(lax.all_gather(w_after, "ctx", axis=0, tiled=True, axis_index_groups=lines))

    half = width // 2
    from_x, from_y = after([from_x, from_y], w_after)
    corner_a, corner_b = swapped(from_y[:, :half], 1), swapped(from_x[:, half:], 2)
    token_parts = [[normed, mine_other]] + [[from_x, other_core(from_x)], [from_y, other_core(from_y)]]

    info = jnp.stack([(index // group - 1) * rows, place, core]).astype(jnp.int32)
    width_mask = tile_mask.shape[1]

    def call(distances, chunk, *earlier):
        chosen = [token_parts[d] for d in distances]
        (start,) = after([info], *earlier)
        return attend(start, marks, distances, chosen, chunk, kv_parts, 2, width_mask)

    pieces, last = {}, ()
    for chunk, distances in ((0, (2, 1, 0)), (0, (3,)), (1, (3, 2, 1)), (1, (0,))):
        if distances == (3,):
            corner = jnp.concatenate(after([corner_a, corner_b], *last), axis=1)
            token_parts.append([corner, other_core(corner)])
        outs = call(distances, w_chunks[chunk], *last)
        last = outs[:1]
        pieces.update({(d, chunk): swapped(out, d) if d else out for d, out in zip(distances, outs)})
    return joined(info, pieces, q_width, [low for low, _ in cuts], group * q_width)


def joined(info, pieces, q_width, lows, columns):
    keys = sorted(pieces)
    rows = pieces[keys[0]].shape[0]
    vmem = pl.BlockSpec(memory_space=pltpu.VMEM)

    def kernel(info_ref, *refs):
        out_ref = refs[-1]
        for k, (distance, chunk) in enumerate(keys):
            at = pl.multiple_of(lax.bitwise_xor(info_ref[1], distance) * q_width + lows[chunk], HD)
            out_ref[:, pl.ds(at, refs[k].shape[1])] = refs[k][...]

    return pl.pallas_call(
        kernel,
        out_shape=jax.ShapeDtypeStruct((rows, columns), jnp.bfloat16),
        in_specs=[pl.BlockSpec(memory_space=pltpu.SMEM)] + [vmem] * len(keys),
        out_specs=vmem,
        cost_estimate=pl.CostEstimate(flops=0, bytes_accessed=4 * rows * columns, transcendentals=0),
    )(info, *[pieces[key] for key in keys])


def plain(tokens, norm_gain, w_query, cache_keys, cache_values, doc_start, tile_mask):
    devices = lax.axis_size("ctx")
    index = lax.axis_index("ctx")
    tok_rows = tokens.shape[0]
    float_tokens = lax.all_gather(tokens, "tp", axis=1, tiled=True).astype(jnp.float32)
    inverse = lax.rsqrt(jnp.mean(float_tokens * float_tokens, axis=-1, keepdims=True) + epsilon)
    normed = (float_tokens * inverse * norm_gain).astype(jnp.bfloat16)
    kv_heads = cache_keys.shape[1] // HD
    q_width = w_query.shape[1] // kv_heads
    w_blocks = lax.all_gather(w_query, "ctx", axis=0)
    reach = (MAXDOC + tok_rows - 2) // tok_rows
    kv_own = jnp.stack([cache_keys, cache_values])
    shards = [
        lax.ppermute(kv_own, "ctx", [(i, i + distance) for i in range(devices - distance)])
        for distance in range(reach, 0, -1)
    ]
    kv_window = jnp.stack(shards + [kv_own])
    info = jnp.stack([(index - reach) * tok_rows, jnp.int32(0), jnp.int32(0)]).astype(jnp.int32)
    marks = marks_of(doc_start, tile_mask)[None]
    outs = [
        attend(
            info,
            marks,
            (0,),
            [[normed]],
            w_blocks[:, :, head * q_width : (head + 1) * q_width],
            [kv_window[:, :, :, head * HD : (head + 1) * HD].reshape(-1, HD)],
            reach + 1,
            tile_mask.shape[1],
        )[0]
        for head in range(kv_heads)
    ]
    return outs[0] if kv_heads == 1 else jnp.concatenate(outs, axis=1)


def on_device(*arrays):
    kv_heads = arrays[3].shape[1] // HD
    group = 4
    rows = group * arrays[0].shape[0]
    if kv_heads == group and lax.axis_size("ctx") % group == 0 and lax.axis_size("tp") == 2 and rows >= MAXDOC - 1:
        return planar(*arrays, group)
    return plain(*arrays)


def solution(mesh):
    return jax.shard_map(
        on_device,
        mesh=mesh,
        in_specs=(
            P("ctx", "tp"),
            P(),
            P("ctx", "tp"),
            P("ctx", "tp"),
            P("ctx", "tp"),
            P("ctx"),
            P("ctx", None),
        ),
        out_specs=P("ctx", "tp"),
        check_vma=False,
    )
```

```python
import math

import jax
import jax.numpy as jnp
from jax import lax
from jax.experimental import pallas as pl
from jax.experimental.pallas import tpu as pltpu
from jax.sharding import PartitionSpec as P

HD = 128
TILE = 128
MAXDOC = 2048
KEYS = 512
QUERIES = 256
CHUNKS = 4
FAR = 1 << 30
MASKED = -1e30


epsilon = 1e-05
exp2_scale = math.log2(math.e) / HD**0.5


def rows_kernel(counts, distances, shapes, info, marks_smem, marks_ref, *refs):
    parts, kv_count, halves, mask_width = counts
    tok_rows, shard_rows, source_rows = shapes
    n = len(distances)
    token_hbm = [refs[k * parts : (k + 1) * parts] for k in range(n)]
    w_hbm = refs[n * parts]
    kv_hbm = refs[n * parts + 1 :][:kv_count]
    out_hbm = refs[n * parts + 1 + kv_count :][:n]
    scratch = refs[n * parts + 1 + kv_count + n :]
    token_ref, w_ref, key_ref, value_ref, total_ref, query_ref, doc_full, acc_ref, max_ref, sum_ref, out_ref = scratch[:11]
    token_sem, w_sem, kv_sem, out_sem = scratch[11:]
    columns = w_ref.shape[1]
    heads = columns // HD
    depth = w_ref.shape[0]
    blocks = depth // source_rows
    swap = info[1]
    chunk = depth // CHUNKS
    chunks_part = CHUNKS // parts
    doc_rows = tok_rows // TILE
    window_rows = halves * kv_count * shard_rows
    base = window_rows - kv_count * shard_rows

    def token_copy(ref, at, c, slot):
        return pltpu.make_async_copy(
            ref.at[:, at * chunk : (at + 1) * chunk],
            token_ref.at[slot, :, c * chunk : (c + 1) * chunk],
            token_sem.at[slot, c],
        )

    def fetch_tokens(k, c):
        token_copy(token_hbm[k][c // chunks_part], c % chunks_part, c, k % 2).start()

    def rows_of(c):
        return lax.bitwise_xor(info[2], c // chunks_part) * chunks_part + c % chunks_part

    def w_copy(at, place):
        target = pl.ds(pl.multiple_of(place * source_rows, 16), source_rows)
        return pltpu.make_async_copy(w_hbm.at[at], w_ref.at[target], w_sem.at[place])

    blocks_chunk = blocks // CHUNKS

    def kv_copy(ref, half, which, place):
        target = pl.ds(pl.multiple_of(KEYS + place * shard_rows, 16), shard_rows)
        return pltpu.make_async_copy(
            ref.at[pl.ds((half * 2 + which) * shard_rows, shard_rows), :],
            (key_ref, value_ref)[which].at[target],
            kv_sem.at[place, which],
        )

    def out_copy(k, slot):
        return pltpu.make_async_copy(out_ref.at[slot], out_hbm[k], out_sem.at[slot])

    for c in range(CHUNKS):
        fetch_tokens(0, c)
        for at in range(blocks_chunk):
            place = rows_of(c) * blocks_chunk + at
            w_copy(lax.bitwise_xor(swap, place), place).start()
    for at in range(kv_count):
        for half in range(halves):
            for which in range(2):
                kv_copy(kv_hbm[at], half, which, half * kv_count + lax.bitwise_xor(swap, at)).start()
    key_ref[0:KEYS, :] = jnp.zeros((KEYS, HD), jnp.bfloat16)
    value_ref[0:KEYS, :] = jnp.zeros((KEYS, HD), jnp.bfloat16)

    stacked = heads * QUERIES
    subs = QUERIES // TILE

    def one_rows(k, carry):
        slot = lax.rem(k, 2)
        for ahead in range(1, n):

            @pl.when(k == ahead - 1)
            def _():
                for c in range(CHUNKS):
                    fetch_tokens(ahead, c)

        for c in range(CHUNKS):
            token_copy(token_hbm[0][0], 0, c, slot).wait()

            @pl.when(k == 0)
            def _():
                for at in range(blocks_chunk):
                    w_copy(0, rows_of(c) * blocks_chunk + at).wait()

            for first in range(0, tok_rows, QUERIES):
                piece = jnp.dot(
                    token_ref[slot, first : first + QUERIES, c * chunk : (c + 1) * chunk],
                    w_ref[pl.ds(pl.multiple_of(rows_of(c) * chunk, 16), chunk), :],
                    preferred_element_type=jnp.float32,
                )
                if c == 0:
                    total_ref[first : first + QUERIES, :] = piece
                else:
                    total_ref[first : first + QUERIES, :] += piece
        for tile in range(tok_rows // QUERIES):
            for head in range(heads):
                at = (tile * heads + head) * QUERIES
                query_ref[at : at + QUERIES, :] = total_ref[
                    tile * QUERIES : (tile + 1) * QUERIES, head * HD : (head + 1) * HD
                ].astype(jnp.bfloat16)

        @pl.when(k == 0)
        def _():
            for place in range(kv_count * halves):
                for which in range(2):
                    kv_copy(kv_hbm[0], 0, which, place).wait()

        @pl.when(k >= 2)
        def _():
            out_copy(0, slot).wait()

        distance = jnp.int32(distances[0])
        for other in range(1, n):
            distance = jnp.where(k == other, distances[other], distance)
        rows_first = base + lax.bitwise_xor(swap, distance) * tok_rows

        def one_tile(tile, carry):
            query = query_ref[pl.ds(pl.multiple_of(tile * stacked, stacked), stacked), :]
            row_first = rows_first + tile * QUERIES
            end = row_first + QUERIES
            for sub in range(subs):
                docs_row = marks_ref[distance, pl.ds(tile * subs + sub, 1), :].astype(jnp.float32)
                doc_full[sub] = jnp.transpose(jnp.broadcast_to(docs_row, (TILE, TILE))).astype(jnp.int32)
            first_key = marks_smem[distance, tile * subs, 0] - info[0]
            count = (end - first_key + KEYS - 1) // KEYS

            def one_block(back, carry):
                start = end - (back + 1) * KEYS
                at = pl.multiple_of(start + KEYS, TILE)
                keys = key_ref[pl.ds(at, KEYS), :]
                values = value_ref[pl.ds(at, KEYS), :]
                scores = lax.dot_general(query, keys, (((1,), (1,)), ((), ())), preferred_element_type=jnp.float32)
                key_tile = (info[0] + start) // TILE
                lane = lax.broadcasted_iota(jnp.int32, (TILE, TILE), 1)
                row = lax.broadcasted_iota(jnp.int32, (TILE, TILE), 0)
                masks = []
                for sub in range(subs):
                    causal = row + (row_first + sub * TILE - start)
                    docs = doc_full[sub] - (info[0] + start)
                    pieces = []
                    for m in range(KEYS // TILE):
                        column = lax.min(lax.max(key_tile + m, 0), mask_width - 1)
                        flat = (tile * subs + sub) * mask_width + column
                        shut = jnp.where(marks_smem[distance, doc_rows + flat // TILE, lax.rem(flat, TILE)] == 1, 0, FAR)
                        pieces.append((lane <= causal - m * TILE) & (lane >= docs + (shut - m * TILE)))
                    masks.append(jnp.concatenate(pieces, axis=1))
                visible = jnp.concatenate(masks, axis=0)
                scores = jnp.where(visible[None], scores.reshape(heads, QUERIES, KEYS), MASKED).reshape(stacked, KEYS)
                old = max_ref[...]
                new = jnp.maximum(old, jnp.max(scores, axis=1, keepdims=True))
                alpha = jnp.exp2((old - new) * exp2_scale)
                shift = jnp.concatenate([new * exp2_scale] * (KEYS // HD), axis=1)
                weights = jnp.exp2(scores * exp2_scale - shift)
                max_ref[...] = new
                folded = weights[:, :HD]
                for m in range(1, KEYS // HD):
                    folded = folded + weights[:, m * HD : (m + 1) * HD]
                sum_ref[...] = sum_ref[...] * alpha + folded
                product = jnp.dot(weights.astype(jnp.bfloat16), values, preferred_element_type=jnp.float32)
                acc_ref[...] = acc_ref[...] * alpha + product
                return carry

            max_ref[...] = jnp.full(max_ref.shape, MASKED, jnp.float32)
            sum_ref[...] = jnp.zeros(sum_ref.shape, jnp.float32)
            acc_ref[...] = jnp.zeros(acc_ref.shape, jnp.float32)
            lax.fori_loop(0, count, one_block, 0)
            result = acc_ref[...] / jnp.sum(sum_ref[...], axis=1, keepdims=True)
            for head in range(heads):
                out_ref[slot, pl.ds(pl.multiple_of(tile * QUERIES, QUERIES), QUERIES), head * HD : (head + 1) * HD] = (
                    result[head * QUERIES : (head + 1) * QUERIES].astype(out_ref.dtype)
                )
            return carry

        lax.fori_loop(0, tok_rows // QUERIES, one_tile, 0)
        for at in range(n):

            @pl.when(k == at)
            def _():
                out_copy(at, at % 2).start()

        return carry

    lax.fori_loop(0, n, one_rows, 0)
    for k in range(max(n - 2, 0), n):
        out_copy(k, k % 2).wait()


def attend(info, marks, distances, token_parts, w_blocks, kv_parts, halves, mask_width):
    n = len(distances)
    parts = len(token_parts[0])
    rows = token_parts[0][0].shape[0]
    source_rows, columns = w_blocks.shape[1:]
    depth = w_blocks.shape[0] * source_rows
    heads = columns // HD
    shard_rows = kv_parts[0].shape[0] // (2 * halves) // TILE * TILE
    shards = len(kv_parts) * halves
    vmem = pl.BlockSpec(memory_space=pltpu.VMEM)
    smem = pl.BlockSpec(memory_space=pltpu.SMEM)
    leave = pl.BlockSpec(memory_space=pl.ANY)
    arrays = [part for block in token_parts for part in block] + [w_blocks] + list(kv_parts)
    counts = (parts, len(kv_parts), halves, mask_width)
    tile_rows = heads * QUERIES

    def kernel(*refs):
        rows_kernel(counts, distances, (rows, shard_rows, source_rows), *refs)

    return pl.pallas_call(
        kernel,
        out_shape=[jax.ShapeDtypeStruct((rows, columns), jnp.bfloat16)] * n,
        in_specs=[smem, smem, vmem] + [leave] * len(arrays),
        out_specs=[leave] * n,
        scratch_shapes=[
            pltpu.VMEM((2, rows, depth), jnp.bfloat16),
            pltpu.VMEM((depth, columns), jnp.bfloat16),
            pltpu.VMEM((KEYS + shards * shard_rows, HD), jnp.bfloat16),
            pltpu.VMEM((KEYS + shards * shard_rows, HD), jnp.bfloat16),
            pltpu.VMEM((rows, columns), jnp.float32),
            pltpu.VMEM((rows * heads, HD), jnp.bfloat16),
            pltpu.VMEM((QUERIES // TILE, TILE, TILE), jnp.int32),
            pltpu.VMEM((tile_rows, HD), jnp.float32),
            pltpu.VMEM((tile_rows, HD), jnp.float32),
            pltpu.VMEM((tile_rows, HD), jnp.float32),
            pltpu.VMEM((2, rows, columns), jnp.bfloat16),
            pltpu.SemaphoreType.DMA((2, CHUNKS)),
            pltpu.SemaphoreType.DMA((w_blocks.shape[0],)),
            pltpu.SemaphoreType.DMA((shards, 2)),
            pltpu.SemaphoreType.DMA((2,)),
        ],
        compiler_params=pltpu.CompilerParams(vmem_limit_bytes=60 << 20),
        cost_estimate=pl.CostEstimate(
            flops=n * (2 * rows * depth * columns + 4 * rows * columns * 1024),
            bytes_accessed=2 * (n * rows * depth + depth * columns + shards * 2 * shard_rows * HD + n * rows * columns),
            transcendentals=n * rows * heads * 1024,
        ),
    )(info, marks, marks, *arrays)


def marks_of(doc_start, tile_mask):
    return jnp.concatenate([doc_start.reshape(-1, TILE), tile_mask.reshape(-1, TILE)])


def planar(tokens, norm_gain, w_query, cache_keys, cache_values, doc_start, tile_mask, group):
    devices = lax.axis_size("ctx")
    index = lax.axis_index("ctx")
    core = lax.axis_index("tp")
    place = lax.rem(index, group)
    tok_rows, width = tokens.shape
    kv_width = cache_keys.shape[1] // group
    q_width = w_query.shape[1] // group
    rows = group * tok_rows
    lines = [[first + k for first in range(0, devices, group)] for k in range(group)]
    far = range(1, group)

    def swapped(block, distance):
        return lax.ppermute(block, "ctx", [(i, i ^ distance) for i in range(devices)])

    def other_core(block):
        return lax.ppermute(block, "tp", [(0, 1), (1, 0)])

    def columns_for(array, distance, first, size, of, axis):
        at = lax.bitwise_xor(place, distance) * of + first
        return lax.dynamic_slice_in_dim(array, at, size, axis)

    def after(values, *earlier):
        flat = lax.optimization_barrier((tuple(values), tuple(earlier)))
        return list(flat[0])

    first_columns = (q_width // HD + 1) // 2 * HD
    cuts = ((0, first_columns), (first_columns, q_width))

    kv_own = jnp.stack([cache_keys, cache_values])
    w_cut = after([columns_for(w_query, d, 0, q_width, q_width, 1) for d in range(group)], kv_own)
    w_plane = w_cut[:1] + [swapped(w_cut[d], d) for d in far]
    kv_before = lax.ppermute(kv_own, "ctx", [(i, i + group) for i in range(devices - group)])

    float_tokens = tokens.astype(jnp.float32)
    squares = jnp.sum(float_tokens * float_tokens, axis=-1)
    squares = squares + other_core(squares)
    inverse = lax.rsqrt(squares / (2 * width) + epsilon)
    gain = lax.dynamic_slice_in_dim(norm_gain, core * width, width, 0)
    normed = (float_tokens * inverse[:, None] * gain).astype(jnp.bfloat16)

    w_plane = after(w_plane, kv_before, normed)
    w_stacks = [jnp.stack([block[:, low:high] for block in w_plane]) for low, high in cuts]
    w_chunks = [lax.all_gather(w_stacks[0], "ctx", axis=0, tiled=True, axis_index_groups=lines)]

    marks_own = marks_of(doc_start, tile_mask)
    marks_rows = marks_own.shape[0]
    bytes_own = jnp.concatenate([marks_own >> 16, (marks_own >> 8) & 255, marks_own & 255]).astype(jnp.bfloat16)
    bytes_own = jnp.pad(bytes_own, ((0, -bytes_own.shape[0] % 16), (0, 0)))

    def kv_for(d):
        cut = [columns_for(array, d, 0, kv_width, kv_width, 2).reshape(-1, kv_width) for array in (kv_before, kv_own)]
        return jnp.concatenate(cut + [bytes_own])

    kv_cut = after([kv_for(d) for d in range(group)], w_stacks[1])
    kv_parts = kv_cut[:1] + [swapped(kv_cut[d], d) for d in far]

    sent = jnp.stack([part[4 * tok_rows :] for part in kv_parts]).astype(jnp.int32)
    marks = sent[:, :marks_rows] * 65536 + sent[:, marks_rows : 2 * marks_rows] * 256
    marks = marks + sent[:, 2 * marks_rows : 3 * marks_rows]
    from_x, from_y = swapped(normed, 1), swapped(normed, 2)
    mine_other = other_core(normed)
    (w_after,) = after([w_stacks[1]], *kv_parts)
    w_chunks.append(lax.all_gather(w_after, "ctx", axis=0, tiled=True, axis_index_groups=lines))

    half = width // 2
    relay_y, relay_x = from_y[:, :half], from_x[:, half:]
    from_x, from_y, relay_y, relay_x = after([from_x, from_y, relay_y, relay_x], *kv_parts)
    corner_a, corner_b = swapped(relay_y, 1), swapped(relay_x, 2)
    token_parts = [[normed, mine_other]] + [[from_x, other_core(from_x)], [from_y, other_core(from_y)]]

    info = jnp.stack([(index // group - 1) * rows, place, core]).astype(jnp.int32)
    width_mask = tile_mask.shape[1]

    def call(distances, chunk, *earlier):
        chosen = [token_parts[d] for d in distances]
        (start,) = after([info], *earlier)
        return attend(start, marks, distances, chosen, chunk, kv_parts, 2, width_mask)

    pieces, last = {}, ()
    for chunk, distances in ((0, (2, 1, 0)), (0, (3,)), (1, (3, 2, 1)), (1, (0,))):
        if distances == (3,):
            corner = jnp.concatenate(after([corner_a, corner_b], *last), axis=1)
            token_parts.append([corner, other_core(corner)])
        outs = call(distances, w_chunks[chunk], *last)
        last = outs[:1]
        pieces.update({(d, chunk): swapped(out, d) if d else out for d, out in zip(distances, outs)})
    return joined(info, pieces, q_width, [low for low, _ in cuts], group * q_width)


def joined(info, pieces, q_width, lows, columns):
    keys = sorted(pieces)
    rows = pieces[keys[0]].shape[0]
    vmem = pl.BlockSpec(memory_space=pltpu.VMEM)

    def kernel(info_ref, *refs):
        out_ref = refs[-1]
        for k, (distance, chunk) in enumerate(keys):
            at = pl.multiple_of(lax.bitwise_xor(info_ref[1], distance) * q_width + lows[chunk], HD)
            out_ref[:, pl.ds(at, refs[k].shape[1])] = refs[k][...]

    return pl.pallas_call(
        kernel,
        out_shape=jax.ShapeDtypeStruct((rows, columns), jnp.bfloat16),
        in_specs=[pl.BlockSpec(memory_space=pltpu.SMEM)] + [vmem] * len(keys),
        out_specs=vmem,
        cost_estimate=pl.CostEstimate(flops=0, bytes_accessed=4 * rows * columns, transcendentals=0),
    )(info, *[pieces[key] for key in keys])


def plain(tokens, norm_gain, w_query, cache_keys, cache_values, doc_start, tile_mask):
    devices = lax.axis_size("ctx")
    index = lax.axis_index("ctx")
    tok_rows = tokens.shape[0]
    float_tokens = lax.all_gather(tokens, "tp", axis=1, tiled=True).astype(jnp.float32)
    inverse = lax.rsqrt(jnp.mean(float_tokens * float_tokens, axis=-1, keepdims=True) + epsilon)
    normed = (float_tokens * inverse * norm_gain).astype(jnp.bfloat16)
    kv_heads = cache_keys.shape[1] // HD
    q_width = w_query.shape[1] // kv_heads
    w_blocks = lax.all_gather(w_query, "ctx", axis=0)
    reach = (MAXDOC + tok_rows - 2) // tok_rows
    kv_own = jnp.stack([cache_keys, cache_values])
    shards = [
        lax.ppermute(kv_own, "ctx", [(i, i + distance) for i in range(devices - distance)])
        for distance in range(reach, 0, -1)
    ]
    kv_window = jnp.stack(shards + [kv_own])
    info = jnp.stack([(index - reach) * tok_rows, jnp.int32(0), jnp.int32(0)]).astype(jnp.int32)
    marks = marks_of(doc_start, tile_mask)[None]
    outs = [
        attend(
            info,
            marks,
            (0,),
            [[normed]],
            w_blocks[:, :, head * q_width : (head + 1) * q_width],
            [kv_window[:, :, :, head * HD : (head + 1) * HD].reshape(-1, HD)],
            reach + 1,
            tile_mask.shape[1],
        )[0]
        for head in range(kv_heads)
    ]
    return outs[0] if kv_heads == 1 else jnp.concatenate(outs, axis=1)


def on_device(*arrays):
    kv_heads = arrays[3].shape[1] // HD
    group = 4
    rows = group * arrays[0].shape[0]
    if kv_heads == group and lax.axis_size("ctx") % group == 0 and lax.axis_size("tp") == 2 and rows >= MAXDOC - 1:
        return planar(*arrays, group)
    return plain(*arrays)


def solution(mesh):
    return jax.shard_map(
        on_device,
        mesh=mesh,
        in_specs=(
            P("ctx", "tp"),
            P(),
            P("ctx", "tp"),
            P("ctx", "tp"),
            P("ctx", "tp"),
            P("ctx"),
            P("ctx", None),
        ),
        out_specs=P("ctx", "tp"),
        check_vma=False,
    )
```

```python
import math

import jax
import jax.numpy as jnp
from jax import lax
from jax.experimental import pallas as pl
from jax.experimental.pallas import tpu as pltpu
from jax.sharding import PartitionSpec as P

HD = 128
TILE = 128
MAXDOC = 2048
KEYS = 512
QUERIES = 256
CHUNKS = 4
FAR = 1 << 30
MASKED = -1e30


epsilon = 1e-05
exp2_scale = math.log2(math.e) / HD**0.5


def rows_kernel(counts, distances, shapes, info, marks_smem, marks_ref, *refs):
    parts, kv_count, halves, mask_width = counts
    tok_rows, shard_rows, source_rows = shapes
    n = len(distances)
    token_hbm = [refs[k * parts : (k + 1) * parts] for k in range(n)]
    w_hbm = refs[n * parts]
    kv_hbm = refs[n * parts + 1 :][:kv_count]
    out_hbm = refs[n * parts + 1 + kv_count :][:n]
    scratch = refs[n * parts + 1 + kv_count + n :]
    token_ref, w_ref, key_ref, value_ref, total_ref, query_ref, doc_full, acc_ref, max_ref, sum_ref, out_ref = scratch[:11]
    token_sem, w_sem, kv_sem, out_sem = scratch[11:]
    columns = w_ref.shape[1]
    heads = columns // HD
    depth = w_ref.shape[0]
    blocks = depth // source_rows
    swap = info[1]
    chunk = depth // CHUNKS
    chunks_part = CHUNKS // parts
    doc_rows = tok_rows // TILE
    window_rows = halves * kv_count * shard_rows
    base = window_rows - kv_count * shard_rows

    def token_copy(ref, at, c, slot):
        return pltpu.make_async_copy(
            ref.at[:, at * chunk : (at + 1) * chunk],
            token_ref.at[slot, :, c * chunk : (c + 1) * chunk],
            token_sem.at[slot, c],
        )

    def fetch_tokens(k, c):
        token_copy(token_hbm[k][c // chunks_part], c % chunks_part, c, k % 2).start()

    def rows_of(c):
        return lax.bitwise_xor(info[2], c // chunks_part) * chunks_part + c % chunks_part

    def w_copy(at, place):
        target = pl.ds(pl.multiple_of(place * source_rows, 16), source_rows)
        return pltpu.make_async_copy(w_hbm.at[at], w_ref.at[target], w_sem.at[place])

    blocks_chunk = blocks // CHUNKS

    def kv_copy(ref, half, which, place):
        target = pl.ds(pl.multiple_of(KEYS + place * shard_rows, 16), shard_rows)
        return pltpu.make_async_copy(
            ref.at[pl.ds((half * 2 + which) * shard_rows, shard_rows), :],
            (key_ref, value_ref)[which].at[target],
            kv_sem.at[place, which],
        )

    def out_copy(k, slot):
        return pltpu.make_async_copy(out_ref.at[slot], out_hbm[k], out_sem.at[slot])

    for c in range(CHUNKS):
        fetch_tokens(0, c)
        for at in range(blocks_chunk):
            place = rows_of(c) * blocks_chunk + at
            w_copy(lax.bitwise_xor(swap, place), place).start()
    for at in range(kv_count):
        for half in range(halves):
            for which in range(2):
                kv_copy(kv_hbm[at], half, which, half * kv_count + lax.bitwise_xor(swap, at)).start()
    key_ref[0:KEYS, :] = jnp.zeros((KEYS, HD), jnp.bfloat16)
    value_ref[0:KEYS, :] = jnp.zeros((KEYS, HD), jnp.bfloat16)

    stacked = heads * QUERIES
    subs = QUERIES // TILE

    def one_rows(k, carry):
        slot = lax.rem(k, 2)
        for ahead in range(1, n):

            @pl.when(k == ahead - 1)
            def _():
                for c in range(CHUNKS):
                    fetch_tokens(ahead, c)

        for c in range(CHUNKS):
            token_copy(token_hbm[0][0], 0, c, slot).wait()

            @pl.when(k == 0)
            def _():
                for at in range(blocks_chunk):
                    w_copy(0, rows_of(c) * blocks_chunk + at).wait()

            for first in range(0, tok_rows, QUERIES):
                piece = jnp.dot(
                    token_ref[slot, first : first + QUERIES, c * chunk : (c + 1) * chunk],
                    w_ref[pl.ds(pl.multiple_of(rows_of(c) * chunk, 16), chunk), :],
                    preferred_element_type=jnp.float32,
                )
                if c == 0:
                    total_ref[first : first + QUERIES, :] = piece
                else:
                    total_ref[first : first + QUERIES, :] += piece
        for tile in range(tok_rows // QUERIES):
            for head in range(heads):
                at = (tile * heads + head) * QUERIES
                query_ref[at : at + QUERIES, :] = total_ref[
                    tile * QUERIES : (tile + 1) * QUERIES, head * HD : (head + 1) * HD
                ].astype(jnp.bfloat16)

        @pl.when(k == 0)
        def _():
            for place in range(kv_count * halves):
                for which in range(2):
                    kv_copy(kv_hbm[0], 0, which, place).wait()

        @pl.when(k >= 2)
        def _():
            out_copy(0, slot).wait()

        distance = jnp.int32(distances[0])
        for other in range(1, n):
            distance = jnp.where(k == other, distances[other], distance)
        rows_first = base + lax.bitwise_xor(swap, distance) * tok_rows

        def one_tile(tile, carry):
            query = query_ref[pl.ds(pl.multiple_of(tile * stacked, stacked), stacked), :]
            row_first = rows_first + tile * QUERIES
            end = row_first + QUERIES
            for sub in range(subs):
                docs_row = marks_ref[distance, pl.ds(tile * subs + sub, 1), :].astype(jnp.float32)
                doc_full[sub] = jnp.transpose(jnp.broadcast_to(docs_row, (TILE, TILE))).astype(jnp.int32)
            first_key = marks_smem[distance, tile * subs, 0] - info[0]
            count = (end - first_key + KEYS - 1) // KEYS

            def one_block(back, carry):
                start = end - (back + 1) * KEYS
                at = pl.multiple_of(start + KEYS, TILE)
                keys = key_ref[pl.ds(at, KEYS), :]
                values = value_ref[pl.ds(at, KEYS), :]
                key_tile = (info[0] + start) // TILE
                lane = lax.broadcasted_iota(jnp.int32, (TILE, TILE), 1)
                row = lax.broadcasted_iota(jnp.int32, (TILE, TILE), 0)
                bias_rows = []
                for sub in range(subs):
                    causal = row + (row_first + sub * TILE - start)
                    docs = doc_full[sub] - (info[0] + start)
                    pieces = []
                    for m in range(KEYS // TILE):
                        column = lax.min(lax.max(key_tile + m, 0), mask_width - 1)
                        flat = (tile * subs + sub) * mask_width + column
                        shut = jnp.where(marks_smem[distance, doc_rows + flat // TILE, lax.rem(flat, TILE)] == 1, 0, FAR)
                        seen = (lane <= causal - m * TILE) & (lane >= docs + (shut - m * TILE))
                        pieces.append(jnp.where(seen, 0.0, MASKED))
                    bias_rows.append(jnp.concatenate(pieces, axis=1))
                bias = jnp.concatenate(bias_rows, axis=0)
                spans = [slice(head * QUERIES, (head + 1) * QUERIES) for head in range(heads)]
                scores = [
                    bias
                    + lax.dot_general(
                        query[span], keys, (((1,), (1,)), ((), ())), preferred_element_type=jnp.float32
                    )
                    for span in spans
                ]
                olds = [max_ref[span, :] for span in spans]
                news = [jnp.maximum(old, jnp.max(x, axis=1, keepdims=True)) for old, x in zip(olds, scores)]
                for span, x, old, new in zip(spans, scores, olds, news):
                    alpha = jnp.exp2((old - new) * exp2_scale)
                    shift = jnp.concatenate([new * exp2_scale] * (KEYS // HD), axis=1)
                    weights = jnp.exp2(x * exp2_scale - shift)
                    max_ref[span, :] = new
                    folded = weights[:, :HD]
                    for m in range(1, KEYS // HD):
                        folded = folded + weights[:, m * HD : (m + 1) * HD]
                    sum_ref[span, :] = sum_ref[span, :] * alpha + folded
                    product = jnp.dot(weights.astype(jnp.bfloat16), values, preferred_element_type=jnp.float32)
                    acc_ref[span, :] = acc_ref[span, :] * alpha + product
                return carry

            max_ref[...] = jnp.full(max_ref.shape, MASKED, jnp.float32)
            sum_ref[...] = jnp.zeros(sum_ref.shape, jnp.float32)
            acc_ref[...] = jnp.zeros(acc_ref.shape, jnp.float32)
            lax.fori_loop(0, count, one_block, 0)
            result = acc_ref[...] / jnp.sum(sum_ref[...], axis=1, keepdims=True)
            for head in range(heads):
                out_ref[slot, pl.ds(pl.multiple_of(tile * QUERIES, QUERIES), QUERIES), head * HD : (head + 1) * HD] = (
                    result[head * QUERIES : (head + 1) * QUERIES].astype(out_ref.dtype)
                )
            return carry

        lax.fori_loop(0, tok_rows // QUERIES, one_tile, 0)
        for at in range(n):

            @pl.when(k == at)
            def _():
                out_copy(at, at % 2).start()

        return carry

    lax.fori_loop(0, n, one_rows, 0)
    for k in range(max(n - 2, 0), n):
        out_copy(k, k % 2).wait()


def attend(info, marks, distances, token_parts, w_blocks, kv_parts, halves, mask_width):
    n = len(distances)
    parts = len(token_parts[0])
    rows = token_parts[0][0].shape[0]
    source_rows, columns = w_blocks.shape[1:]
    depth = w_blocks.shape[0] * source_rows
    heads = columns // HD
    shard_rows = kv_parts[0].shape[0] // (2 * halves) // TILE * TILE
    shards = len(kv_parts) * halves
    vmem = pl.BlockSpec(memory_space=pltpu.VMEM)
    smem = pl.BlockSpec(memory_space=pltpu.SMEM)
    leave = pl.BlockSpec(memory_space=pl.ANY)
    arrays = [part for block in token_parts for part in block] + [w_blocks] + list(kv_parts)
    counts = (parts, len(kv_parts), halves, mask_width)
    tile_rows = heads * QUERIES

    def kernel(*refs):
        rows_kernel(counts, distances, (rows, shard_rows, source_rows), *refs)

    return pl.pallas_call(
        kernel,
        out_shape=[jax.ShapeDtypeStruct((rows, columns), jnp.bfloat16)] * n,
        in_specs=[smem, smem, vmem] + [leave] * len(arrays),
        out_specs=[leave] * n,
        scratch_shapes=[
            pltpu.VMEM((2, rows, depth), jnp.bfloat16),
            pltpu.VMEM((depth, columns), jnp.bfloat16),
            pltpu.VMEM((KEYS + shards * shard_rows, HD), jnp.bfloat16),
            pltpu.VMEM((KEYS + shards * shard_rows, HD), jnp.bfloat16),
            pltpu.VMEM((rows, columns), jnp.float32),
            pltpu.VMEM((rows * heads, HD), jnp.bfloat16),
            pltpu.VMEM((QUERIES // TILE, TILE, TILE), jnp.int32),
            pltpu.VMEM((tile_rows, HD), jnp.float32),
            pltpu.VMEM((tile_rows, HD), jnp.float32),
            pltpu.VMEM((tile_rows, HD), jnp.float32),
            pltpu.VMEM((2, rows, columns), jnp.bfloat16),
            pltpu.SemaphoreType.DMA((2, CHUNKS)),
            pltpu.SemaphoreType.DMA((w_blocks.shape[0],)),
            pltpu.SemaphoreType.DMA((shards, 2)),
            pltpu.SemaphoreType.DMA((2,)),
        ],
        compiler_params=pltpu.CompilerParams(vmem_limit_bytes=60 << 20),
        cost_estimate=pl.CostEstimate(
            flops=n * (2 * rows * depth * columns + 4 * rows * columns * 1024),
            bytes_accessed=2 * (n * rows * depth + depth * columns + shards * 2 * shard_rows * HD + n * rows * columns),
            transcendentals=n * rows * heads * 1024,
        ),
    )(info, marks, marks, *arrays)


def marks_of(doc_start, tile_mask):
    return jnp.concatenate([doc_start.reshape(-1, TILE), tile_mask.reshape(-1, TILE)])


def planar(tokens, norm_gain, w_query, cache_keys, cache_values, doc_start, tile_mask, group):
    devices = lax.axis_size("ctx")
    index = lax.axis_index("ctx")
    core = lax.axis_index("tp")
    place = lax.rem(index, group)
    tok_rows, width = tokens.shape
    kv_width = cache_keys.shape[1] // group
    q_width = w_query.shape[1] // group
    rows = group * tok_rows
    lines = [[first + k for first in range(0, devices, group)] for k in range(group)]
    far = range(1, group)

    def swapped(block, distance):
        return lax.ppermute(block, "ctx", [(i, i ^ distance) for i in range(devices)])

    def other_core(block):
        return lax.ppermute(block, "tp", [(0, 1), (1, 0)])

    def columns_for(array, distance, first, size, of, axis):
        at = lax.bitwise_xor(place, distance) * of + first
        return lax.dynamic_slice_in_dim(array, at, size, axis)

    def after(values, *earlier):
        flat = lax.optimization_barrier((tuple(values), tuple(earlier)))
        return list(flat[0])

    first_columns = (q_width // HD + 1) // 2 * HD
    cuts = ((0, first_columns), (first_columns, q_width))

    w_cut = [columns_for(w_query, d, 0, q_width, q_width, 1) for d in range(group)]
    w_plane = w_cut[:1] + [swapped(w_cut[d], d) for d in far]
    float_tokens = tokens.astype(jnp.float32)
    squares = jnp.sum(float_tokens * float_tokens, axis=-1)
    squares = squares + other_core(squares)
    inverse = lax.rsqrt(squares / (2 * width) + epsilon)
    gain = lax.dynamic_slice_in_dim(norm_gain, core * width, width, 0)
    normed = (float_tokens * inverse[:, None] * gain).astype(jnp.bfloat16)

    w_plane = after(w_plane, normed)
    w_stacks = [jnp.stack([block[:, low:high] for block in w_plane]) for low, high in cuts]
    w_chunks = [lax.all_gather(w_stacks[0], "ctx", axis=0, tiled=True, axis_index_groups=lines)]

    (keys_later,) = after([cache_keys], w_stacks[0])
    kv_own = jnp.stack([keys_later, cache_values])
    kv_before = lax.ppermute(kv_own, "ctx", [(i, i + group) for i in range(devices - group)])

    marks_own = marks_of(doc_start, tile_mask)
    marks_rows = marks_own.shape[0]
    bytes_own = jnp.concatenate([marks_own >> 16, (marks_own >> 8) & 255, marks_own & 255]).astype(jnp.bfloat16)
    bytes_own = jnp.pad(bytes_own, ((0, -bytes_own.shape[0] % 16), (0, 0)))

    def kv_for(d):
        cut = [columns_for(array, d, 0, kv_width, kv_width, 2).reshape(-1, kv_width) for array in (kv_before, kv_own)]
        return jnp.concatenate(cut + [bytes_own])

    kv_cut = after([kv_for(d) for d in range(group)], w_stacks[1])
    kv_parts = kv_cut[:1] + [swapped(kv_cut[d], d) for d in far]

    sent = jnp.stack([part[4 * tok_rows :] for part in kv_parts]).astype(jnp.int32)
    marks = sent[:, :marks_rows] * 65536 + sent[:, marks_rows : 2 * marks_rows] * 256
    marks = marks + sent[:, 2 * marks_rows : 3 * marks_rows]
    from_x, from_y = swapped(normed, 1), swapped(normed, 2)
    mine_other = other_core(normed)
    (w_after,) = after([w_stacks[1]], *kv_parts)
    w_chunks.append(lax.all_gather(w_after, "ctx", axis=0, tiled=True, axis_index_groups=lines))

    half = width // 2
    relay_y, relay_x = from_y[:, :half], from_x[:, half:]
    from_x, from_y, relay_y, relay_x = after([from_x, from_y, relay_y, relay_x], *kv_parts)
    corner_a, corner_b = swapped(relay_y, 1), swapped(relay_x, 2)
    token_parts = [[normed, mine_other]] + [[from_x, other_core(from_x)], [from_y, other_core(from_y)]]

    info = jnp.stack([(index // group - 1) * rows, place, core]).astype(jnp.int32)
    width_mask = tile_mask.shape[1]

    def call(distances, chunk, *earlier):
        chosen = [token_parts[d] for d in distances]
        (start,) = after([info], *earlier)
        return attend(start, marks, distances, chosen, chunk, kv_parts, 2, width_mask)

    pieces, last = {}, ()
    for chunk, distances in ((0, (2, 1, 0)), (0, (3,)), (1, (3, 2, 1)), (1, (0,))):
        if distances == (3,):
            corner = jnp.concatenate(after([corner_a, corner_b], *last), axis=1)
            token_parts.append([corner, other_core(corner)])
        outs = call(distances, w_chunks[chunk], *last)
        last = outs[:1]
        pieces.update({(d, chunk): swapped(out, d) if d else out for d, out in zip(distances, outs)})
    return joined(info, pieces, q_width, [low for low, _ in cuts], group * q_width)


def joined(info, pieces, q_width, lows, columns):
    keys = sorted(pieces)
    rows = pieces[keys[0]].shape[0]
    vmem = pl.BlockSpec(memory_space=pltpu.VMEM)

    def kernel(info_ref, *refs):
        out_ref = refs[-1]
        for k, (distance, chunk) in enumerate(keys):
            at = pl.multiple_of(lax.bitwise_xor(info_ref[1], distance) * q_width + lows[chunk], HD)
            out_ref[:, pl.ds(at, refs[k].shape[1])] = refs[k][...]

    return pl.pallas_call(
        kernel,
        out_shape=jax.ShapeDtypeStruct((rows, columns), jnp.bfloat16),
        in_specs=[pl.BlockSpec(memory_space=pltpu.SMEM)] + [vmem] * len(keys),
        out_specs=vmem,
        cost_estimate=pl.CostEstimate(flops=0, bytes_accessed=4 * rows * columns, transcendentals=0),
    )(info, *[pieces[key] for key in keys])


def plain(tokens, norm_gain, w_query, cache_keys, cache_values, doc_start, tile_mask):
    devices = lax.axis_size("ctx")
    index = lax.axis_index("ctx")
    tok_rows = tokens.shape[0]
    float_tokens = lax.all_gather(tokens, "tp", axis=1, tiled=True).astype(jnp.float32)
    inverse = lax.rsqrt(jnp.mean(float_tokens * float_tokens, axis=-1, keepdims=True) + epsilon)
    normed = (float_tokens * inverse * norm_gain).astype(jnp.bfloat16)
    kv_heads = cache_keys.shape[1] // HD
    q_width = w_query.shape[1] // kv_heads
    w_blocks = lax.all_gather(w_query, "ctx", axis=0)
    reach = (MAXDOC + tok_rows - 2) // tok_rows
    kv_own = jnp.stack([cache_keys, cache_values])
    shards = [
        lax.ppermute(kv_own, "ctx", [(i, i + distance) for i in range(devices - distance)])
        for distance in range(reach, 0, -1)
    ]
    kv_window = jnp.stack(shards + [kv_own])
    info = jnp.stack([(index - reach) * tok_rows, jnp.int32(0), jnp.int32(0)]).astype(jnp.int32)
    marks = marks_of(doc_start, tile_mask)[None]
    outs = [
        attend(
            info,
            marks,
            (0,),
            [[normed]],
            w_blocks[:, :, head * q_width : (head + 1) * q_width],
            [kv_window[:, :, :, head * HD : (head + 1) * HD].reshape(-1, HD)],
            reach + 1,
            tile_mask.shape[1],
        )[0]
        for head in range(kv_heads)
    ]
    return outs[0] if kv_heads == 1 else jnp.concatenate(outs, axis=1)


def on_device(*arrays):
    kv_heads = arrays[3].shape[1] // HD
    group = 4
    rows = group * arrays[0].shape[0]
    if kv_heads == group and lax.axis_size("ctx") % group == 0 and lax.axis_size("tp") == 2 and rows >= MAXDOC - 1:
        return planar(*arrays, group)
    return plain(*arrays)


def solution(mesh):
    return jax.shard_map(
        on_device,
        mesh=mesh,
        in_specs=(
            P("ctx", "tp"),
            P(),
            P("ctx", "tp"),
            P("ctx", "tp"),
            P("ctx", "tp"),
            P("ctx"),
            P("ctx", None),
        ),
        out_specs=P("ctx", "tp"),
        check_vma=False,
    )
```

```python
import math

import jax
import jax.numpy as jnp
from jax import lax
from jax.experimental import pallas as pl
from jax.experimental.pallas import tpu as pltpu
from jax.sharding import PartitionSpec as P

HD = 128
TILE = 128
MAXDOC = 2048
KEYS = 512
QUERIES = 256
CHUNKS = 4
FAR = 1 << 30
MASKED = -1e30


epsilon = 1e-05
exp2_scale = math.log2(math.e) / HD**0.5


def rows_kernel(counts, distances, shapes, info, marks_smem, marks_ref, *refs):
    parts, kv_count, halves, mask_width = counts
    tok_rows, shard_rows, source_rows = shapes
    n = len(distances)
    token_hbm = [refs[k * parts : (k + 1) * parts] for k in range(n)]
    w_hbm = refs[n * parts]
    kv_hbm = refs[n * parts + 1 :][:kv_count]
    out_hbm = refs[n * parts + 1 + kv_count :][:n]
    scratch = refs[n * parts + 1 + kv_count + n :]
    token_ref, w_ref, key_ref, value_ref, total_ref, query_ref, doc_full, acc_ref, max_ref, sum_ref, out_ref = scratch[:11]
    token_sem, w_sem, kv_sem, out_sem = scratch[11:]
    columns = w_ref.shape[1]
    heads = columns // HD
    depth = w_ref.shape[0]
    blocks = depth // source_rows
    swap = info[1]
    chunk = depth // CHUNKS
    chunks_part = CHUNKS // parts
    doc_rows = tok_rows // TILE
    window_rows = halves * kv_count * shard_rows
    base = window_rows - kv_count * shard_rows

    def token_copy(ref, at, c, slot):
        return pltpu.make_async_copy(
            ref.at[:, at * chunk : (at + 1) * chunk],
            token_ref.at[slot, :, c * chunk : (c + 1) * chunk],
            token_sem.at[slot, c],
        )

    def fetch_tokens(k, c):
        token_copy(token_hbm[k][c // chunks_part], c % chunks_part, c, k % 2).start()

    def rows_of(c):
        return lax.bitwise_xor(info[2], c // chunks_part) * chunks_part + c % chunks_part

    def w_copy(at, place):
        target = pl.ds(pl.multiple_of(place * source_rows, 16), source_rows)
        return pltpu.make_async_copy(w_hbm.at[at], w_ref.at[target], w_sem.at[place])

    blocks_chunk = blocks // CHUNKS

    def kv_copy(ref, half, which, place):
        target = pl.ds(pl.multiple_of(KEYS + place * shard_rows, 16), shard_rows)
        return pltpu.make_async_copy(
            ref.at[pl.ds((half * 2 + which) * shard_rows, shard_rows), :],
            (key_ref, value_ref)[which].at[target],
            kv_sem.at[place, which],
        )

    def out_copy(k, slot):
        return pltpu.make_async_copy(out_ref.at[slot], out_hbm[k], out_sem.at[slot])

    for c in range(CHUNKS):
        fetch_tokens(0, c)
        for at in range(blocks_chunk):
            place = rows_of(c) * blocks_chunk + at
            w_copy(lax.bitwise_xor(swap, place), place).start()
    for at in range(kv_count):
        for half in range(halves):
            for which in range(2):
                kv_copy(kv_hbm[at], half, which, half * kv_count + lax.bitwise_xor(swap, at)).start()
    key_ref[0:KEYS, :] = jnp.zeros((KEYS, HD), jnp.bfloat16)
    value_ref[0:KEYS, :] = jnp.zeros((KEYS, HD), jnp.bfloat16)

    stacked = heads * QUERIES
    subs = QUERIES // TILE

    def one_rows(k, carry):
        slot = lax.rem(k, 2)
        for ahead in range(1, n):

            @pl.when(k == ahead - 1)
            def _():
                for c in range(CHUNKS):
                    fetch_tokens(ahead, c)

        for c in range(CHUNKS):
            token_copy(token_hbm[0][0], 0, c, slot).wait()

            @pl.when(k == 0)
            def _():
                for at in range(blocks_chunk):
                    w_copy(0, rows_of(c) * blocks_chunk + at).wait()

            for first in range(0, tok_rows, QUERIES):
                piece = jnp.dot(
                    token_ref[slot, first : first + QUERIES, c * chunk : (c + 1) * chunk],
                    w_ref[pl.ds(pl.multiple_of(rows_of(c) * chunk, 16), chunk), :],
                    preferred_element_type=jnp.float32,
                )
                if c == 0:
                    total_ref[first : first + QUERIES, :] = piece
                else:
                    total_ref[first : first + QUERIES, :] += piece
        for tile in range(tok_rows // QUERIES):
            for head in range(heads):
                at = (tile * heads + head) * QUERIES
                query_ref[at : at + QUERIES, :] = total_ref[
                    tile * QUERIES : (tile + 1) * QUERIES, head * HD : (head + 1) * HD
                ].astype(jnp.bfloat16)

        @pl.when(k == 0)
        def _():
            for place in range(kv_count * halves):
                for which in range(2):
                    kv_copy(kv_hbm[0], 0, which, place).wait()

        @pl.when(k >= 2)
        def _():
            out_copy(0, slot).wait()

        distance = jnp.int32(distances[0])
        for other in range(1, n):
            distance = jnp.where(k == other, distances[other], distance)
        rows_first = base + lax.bitwise_xor(swap, distance) * tok_rows

        def one_tile(tile, carry):
            query = query_ref[pl.ds(pl.multiple_of(tile * stacked, stacked), stacked), :]
            row_first = rows_first + tile * QUERIES
            end = row_first + QUERIES
            for sub in range(subs):
                docs_row = marks_ref[distance, pl.ds(tile * subs + sub, 1), :].astype(jnp.float32)
                doc_full[sub] = jnp.transpose(jnp.broadcast_to(docs_row, (TILE, TILE))).astype(jnp.int32)
            first_key = marks_smem[distance, tile * subs, 0] - info[0]
            count = (end - first_key + KEYS - 1) // KEYS

            def one_block(back, carry):
                start = end - (back + 1) * KEYS
                at = pl.multiple_of(start + KEYS, TILE)
                keys = key_ref[pl.ds(at, KEYS), :]
                values = value_ref[pl.ds(at, KEYS), :]
                key_tile = (info[0] + start) // TILE
                lane = lax.broadcasted_iota(jnp.int32, (TILE, TILE), 1)
                row = lax.broadcasted_iota(jnp.int32, (TILE, TILE), 0)
                bias_rows = []
                for sub in range(subs):
                    causal = row + (row_first + sub * TILE - start)
                    docs = doc_full[sub] - (info[0] + start)
                    pieces = []
                    for m in range(KEYS // TILE):
                        column = lax.min(lax.max(key_tile + m, 0), mask_width - 1)
                        flat = (tile * subs + sub) * mask_width + column
                        shut = jnp.where(marks_smem[distance, doc_rows + flat // TILE, lax.rem(flat, TILE)] == 1, 0, FAR)
                        seen = (lane <= causal - m * TILE) & (lane >= docs + (shut - m * TILE))
                        pieces.append(jnp.where(seen, 0.0, MASKED))
                    bias_rows.append(jnp.concatenate(pieces, axis=1))
                bias = jnp.concatenate(bias_rows, axis=0)
                spans = [slice(head * QUERIES, (head + 1) * QUERIES) for head in range(heads)]
                scores = [
                    bias
                    + lax.dot_general(
                        query[span], keys, (((1,), (1,)), ((), ())), preferred_element_type=jnp.float32
                    )
                    for span in spans
                ]
                olds = [max_ref[span, :] for span in spans]
                news = [jnp.maximum(old, jnp.max(x, axis=1, keepdims=True)) for old, x in zip(olds, scores)]
                for span, x, old, new in zip(spans, scores, olds, news):
                    alpha = jnp.exp2((old - new) * exp2_scale)
                    shift = jnp.concatenate([new * exp2_scale] * (KEYS // HD), axis=1)
                    weights = jnp.exp2(x * exp2_scale - shift)
                    max_ref[span, :] = new
                    folded = weights[:, :HD]
                    for m in range(1, KEYS // HD):
                        folded = folded + weights[:, m * HD : (m + 1) * HD]
                    sum_ref[span, :] = sum_ref[span, :] * alpha + folded
                    product = jnp.dot(weights.astype(jnp.bfloat16), values, preferred_element_type=jnp.float32)
                    acc_ref[span, :] = acc_ref[span, :] * alpha + product
                return carry

            max_ref[...] = jnp.full(max_ref.shape, MASKED, jnp.float32)
            sum_ref[...] = jnp.zeros(sum_ref.shape, jnp.float32)
            acc_ref[...] = jnp.zeros(acc_ref.shape, jnp.float32)
            lax.fori_loop(0, count, one_block, 0)
            result = acc_ref[...] / jnp.sum(sum_ref[...], axis=1, keepdims=True)
            for head in range(heads):
                out_ref[slot, pl.ds(pl.multiple_of(tile * QUERIES, QUERIES), QUERIES), head * HD : (head + 1) * HD] = (
                    result[head * QUERIES : (head + 1) * QUERIES].astype(out_ref.dtype)
                )
            return carry

        lax.fori_loop(0, tok_rows // QUERIES, one_tile, 0)
        for at in range(n):

            @pl.when(k == at)
            def _():
                out_copy(at, at % 2).start()

        return carry

    lax.fori_loop(0, n, one_rows, 0)
    for k in range(max(n - 2, 0), n):
        out_copy(k, k % 2).wait()


def attend(info, marks, distances, token_parts, w_blocks, kv_parts, halves, mask_width):
    n = len(distances)
    parts = len(token_parts[0])
    rows = token_parts[0][0].shape[0]
    source_rows, columns = w_blocks.shape[1:]
    depth = w_blocks.shape[0] * source_rows
    heads = columns // HD
    shard_rows = kv_parts[0].shape[0] // (2 * halves) // TILE * TILE
    shards = len(kv_parts) * halves
    vmem = pl.BlockSpec(memory_space=pltpu.VMEM)
    smem = pl.BlockSpec(memory_space=pltpu.SMEM)
    leave = pl.BlockSpec(memory_space=pl.ANY)
    arrays = [part for block in token_parts for part in block] + [w_blocks] + list(kv_parts)
    counts = (parts, len(kv_parts), halves, mask_width)
    tile_rows = heads * QUERIES

    def kernel(*refs):
        rows_kernel(counts, distances, (rows, shard_rows, source_rows), *refs)

    return pl.pallas_call(
        kernel,
        out_shape=[jax.ShapeDtypeStruct((rows, columns), jnp.bfloat16)] * n,
        in_specs=[smem, smem, vmem] + [leave] * len(arrays),
        out_specs=[leave] * n,
        scratch_shapes=[
            pltpu.VMEM((2, rows, depth), jnp.bfloat16),
            pltpu.VMEM((depth, columns), jnp.bfloat16),
            pltpu.VMEM((KEYS + shards * shard_rows, HD), jnp.bfloat16),
            pltpu.VMEM((KEYS + shards * shard_rows, HD), jnp.bfloat16),
            pltpu.VMEM((rows, columns), jnp.float32),
            pltpu.VMEM((rows * heads, HD), jnp.bfloat16),
            pltpu.VMEM((QUERIES // TILE, TILE, TILE), jnp.int32),
            pltpu.VMEM((tile_rows, HD), jnp.float32),
            pltpu.VMEM((tile_rows, HD), jnp.float32),
            pltpu.VMEM((tile_rows, HD), jnp.float32),
            pltpu.VMEM((2, rows, columns), jnp.bfloat16),
            pltpu.SemaphoreType.DMA((2, CHUNKS)),
            pltpu.SemaphoreType.DMA((w_blocks.shape[0],)),
            pltpu.SemaphoreType.DMA((shards, 2)),
            pltpu.SemaphoreType.DMA((2,)),
        ],
        compiler_params=pltpu.CompilerParams(vmem_limit_bytes=60 << 20),
        cost_estimate=pl.CostEstimate(
            flops=n * (2 * rows * depth * columns + 4 * rows * columns * 1024),
            bytes_accessed=2 * (n * rows * depth + depth * columns + shards * 2 * shard_rows * HD + n * rows * columns),
            transcendentals=n * rows * heads * 1024,
        ),
    )(info, marks, marks, *arrays)


def marks_of(doc_start, tile_mask):
    return jnp.concatenate([doc_start.reshape(-1, TILE), tile_mask.reshape(-1, TILE)])


def planar(tokens, norm_gain, w_query, cache_keys, cache_values, doc_start, tile_mask, group):
    devices = lax.axis_size("ctx")
    index = lax.axis_index("ctx")
    core = lax.axis_index("tp")
    place = lax.rem(index, group)
    tok_rows, width = tokens.shape
    kv_width = cache_keys.shape[1] // group
    q_width = w_query.shape[1] // group
    rows = group * tok_rows
    lines = [[first + k for first in range(0, devices, group)] for k in range(group)]
    far = range(1, group)

    def swapped(block, distance):
        return lax.ppermute(block, "ctx", [(i, i ^ distance) for i in range(devices)])

    def other_core(block):
        return lax.ppermute(block, "tp", [(0, 1), (1, 0)])

    def columns_for(array, distance, first, size, of, axis):
        at = lax.bitwise_xor(place, distance) * of + first
        return lax.dynamic_slice_in_dim(array, at, size, axis)

    def after(values, *earlier):
        flat = lax.optimization_barrier((tuple(values), tuple(earlier)))
        return list(flat[0])

    first_columns = (q_width // HD + 1) // 2 * HD
    cuts = ((0, first_columns), (first_columns, q_width))

    def w_blocks_of(chunk, *earlier):
        low, high = cuts[chunk]
        blocks = after([columns_for(w_query, d, low, high - low, q_width, 1) for d in range(group)], *earlier)
        return blocks[:1] + [swapped(blocks[d], d) for d in far]

    w_first = w_blocks_of(0)

    float_tokens = tokens.astype(jnp.float32)
    squares = jnp.sum(float_tokens * float_tokens, axis=-1)
    squares = squares + other_core(squares)
    inverse = lax.rsqrt(squares / (2 * width) + epsilon)
    gain = lax.dynamic_slice_in_dim(norm_gain, core * width, width, 0)
    normed = (float_tokens * inverse[:, None] * gain).astype(jnp.bfloat16)

    w_stacks = [jnp.stack(after(w_first, normed))]
    w_chunks = [lax.all_gather(w_stacks[0], "ctx", axis=0, tiled=True, axis_index_groups=lines)]

    (keys_later,) = after([cache_keys], w_stacks[0])
    kv_own = jnp.stack([keys_later, cache_values])
    kv_before = lax.ppermute(kv_own, "ctx", [(i, i + group) for i in range(devices - group)])

    marks_own = marks_of(doc_start, tile_mask)
    marks_rows = marks_own.shape[0]
    bytes_own = jnp.concatenate([marks_own >> 16, (marks_own >> 8) & 255, marks_own & 255]).astype(jnp.bfloat16)
    bytes_own = jnp.pad(bytes_own, ((0, -bytes_own.shape[0] % 16), (0, 0)))

    def kv_for(d):
        cut = [columns_for(array, d, 0, kv_width, kv_width, 2).reshape(-1, kv_width) for array in (kv_before, kv_own)]
        return jnp.concatenate(cut + [bytes_own])

    kv_cut = [kv_for(d) for d in range(group)]
    w_stacks.append(jnp.stack(w_blocks_of(1, *kv_cut)))
    kv_parts = kv_cut[:1] + [swapped(kv_cut[d], d) for d in far]

    sent = jnp.stack([part[4 * tok_rows :] for part in kv_parts]).astype(jnp.int32)
    marks = sent[:, :marks_rows] * 65536 + sent[:, marks_rows : 2 * marks_rows] * 256
    marks = marks + sent[:, 2 * marks_rows : 3 * marks_rows]
    from_x, from_y = swapped(normed, 1), swapped(normed, 2)
    mine_other = other_core(normed)
    (w_after,) = after([w_stacks[1]], *kv_parts)
    w_chunks.append(lax.all_gather(w_after, "ctx", axis=0, tiled=True, axis_index_groups=lines))

    half = width // 2
    relay_y, relay_x = from_y[:, :half], from_x[:, half:]
    from_x, from_y, relay_y, relay_x = after([from_x, from_y, relay_y, relay_x], *kv_parts, w_stacks[1])
    corner_a, corner_b = swapped(relay_y, 1), swapped(relay_x, 2)
    token_parts = [[normed, mine_other]] + [[from_x, other_core(from_x)], [from_y, other_core(from_y)]]

    info = jnp.stack([(index // group - 1) * rows, place, core]).astype(jnp.int32)
    width_mask = tile_mask.shape[1]

    def call(distances, chunk, *earlier):
        chosen = [token_parts[d] for d in distances]
        (start,) = after([info], *earlier)
        return attend(start, marks, distances, chosen, chunk, kv_parts, 2, width_mask)

    pieces, last = {}, ()
    for chunk, distances in ((0, (2, 1, 0)), (0, (3,)), (1, (3, 2, 1)), (1, (0,))):
        if distances == (3,):
            corner = jnp.concatenate(after([corner_a, corner_b], *last), axis=1)
            token_parts.append([corner, other_core(corner)])
        outs = call(distances, w_chunks[chunk], *last)
        last = outs[:1]
        pieces.update({(d, chunk): swapped(out, d) if d else out for d, out in zip(distances, outs)})
    return joined(info, pieces, q_width, [low for low, _ in cuts], group * q_width)


def joined(info, pieces, q_width, lows, columns):
    keys = sorted(pieces)
    rows = pieces[keys[0]].shape[0]
    vmem = pl.BlockSpec(memory_space=pltpu.VMEM)

    def kernel(info_ref, *refs):
        out_ref = refs[-1]
        for k, (distance, chunk) in enumerate(keys):
            at = pl.multiple_of(lax.bitwise_xor(info_ref[1], distance) * q_width + lows[chunk], HD)
            out_ref[:, pl.ds(at, refs[k].shape[1])] = refs[k][...]

    return pl.pallas_call(
        kernel,
        out_shape=jax.ShapeDtypeStruct((rows, columns), jnp.bfloat16),
        in_specs=[pl.BlockSpec(memory_space=pltpu.SMEM)] + [vmem] * len(keys),
        out_specs=vmem,
        cost_estimate=pl.CostEstimate(flops=0, bytes_accessed=4 * rows * columns, transcendentals=0),
    )(info, *[pieces[key] for key in keys])


def plain(tokens, norm_gain, w_query, cache_keys, cache_values, doc_start, tile_mask):
    devices = lax.axis_size("ctx")
    index = lax.axis_index("ctx")
    tok_rows = tokens.shape[0]
    float_tokens = lax.all_gather(tokens, "tp", axis=1, tiled=True).astype(jnp.float32)
    inverse = lax.rsqrt(jnp.mean(float_tokens * float_tokens, axis=-1, keepdims=True) + epsilon)
    normed = (float_tokens * inverse * norm_gain).astype(jnp.bfloat16)
    kv_heads = cache_keys.shape[1] // HD
    q_width = w_query.shape[1] // kv_heads
    w_blocks = lax.all_gather(w_query, "ctx", axis=0)
    reach = (MAXDOC + tok_rows - 2) // tok_rows
    kv_own = jnp.stack([cache_keys, cache_values])
    shards = [
        lax.ppermute(kv_own, "ctx", [(i, i + distance) for i in range(devices - distance)])
        for distance in range(reach, 0, -1)
    ]
    kv_window = jnp.stack(shards + [kv_own])
    info = jnp.stack([(index - reach) * tok_rows, jnp.int32(0), jnp.int32(0)]).astype(jnp.int32)
    marks = marks_of(doc_start, tile_mask)[None]
    outs = [
        attend(
            info,
            marks,
            (0,),
            [[normed]],
            w_blocks[:, :, head * q_width : (head + 1) * q_width],
            [kv_window[:, :, :, head * HD : (head + 1) * HD].reshape(-1, HD)],
            reach + 1,
            tile_mask.shape[1],
        )[0]
        for head in range(kv_heads)
    ]
    return outs[0] if kv_heads == 1 else jnp.concatenate(outs, axis=1)


def on_device(*arrays):
    kv_heads = arrays[3].shape[1] // HD
    group = 4
    rows = group * arrays[0].shape[0]
    if kv_heads == group and lax.axis_size("ctx") % group == 0 and lax.axis_size("tp") == 2 and rows >= MAXDOC - 1:
        return planar(*arrays, group)
    return plain(*arrays)


def solution(mesh):
    return jax.shard_map(
        on_device,
        mesh=mesh,
        in_specs=(
            P("ctx", "tp"),
            P(),
            P("ctx", "tp"),
            P("ctx", "tp"),
            P("ctx", "tp"),
            P("ctx"),
            P("ctx", None),
        ),
        out_specs=P("ctx", "tp"),
        check_vma=False,
    )
```

```python
import math

import jax
import jax.numpy as jnp
from jax import lax
from jax.experimental import pallas as pl
from jax.experimental.pallas import tpu as pltpu
from jax.sharding import PartitionSpec as P

HD = 128
TILE = 128
MAXDOC = 2048
KEYS = 512
QUERIES = 256
CHUNKS = 4
FAR = 1 << 30
MASKED = -1e30


epsilon = 1e-05
exp2_scale = math.log2(math.e) / HD**0.5


def rows_kernel(counts, distances, shapes, info, marks_smem, marks_ref, *refs):
    parts, kv_count, halves, mask_width = counts
    tok_rows, shard_rows, source_rows = shapes
    n = len(distances)
    token_hbm = [refs[k * parts : (k + 1) * parts] for k in range(n)]
    w_hbm = refs[n * parts]
    kv_hbm = refs[n * parts + 1 :][:kv_count]
    out_hbm = refs[n * parts + 1 + kv_count :][:n]
    scratch = refs[n * parts + 1 + kv_count + n :]
    token_ref, w_ref, key_ref, value_ref, total_ref, query_ref, doc_full, acc_ref, max_ref, sum_ref, out_ref = scratch[:11]
    token_sem, w_sem, kv_sem, out_sem = scratch[11:]
    columns = w_ref.shape[1]
    heads = columns // HD
    depth = w_ref.shape[0]
    blocks = depth // source_rows
    swap = info[1]
    chunk = depth // CHUNKS
    chunks_part = CHUNKS // parts
    doc_rows = tok_rows // TILE
    window_rows = halves * kv_count * shard_rows
    base = window_rows - kv_count * shard_rows

    def token_copy(ref, at, c, slot):
        return pltpu.make_async_copy(
            ref.at[:, at * chunk : (at + 1) * chunk],
            token_ref.at[slot, :, c * chunk : (c + 1) * chunk],
            token_sem.at[slot, c],
        )

    def fetch_tokens(k, c):
        token_copy(token_hbm[k][c // chunks_part], c % chunks_part, c, k % 2).start()

    def rows_of(c):
        return lax.bitwise_xor(info[2], c // chunks_part) * chunks_part + c % chunks_part

    def w_copy(at, place):
        target = pl.ds(pl.multiple_of(place * source_rows, 16), source_rows)
        return pltpu.make_async_copy(w_hbm.at[at], w_ref.at[target], w_sem.at[place])

    blocks_chunk = blocks // CHUNKS

    def kv_copy(ref, half, which, place):
        target = pl.ds(pl.multiple_of(KEYS + place * shard_rows, 16), shard_rows)
        return pltpu.make_async_copy(
            ref.at[pl.ds((half * 2 + which) * shard_rows, shard_rows), :],
            (key_ref, value_ref)[which].at[target],
            kv_sem.at[place, which],
        )

    def out_copy(k, slot):
        return pltpu.make_async_copy(out_ref.at[slot], out_hbm[k], out_sem.at[slot])

    for c in range(CHUNKS):
        fetch_tokens(0, c)
        for at in range(blocks_chunk):
            place = rows_of(c) * blocks_chunk + at
            w_copy(lax.bitwise_xor(swap, place), place).start()
    for at in range(kv_count):
        for half in range(halves):
            for which in range(2):
                kv_copy(kv_hbm[at], half, which, half * kv_count + lax.bitwise_xor(swap, at)).start()
    key_ref[0:KEYS, :] = jnp.zeros((KEYS, HD), jnp.bfloat16)
    value_ref[0:KEYS, :] = jnp.zeros((KEYS, HD), jnp.bfloat16)

    stacked = heads * QUERIES
    subs = QUERIES // TILE

    def one_rows(k, carry):
        slot = lax.rem(k, 2)
        for ahead in range(1, n):

            @pl.when(k == ahead - 1)
            def _():
                for c in range(CHUNKS):
                    fetch_tokens(ahead, c)

        for c in range(CHUNKS):
            token_copy(token_hbm[0][0], 0, c, slot).wait()

            @pl.when(k == 0)
            def _():
                for at in range(blocks_chunk):
                    w_copy(0, rows_of(c) * blocks_chunk + at).wait()

            for first in range(0, tok_rows, QUERIES):
                piece = jnp.dot(
                    token_ref[slot, first : first + QUERIES, c * chunk : (c + 1) * chunk],
                    w_ref[pl.ds(pl.multiple_of(rows_of(c) * chunk, 16), chunk), :],
                    preferred_element_type=jnp.float32,
                )
                if c == 0:
                    total_ref[first : first + QUERIES, :] = piece
                else:
                    total_ref[first : first + QUERIES, :] += piece
        for tile in range(tok_rows // QUERIES):
            for head in range(heads):
                at = (tile * heads + head) * QUERIES
                query_ref[at : at + QUERIES, :] = total_ref[
                    tile * QUERIES : (tile + 1) * QUERIES, head * HD : (head + 1) * HD
                ].astype(jnp.bfloat16)

        @pl.when(k == 0)
        def _():
            for place in range(kv_count * halves):
                for which in range(2):
                    kv_copy(kv_hbm[0], 0, which, place).wait()

        @pl.when(k >= 2)
        def _():
            out_copy(0, slot).wait()

        distance = jnp.int32(distances[0])
        for other in range(1, n):
            distance = jnp.where(k == other, distances[other], distance)
        rows_first = base + lax.bitwise_xor(swap, distance) * tok_rows

        def one_tile(tile, carry):
            query = query_ref[pl.ds(pl.multiple_of(tile * stacked, stacked), stacked), :]
            row_first = rows_first + tile * QUERIES
            end = row_first + QUERIES
            for sub in range(subs):
                docs_row = marks_ref[distance, pl.ds(tile * subs + sub, 1), :].astype(jnp.float32)
                doc_full[sub] = jnp.transpose(jnp.broadcast_to(docs_row, (TILE, TILE))).astype(jnp.int32)
            first_key = marks_smem[distance, tile * subs, 0] - info[0]
            count = (end - first_key + KEYS - 1) // KEYS

            def one_block(back, carry):
                start = end - (back + 1) * KEYS
                at = pl.multiple_of(start + KEYS, TILE)
                keys = key_ref[pl.ds(at, KEYS), :]
                values = value_ref[pl.ds(at, KEYS), :]
                key_tile = (info[0] + start) // TILE
                lane = lax.broadcasted_iota(jnp.int32, (TILE, TILE), 1)
                row = lax.broadcasted_iota(jnp.int32, (TILE, TILE), 0)
                bias_rows = []
                for sub in range(subs):
                    causal = row + (row_first + sub * TILE - start)
                    docs = doc_full[sub] - (info[0] + start)
                    pieces = []
                    for m in range(KEYS // TILE):
                        column = lax.min(lax.max(key_tile + m, 0), mask_width - 1)
                        flat = (tile * subs + sub) * mask_width + column
                        shut = jnp.where(marks_smem[distance, doc_rows + flat // TILE, lax.rem(flat, TILE)] == 1, 0, FAR)
                        seen = (lane <= causal - m * TILE) & (lane >= docs + (shut - m * TILE))
                        pieces.append(jnp.where(seen, 0.0, MASKED))
                    bias_rows.append(jnp.concatenate(pieces, axis=1))
                bias = jnp.concatenate(bias_rows, axis=0)
                spans = [slice(head * QUERIES, (head + 1) * QUERIES) for head in range(heads)]
                scores = [
                    bias
                    + lax.dot_general(
                        query[span], keys, (((1,), (1,)), ((), ())), preferred_element_type=jnp.float32
                    )
                    for span in spans
                ]
                olds = [max_ref[span, :] for span in spans]
                news = [jnp.maximum(old, jnp.max(x, axis=1, keepdims=True)) for old, x in zip(olds, scores)]
                for span, x, old, new in zip(spans, scores, olds, news):
                    alpha = jnp.exp2((old - new) * exp2_scale)
                    shift = jnp.concatenate([new * exp2_scale] * (KEYS // HD), axis=1)
                    weights = jnp.exp2(x * exp2_scale - shift)
                    max_ref[span, :] = new
                    folded = weights[:, :HD]
                    for m in range(1, KEYS // HD):
                        folded = folded + weights[:, m * HD : (m + 1) * HD]
                    sum_ref[span, :] = sum_ref[span, :] * alpha + folded
                    product = jnp.dot(weights.astype(jnp.bfloat16), values, preferred_element_type=jnp.float32)
                    acc_ref[span, :] = acc_ref[span, :] * alpha + product
                return carry

            max_ref[...] = jnp.full(max_ref.shape, MASKED, jnp.float32)
            sum_ref[...] = jnp.zeros(sum_ref.shape, jnp.float32)
            acc_ref[...] = jnp.zeros(acc_ref.shape, jnp.float32)
            lax.fori_loop(0, count, one_block, 0)
            result = acc_ref[...] / jnp.sum(sum_ref[...], axis=1, keepdims=True)
            for head in range(heads):
                out_ref[slot, pl.ds(pl.multiple_of(tile * QUERIES, QUERIES), QUERIES), head * HD : (head + 1) * HD] = (
                    result[head * QUERIES : (head + 1) * QUERIES].astype(out_ref.dtype)
                )
            return carry

        lax.fori_loop(0, tok_rows // QUERIES, one_tile, 0)
        for at in range(n):

            @pl.when(k == at)
            def _():
                out_copy(at, at % 2).start()

        return carry

    lax.fori_loop(0, n, one_rows, 0)
    for k in range(max(n - 2, 0), n):
        out_copy(k, k % 2).wait()


def attend(info, marks, distances, token_parts, w_blocks, kv_parts, halves, mask_width):
    n = len(distances)
    parts = len(token_parts[0])
    rows = token_parts[0][0].shape[0]
    source_rows, columns = w_blocks.shape[1:]
    depth = w_blocks.shape[0] * source_rows
    heads = columns // HD
    shard_rows = kv_parts[0].shape[0] // (2 * halves) // TILE * TILE
    shards = len(kv_parts) * halves
    vmem = pl.BlockSpec(memory_space=pltpu.VMEM)
    smem = pl.BlockSpec(memory_space=pltpu.SMEM)
    leave = pl.BlockSpec(memory_space=pl.ANY)
    arrays = [part for block in token_parts for part in block] + [w_blocks] + list(kv_parts)
    counts = (parts, len(kv_parts), halves, mask_width)
    tile_rows = heads * QUERIES

    def kernel(*refs):
        rows_kernel(counts, distances, (rows, shard_rows, source_rows), *refs)

    return pl.pallas_call(
        kernel,
        out_shape=[jax.ShapeDtypeStruct((rows, columns), jnp.bfloat16)] * n,
        in_specs=[smem, smem, vmem] + [leave] * len(arrays),
        out_specs=[leave] * n,
        scratch_shapes=[
            pltpu.VMEM((2, rows, depth), jnp.bfloat16),
            pltpu.VMEM((depth, columns), jnp.bfloat16),
            pltpu.VMEM((KEYS + shards * shard_rows, HD), jnp.bfloat16),
            pltpu.VMEM((KEYS + shards * shard_rows, HD), jnp.bfloat16),
            pltpu.VMEM((rows, columns), jnp.float32),
            pltpu.VMEM((rows * heads, HD), jnp.bfloat16),
            pltpu.VMEM((QUERIES // TILE, TILE, TILE), jnp.int32),
            pltpu.VMEM((tile_rows, HD), jnp.float32),
            pltpu.VMEM((tile_rows, HD), jnp.float32),
            pltpu.VMEM((tile_rows, HD), jnp.float32),
            pltpu.VMEM((2, rows, columns), jnp.bfloat16),
            pltpu.SemaphoreType.DMA((2, CHUNKS)),
            pltpu.SemaphoreType.DMA((w_blocks.shape[0],)),
            pltpu.SemaphoreType.DMA((shards, 2)),
            pltpu.SemaphoreType.DMA((2,)),
        ],
        compiler_params=pltpu.CompilerParams(vmem_limit_bytes=60 << 20),
        cost_estimate=pl.CostEstimate(
            flops=n * (2 * rows * depth * columns + 4 * rows * columns * 1024),
            bytes_accessed=2 * (n * rows * depth + depth * columns + shards * 2 * shard_rows * HD + n * rows * columns),
            transcendentals=n * rows * heads * 1024,
        ),
    )(info, marks, marks, *arrays)


def marks_of(doc_start, tile_mask):
    return jnp.concatenate([doc_start.reshape(-1, TILE), tile_mask.reshape(-1, TILE)])


def planar(tokens, norm_gain, w_query, cache_keys, cache_values, doc_start, tile_mask, group):
    devices = lax.axis_size("ctx")
    index = lax.axis_index("ctx")
    core = lax.axis_index("tp")
    place = lax.rem(index, group)
    tok_rows, width = tokens.shape
    kv_width = cache_keys.shape[1] // group
    q_width = w_query.shape[1] // group
    rows = group * tok_rows
    lines = [[first + k for first in range(0, devices, group)] for k in range(group)]
    far = range(1, group)

    def swapped(block, distance):
        return lax.ppermute(block, "ctx", [(i, i ^ distance) for i in range(devices)])

    def other_core(block):
        return lax.ppermute(block, "tp", [(0, 1), (1, 0)])

    def columns_for(array, distance, first, size, of, axis):
        at = lax.bitwise_xor(place, distance) * of + first
        return lax.dynamic_slice_in_dim(array, at, size, axis)

    def after(values, *earlier):
        flat = lax.optimization_barrier((tuple(values), tuple(earlier)))
        return list(flat[0])

    first_columns = (q_width // HD + 1) // 2 * HD
    cuts = ((0, first_columns), (first_columns, q_width))

    w_cut = [columns_for(w_query, d, 0, q_width, q_width, 1) for d in range(group)]
    kv_own = jnp.stack(after([cache_keys, cache_values], *w_cut))
    kv_before = lax.ppermute(kv_own, "ctx", [(i, i + group) for i in range(devices - group)])
    w_plane = w_cut[:1] + [swapped(w_cut[d], d) for d in far]
    float_tokens = tokens.astype(jnp.float32)
    squares = jnp.sum(float_tokens * float_tokens, axis=-1)
    squares = squares + other_core(squares)
    inverse = lax.rsqrt(squares / (2 * width) + epsilon)
    gain = lax.dynamic_slice_in_dim(norm_gain, core * width, width, 0)
    normed = (float_tokens * inverse[:, None] * gain).astype(jnp.bfloat16)

    w_plane = after(w_plane, kv_before, normed)
    w_stacks = [jnp.stack([block[:, low:high] for block in w_plane]) for low, high in cuts]
    w_chunks = [lax.all_gather(w_stacks[0], "ctx", axis=0, tiled=True, axis_index_groups=lines)]

    marks_own = marks_of(doc_start, tile_mask)
    marks_rows = marks_own.shape[0]
    bytes_own = jnp.concatenate([marks_own >> 16, (marks_own >> 8) & 255, marks_own & 255]).astype(jnp.bfloat16)
    bytes_own = jnp.pad(bytes_own, ((0, -bytes_own.shape[0] % 16), (0, 0)))

    def kv_for(d):
        cut = [columns_for(array, d, 0, kv_width, kv_width, 2).reshape(-1, kv_width) for array in (kv_before, kv_own)]
        return jnp.concatenate(cut + [bytes_own])

    kv_cut = after([kv_for(d) for d in range(group)], w_stacks[1])
    kv_parts = kv_cut[:1] + [swapped(kv_cut[d], d) for d in far]

    sent = jnp.stack([part[4 * tok_rows :] for part in kv_parts]).astype(jnp.int32)
    marks = sent[:, :marks_rows] * 65536 + sent[:, marks_rows : 2 * marks_rows] * 256
    marks = marks + sent[:, 2 * marks_rows : 3 * marks_rows]
    from_x, from_y = swapped(normed, 1), swapped(normed, 2)
    mine_other = other_core(normed)
    (w_after,) = after([w_stacks[1]], *kv_parts)
    w_chunks.append(lax.all_gather(w_after, "ctx", axis=0, tiled=True, axis_index_groups=lines))

    half = width // 2
    relay_y, relay_x = from_y[:, :half], from_x[:, half:]
    from_x, from_y, relay_y, relay_x = after([from_x, from_y, relay_y, relay_x], *kv_parts)
    corner_a, corner_b = swapped(relay_y, 1), swapped(relay_x, 2)
    token_parts = [[normed, mine_other]] + [[from_x, other_core(from_x)], [from_y, other_core(from_y)]]

    info = jnp.stack([(index // group - 1) * rows, place, core]).astype(jnp.int32)
    width_mask = tile_mask.shape[1]

    def call(distances, chunk, *earlier):
        chosen = [token_parts[d] for d in distances]
        (start,) = after([info], *earlier)
        return attend(start, marks, distances, chosen, chunk, kv_parts, 2, width_mask)

    pieces, last = {}, ()
    for chunk, distances in ((0, (2, 1, 0)), (0, (3,)), (1, (3, 2, 1)), (1, (0,))):
        if distances == (3,):
            corner = jnp.concatenate(after([corner_a, corner_b], *last), axis=1)
            token_parts.append([corner, other_core(corner)])
        outs = call(distances, w_chunks[chunk], *last)
        last = outs[:1]
        pieces.update({(d, chunk): swapped(out, d) if d else out for d, out in zip(distances, outs)})
    return joined(info, pieces, q_width, [low for low, _ in cuts], group * q_width)


def joined(info, pieces, q_width, lows, columns):
    keys = sorted(pieces)
    rows = pieces[keys[0]].shape[0]
    vmem = pl.BlockSpec(memory_space=pltpu.VMEM)

    def kernel(info_ref, *refs):
        out_ref = refs[-1]
        for k, (distance, chunk) in enumerate(keys):
            at = pl.multiple_of(lax.bitwise_xor(info_ref[1], distance) * q_width + lows[chunk], HD)
            out_ref[:, pl.ds(at, refs[k].shape[1])] = refs[k][...]

    return pl.pallas_call(
        kernel,
        out_shape=jax.ShapeDtypeStruct((rows, columns), jnp.bfloat16),
        in_specs=[pl.BlockSpec(memory_space=pltpu.SMEM)] + [vmem] * len(keys),
        out_specs=vmem,
        cost_estimate=pl.CostEstimate(flops=0, bytes_accessed=4 * rows * columns, transcendentals=0),
    )(info, *[pieces[key] for key in keys])


def plain(tokens, norm_gain, w_query, cache_keys, cache_values, doc_start, tile_mask):
    devices = lax.axis_size("ctx")
    index = lax.axis_index("ctx")
    tok_rows = tokens.shape[0]
    float_tokens = lax.all_gather(tokens, "tp", axis=1, tiled=True).astype(jnp.float32)
    inverse = lax.rsqrt(jnp.mean(float_tokens * float_tokens, axis=-1, keepdims=True) + epsilon)
    normed = (float_tokens * inverse * norm_gain).astype(jnp.bfloat16)
    kv_heads = cache_keys.shape[1] // HD
    q_width = w_query.shape[1] // kv_heads
    w_blocks = lax.all_gather(w_query, "ctx", axis=0)
    reach = (MAXDOC + tok_rows - 2) // tok_rows
    kv_own = jnp.stack([cache_keys, cache_values])
    shards = [
        lax.ppermute(kv_own, "ctx", [(i, i + distance) for i in range(devices - distance)])
        for distance in range(reach, 0, -1)
    ]
    kv_window = jnp.stack(shards + [kv_own])
    info = jnp.stack([(index - reach) * tok_rows, jnp.int32(0), jnp.int32(0)]).astype(jnp.int32)
    marks = marks_of(doc_start, tile_mask)[None]
    outs = [
        attend(
            info,
            marks,
            (0,),
            [[normed]],
            w_blocks[:, :, head * q_width : (head + 1) * q_width],
            [kv_window[:, :, :, head * HD : (head + 1) * HD].reshape(-1, HD)],
            reach + 1,
            tile_mask.shape[1],
        )[0]
        for head in range(kv_heads)
    ]
    return outs[0] if kv_heads == 1 else jnp.concatenate(outs, axis=1)


def on_device(*arrays):
    kv_heads = arrays[3].shape[1] // HD
    group = 4
    rows = group * arrays[0].shape[0]
    if kv_heads == group and lax.axis_size("ctx") % group == 0 and lax.axis_size("tp") == 2 and rows >= MAXDOC - 1:
        return planar(*arrays, group)
    return plain(*arrays)


def solution(mesh):
    return jax.shard_map(
        on_device,
        mesh=mesh,
        in_specs=(
            P("ctx", "tp"),
            P(),
            P("ctx", "tp"),
            P("ctx", "tp"),
            P("ctx", "tp"),
            P("ctx"),
            P("ctx", None),
        ),
        out_specs=P("ctx", "tp"),
        check_vma=False,
    )
```

```python
import math

import jax
import jax.numpy as jnp
from jax import lax
from jax.experimental import pallas as pl
from jax.experimental.pallas import tpu as pltpu
from jax.sharding import PartitionSpec as P

HD = 128
TILE = 128
MAXDOC = 2048
KEYS = 512
QUERIES = 256
CHUNKS = 4
FAR = 1 << 30
MASKED = -1e30


epsilon = 1e-05
exp2_scale = math.log2(math.e) / HD**0.5


def rows_kernel(counts, distances, shapes, info, marks_smem, marks_ref, *refs):
    parts, kv_count, halves, mask_width = counts
    tok_rows, shard_rows, source_rows = shapes
    n = len(distances)
    token_hbm = [refs[k * parts : (k + 1) * parts] for k in range(n)]
    w_hbm = refs[n * parts]
    kv_hbm = refs[n * parts + 1 :][:kv_count]
    out_hbm = refs[n * parts + 1 + kv_count :][:n]
    scratch = refs[n * parts + 1 + kv_count + n :]
    token_ref, w_ref, key_ref, value_ref, total_ref, query_ref, doc_full, acc_ref, max_ref, sum_ref, out_ref = scratch[:11]
    token_sem, w_sem, kv_sem, out_sem = scratch[11:]
    columns = w_ref.shape[1]
    heads = columns // HD
    depth = w_ref.shape[0]
    blocks = depth // source_rows
    swap = info[1]
    chunk = depth // CHUNKS
    chunks_part = CHUNKS // parts
    doc_rows = tok_rows // TILE
    window_rows = halves * kv_count * shard_rows
    base = window_rows - kv_count * shard_rows

    def token_copy(ref, at, c, slot):
        return pltpu.make_async_copy(
            ref.at[:, at * chunk : (at + 1) * chunk],
            token_ref.at[slot, :, c * chunk : (c + 1) * chunk],
            token_sem.at[slot, c],
        )

    def fetch_tokens(k, c):
        token_copy(token_hbm[k][c // chunks_part], c % chunks_part, c, k % 2).start()

    def rows_of(c):
        return lax.bitwise_xor(info[2], c // chunks_part) * chunks_part + c % chunks_part

    def w_copy(at, place):
        target = pl.ds(pl.multiple_of(place * source_rows, 16), source_rows)
        return pltpu.make_async_copy(w_hbm.at[at], w_ref.at[target], w_sem.at[place])

    blocks_chunk = blocks // CHUNKS

    def kv_copy(ref, half, which, place):
        target = pl.ds(pl.multiple_of(KEYS + place * shard_rows, 16), shard_rows)
        return pltpu.make_async_copy(
            ref.at[pl.ds((half * 2 + which) * shard_rows, shard_rows), :],
            (key_ref, value_ref)[which].at[target],
            kv_sem.at[place, which],
        )

    def out_copy(k, slot):
        return pltpu.make_async_copy(out_ref.at[slot], out_hbm[k], out_sem.at[slot])

    for c in range(CHUNKS):
        fetch_tokens(0, c)
        for at in range(blocks_chunk):
            place = rows_of(c) * blocks_chunk + at
            w_copy(lax.bitwise_xor(swap, place), place).start()
    for at in range(kv_count):
        for half in range(halves):
            for which in range(2):
                kv_copy(kv_hbm[at], half, which, half * kv_count + lax.bitwise_xor(swap, at)).start()
    key_ref[0:KEYS, :] = jnp.zeros((KEYS, HD), jnp.bfloat16)
    value_ref[0:KEYS, :] = jnp.zeros((KEYS, HD), jnp.bfloat16)

    stacked = heads * QUERIES
    subs = QUERIES // TILE

    def one_rows(k, carry):
        slot = lax.rem(k, 2)
        for ahead in range(1, n):

            @pl.when(k == ahead - 1)
            def _():
                for c in range(CHUNKS):
                    fetch_tokens(ahead, c)

        for c in range(CHUNKS):
            token_copy(token_hbm[0][0], 0, c, slot).wait()

            @pl.when(k == 0)
            def _():
                for at in range(blocks_chunk):
                    w_copy(0, rows_of(c) * blocks_chunk + at).wait()

            for first in range(0, tok_rows, QUERIES):
                piece = jnp.dot(
                    token_ref[slot, first : first + QUERIES, c * chunk : (c + 1) * chunk],
                    w_ref[pl.ds(pl.multiple_of(rows_of(c) * chunk, 16), chunk), :],
                    preferred_element_type=jnp.float32,
                )
                if c == 0:
                    total_ref[first : first + QUERIES, :] = piece
                else:
                    total_ref[first : first + QUERIES, :] += piece
        for tile in range(tok_rows // QUERIES):
            for head in range(heads):
                at = (tile * heads + head) * QUERIES
                query_ref[at : at + QUERIES, :] = total_ref[
                    tile * QUERIES : (tile + 1) * QUERIES, head * HD : (head + 1) * HD
                ].astype(jnp.bfloat16)

        @pl.when(k == 0)
        def _():
            for place in range(kv_count * halves):
                for which in range(2):
                    kv_copy(kv_hbm[0], 0, which, place).wait()

        @pl.when(k >= 2)
        def _():
            out_copy(0, slot).wait()

        distance = jnp.int32(distances[0])
        for other in range(1, n):
            distance = jnp.where(k == other, distances[other], distance)
        rows_first = base + lax.bitwise_xor(swap, distance) * tok_rows

        def one_tile(tile, carry):
            query = query_ref[pl.ds(pl.multiple_of(tile * stacked, stacked), stacked), :]
            row_first = rows_first + tile * QUERIES
            end = row_first + QUERIES
            for sub in range(subs):
                docs_row = marks_ref[distance, pl.ds(tile * subs + sub, 1), :].astype(jnp.float32)
                doc_full[sub] = jnp.transpose(jnp.broadcast_to(docs_row, (TILE, TILE))).astype(jnp.int32)
            first_key = marks_smem[distance, tile * subs, 0] - info[0]
            count = (end - first_key + KEYS - 1) // KEYS

            def one_block(back, carry):
                start = end - (back + 1) * KEYS
                at = pl.multiple_of(start + KEYS, TILE)
                keys = key_ref[pl.ds(at, KEYS), :]
                values = value_ref[pl.ds(at, KEYS), :]
                key_tile = (info[0] + start) // TILE
                lane = lax.broadcasted_iota(jnp.int32, (TILE, TILE), 1)
                row = lax.broadcasted_iota(jnp.int32, (TILE, TILE), 0)
                bias_rows = []
                for sub in range(subs):
                    causal = row + (row_first + sub * TILE - start)
                    docs = doc_full[sub] - (info[0] + start)
                    pieces = []
                    for m in range(KEYS // TILE):
                        column = lax.min(lax.max(key_tile + m, 0), mask_width - 1)
                        flat = (tile * subs + sub) * mask_width + column
                        shut = jnp.where(marks_smem[distance, doc_rows + flat // TILE, lax.rem(flat, TILE)] == 1, 0, FAR)
                        seen = (lane <= causal - m * TILE) & (lane >= docs + (shut - m * TILE))
                        pieces.append(jnp.where(seen, 0.0, MASKED))
                    bias_rows.append(jnp.concatenate(pieces, axis=1))
                bias = jnp.concatenate(bias_rows, axis=0)
                spans = [slice(head * QUERIES, (head + 1) * QUERIES) for head in range(heads)]
                scores = [
                    bias
                    + lax.dot_general(
                        query[span], keys, (((1,), (1,)), ((), ())), preferred_element_type=jnp.float32
                    )
                    for span in spans
                ]
                olds = [max_ref[span, :] for span in spans]
                news = [jnp.maximum(old, jnp.max(x, axis=1, keepdims=True)) for old, x in zip(olds, scores)]
                for span, x, old, new in zip(spans, scores, olds, news):
                    alpha = jnp.exp2((old - new) * exp2_scale)
                    shift = jnp.concatenate([new * exp2_scale] * (KEYS // HD), axis=1)
                    weights = jnp.exp2(x * exp2_scale - shift)
                    max_ref[span, :] = new
                    folded = weights[:, :HD]
                    for m in range(1, KEYS // HD):
                        folded = folded + weights[:, m * HD : (m + 1) * HD]
                    sum_ref[span, :] = sum_ref[span, :] * alpha + folded
                    product = jnp.dot(weights.astype(jnp.bfloat16), values, preferred_element_type=jnp.float32)
                    acc_ref[span, :] = acc_ref[span, :] * alpha + product
                return carry

            max_ref[...] = jnp.full(max_ref.shape, MASKED, jnp.float32)
            sum_ref[...] = jnp.zeros(sum_ref.shape, jnp.float32)
            acc_ref[...] = jnp.zeros(acc_ref.shape, jnp.float32)
            lax.fori_loop(0, count, one_block, 0)
            result = acc_ref[...] / jnp.sum(sum_ref[...], axis=1, keepdims=True)
            for head in range(heads):
                out_ref[slot, pl.ds(pl.multiple_of(tile * QUERIES, QUERIES), QUERIES), head * HD : (head + 1) * HD] = (
                    result[head * QUERIES : (head + 1) * QUERIES].astype(out_ref.dtype)
                )
            return carry

        lax.fori_loop(0, tok_rows // QUERIES, one_tile, 0)
        for at in range(n):

            @pl.when(k == at)
            def _():
                out_copy(at, at % 2).start()

        return carry

    lax.fori_loop(0, n, one_rows, 0)
    for k in range(max(n - 2, 0), n):
        out_copy(k, k % 2).wait()


def attend(info, marks, distances, token_parts, w_blocks, kv_parts, halves, mask_width):
    n = len(distances)
    parts = len(token_parts[0])
    rows = token_parts[0][0].shape[0]
    source_rows, columns = w_blocks.shape[1:]
    depth = w_blocks.shape[0] * source_rows
    heads = columns // HD
    shard_rows = kv_parts[0].shape[0] // (2 * halves) // TILE * TILE
    shards = len(kv_parts) * halves
    vmem = pl.BlockSpec(memory_space=pltpu.VMEM)
    smem = pl.BlockSpec(memory_space=pltpu.SMEM)
    leave = pl.BlockSpec(memory_space=pl.ANY)
    arrays = [part for block in token_parts for part in block] + [w_blocks] + list(kv_parts)
    counts = (parts, len(kv_parts), halves, mask_width)
    tile_rows = heads * QUERIES

    def kernel(*refs):
        rows_kernel(counts, distances, (rows, shard_rows, source_rows), *refs)

    return pl.pallas_call(
        kernel,
        out_shape=[jax.ShapeDtypeStruct((rows, columns), jnp.bfloat16)] * n,
        in_specs=[smem, smem, vmem] + [leave] * len(arrays),
        out_specs=[leave] * n,
        scratch_shapes=[
            pltpu.VMEM((2, rows, depth), jnp.bfloat16),
            pltpu.VMEM((depth, columns), jnp.bfloat16),
            pltpu.VMEM((KEYS + shards * shard_rows, HD), jnp.bfloat16),
            pltpu.VMEM((KEYS + shards * shard_rows, HD), jnp.bfloat16),
            pltpu.VMEM((rows, columns), jnp.float32),
            pltpu.VMEM((rows * heads, HD), jnp.bfloat16),
            pltpu.VMEM((QUERIES // TILE, TILE, TILE), jnp.int32),
            pltpu.VMEM((tile_rows, HD), jnp.float32),
            pltpu.VMEM((tile_rows, HD), jnp.float32),
            pltpu.VMEM((tile_rows, HD), jnp.float32),
            pltpu.VMEM((2, rows, columns), jnp.bfloat16),
            pltpu.SemaphoreType.DMA((2, CHUNKS)),
            pltpu.SemaphoreType.DMA((w_blocks.shape[0],)),
            pltpu.SemaphoreType.DMA((shards, 2)),
            pltpu.SemaphoreType.DMA((2,)),
        ],
        compiler_params=pltpu.CompilerParams(vmem_limit_bytes=60 << 20),
        cost_estimate=pl.CostEstimate(
            flops=n * (2 * rows * depth * columns + 4 * rows * columns * 1024),
            bytes_accessed=2 * (n * rows * depth + depth * columns + shards * 2 * shard_rows * HD + n * rows * columns),
            transcendentals=n * rows * heads * 1024,
        ),
    )(info, marks, marks, *arrays)


def marks_of(doc_start, tile_mask):
    return jnp.concatenate([doc_start.reshape(-1, TILE), tile_mask.reshape(-1, TILE)])


def planar(tokens, norm_gain, w_query, cache_keys, cache_values, doc_start, tile_mask, group):
    devices = lax.axis_size("ctx")
    index = lax.axis_index("ctx")
    core = lax.axis_index("tp")
    place = lax.rem(index, group)
    tok_rows, width = tokens.shape
    kv_width = cache_keys.shape[1] // group
    q_width = w_query.shape[1] // group
    rows = group * tok_rows
    lines = [[first + k for first in range(0, devices, group)] for k in range(group)]
    far = range(1, group)

    def swapped(block, distance):
        return lax.ppermute(block, "ctx", [(i, i ^ distance) for i in range(devices)])

    def other_core(block):
        return lax.ppermute(block, "tp", [(0, 1), (1, 0)])

    def columns_for(array, distance, first, size, of, axis):
        at = lax.bitwise_xor(place, distance) * of + first
        return lax.dynamic_slice_in_dim(array, at, size, axis)

    def after(values, *earlier):
        flat = lax.optimization_barrier((tuple(values), tuple(earlier)))
        return list(flat[0])

    first_columns = (q_width // HD + 1) // 2 * HD
    cuts = ((0, first_columns), (first_columns, q_width))

    w_cut = [columns_for(w_query, d, 0, q_width, q_width, 1) for d in range(group)]
    kv_own = jnp.stack(after([cache_keys, cache_values], *w_cut))
    kv_before = lax.ppermute(kv_own, "ctx", [(i, i + group) for i in range(devices - group)])
    w_plane = w_cut[:1] + [swapped(w_cut[d], d) for d in far]
    float_tokens = tokens.astype(jnp.float32)
    squares = jnp.sum(float_tokens * float_tokens, axis=-1)
    squares = squares + other_core(squares)
    inverse = lax.rsqrt(squares / (2 * width) + epsilon)
    gain = lax.dynamic_slice_in_dim(norm_gain, core * width, width, 0)
    normed = (float_tokens * inverse[:, None] * gain).astype(jnp.bfloat16)

    w_plane = after(w_plane, kv_before, normed)
    w_stacks = [jnp.stack([block[:, low:high] for block in w_plane]) for low, high in cuts]
    w_chunks = [lax.all_gather(w_stacks[0], "ctx", axis=0, tiled=True, axis_index_groups=lines)]

    marks_own = marks_of(doc_start, tile_mask)
    marks_rows = marks_own.shape[0]
    bytes_own = jnp.concatenate([marks_own >> 16, (marks_own >> 8) & 255, marks_own & 255]).astype(jnp.bfloat16)
    bytes_own = jnp.pad(bytes_own, ((0, -bytes_own.shape[0] % 16), (0, 0)))

    def kv_for(d):
        cut = [columns_for(array, d, 0, kv_width, kv_width, 2).reshape(-1, kv_width) for array in (kv_before, kv_own)]
        return jnp.concatenate(cut + [bytes_own])

    kv_cut = after([kv_for(d) for d in range(group)], w_stacks[1])
    kv_parts = kv_cut[:1] + [swapped(kv_cut[d], d) for d in far]

    sent = jnp.stack([part[4 * tok_rows :] for part in kv_parts]).astype(jnp.int32)
    marks = sent[:, :marks_rows] * 65536 + sent[:, marks_rows : 2 * marks_rows] * 256
    marks = marks + sent[:, 2 * marks_rows : 3 * marks_rows]
    from_x, from_y = swapped(normed, 1), swapped(normed, 2)
    mine_other = other_core(normed)
    (w_after,) = after([w_stacks[1]], *kv_parts)
    w_chunks.append(lax.all_gather(w_after, "ctx", axis=0, tiled=True, axis_index_groups=lines))

    half = width // 2
    relay_y, relay_x = from_y[:, :half], from_x[:, half:]
    from_x, from_y = after([from_x, from_y], kv_parts[3])
    relay_y, relay_x = after([relay_y, relay_x], *kv_parts)
    corner_a, corner_b = swapped(relay_y, 1), swapped(relay_x, 2)
    token_parts = [[normed, mine_other]] + [[from_x, other_core(from_x)], [from_y, other_core(from_y)]]

    info = jnp.stack([(index // group - 1) * rows, place, core]).astype(jnp.int32)
    width_mask = tile_mask.shape[1]

    def call(distances, chunk, *earlier):
        chosen = [token_parts[d] for d in distances]
        (start,) = after([info], *earlier)
        return attend(start, marks, distances, chosen, chunk, kv_parts, 2, width_mask)

    pieces, last = {}, ()
    for chunk, distances in ((0, (2, 1, 0)), (0, (3,)), (1, (3, 2, 1)), (1, (0,))):
        if distances == (3,):
            corner = jnp.concatenate(after([corner_a, corner_b], *last), axis=1)
            token_parts.append([corner, other_core(corner)])
        outs = call(distances, w_chunks[chunk], *last)
        last = outs[:1]
        pieces.update({(d, chunk): swapped(out, d) if d else out for d, out in zip(distances, outs)})
    return joined(info, pieces, q_width, [low for low, _ in cuts], group * q_width)


def joined(info, pieces, q_width, lows, columns):
    keys = sorted(pieces)
    rows = pieces[keys[0]].shape[0]
    vmem = pl.BlockSpec(memory_space=pltpu.VMEM)

    def kernel(info_ref, *refs):
        out_ref = refs[-1]
        for k, (distance, chunk) in enumerate(keys):
            at = pl.multiple_of(lax.bitwise_xor(info_ref[1], distance) * q_width + lows[chunk], HD)
            out_ref[:, pl.ds(at, refs[k].shape[1])] = refs[k][...]

    return pl.pallas_call(
        kernel,
        out_shape=jax.ShapeDtypeStruct((rows, columns), jnp.bfloat16),
        in_specs=[pl.BlockSpec(memory_space=pltpu.SMEM)] + [vmem] * len(keys),
        out_specs=vmem,
        cost_estimate=pl.CostEstimate(flops=0, bytes_accessed=4 * rows * columns, transcendentals=0),
    )(info, *[pieces[key] for key in keys])


def plain(tokens, norm_gain, w_query, cache_keys, cache_values, doc_start, tile_mask):
    devices = lax.axis_size("ctx")
    index = lax.axis_index("ctx")
    tok_rows = tokens.shape[0]
    float_tokens = lax.all_gather(tokens, "tp", axis=1, tiled=True).astype(jnp.float32)
    inverse = lax.rsqrt(jnp.mean(float_tokens * float_tokens, axis=-1, keepdims=True) + epsilon)
    normed = (float_tokens * inverse * norm_gain).astype(jnp.bfloat16)
    kv_heads = cache_keys.shape[1] // HD
    q_width = w_query.shape[1] // kv_heads
    w_blocks = lax.all_gather(w_query, "ctx", axis=0)
    reach = (MAXDOC + tok_rows - 2) // tok_rows
    kv_own = jnp.stack([cache_keys, cache_values])
    shards = [
        lax.ppermute(kv_own, "ctx", [(i, i + distance) for i in range(devices - distance)])
        for distance in range(reach, 0, -1)
    ]
    kv_window = jnp.stack(shards + [kv_own])
    info = jnp.stack([(index - reach) * tok_rows, jnp.int32(0), jnp.int32(0)]).astype(jnp.int32)
    marks = marks_of(doc_start, tile_mask)[None]
    outs = [
        attend(
            info,
            marks,
            (0,),
            [[normed]],
            w_blocks[:, :, head * q_width : (head + 1) * q_width],
            [kv_window[:, :, :, head * HD : (head + 1) * HD].reshape(-1, HD)],
            reach + 1,
            tile_mask.shape[1],
        )[0]
        for head in range(kv_heads)
    ]
    return outs[0] if kv_heads == 1 else jnp.concatenate(outs, axis=1)


def on_device(*arrays):
    kv_heads = arrays[3].shape[1] // HD
    group = 4
    rows = group * arrays[0].shape[0]
    if kv_heads == group and lax.axis_size("ctx") % group == 0 and lax.axis_size("tp") == 2 and rows >= MAXDOC - 1:
        return planar(*arrays, group)
    return plain(*arrays)


def solution(mesh):
    return jax.shard_map(
        on_device,
        mesh=mesh,
        in_specs=(
            P("ctx", "tp"),
            P(),
            P("ctx", "tp"),
            P("ctx", "tp"),
            P("ctx", "tp"),
            P("ctx"),
            P("ctx", None),
        ),
        out_specs=P("ctx", "tp"),
        check_vma=False,
    )
```

```python
import math

import jax
import jax.numpy as jnp
from jax import lax
from jax.experimental import pallas as pl
from jax.experimental.pallas import tpu as pltpu
from jax.sharding import PartitionSpec as P

HD = 128
TILE = 128
MAXDOC = 2048
KEYS = 512
QUERIES = 256
CHUNKS = 2
FAR = 1 << 30
MASKED = -1e30


epsilon = 1e-05
exp2_scale = math.log2(math.e) / HD**0.5


def rows_kernel(counts, distances, shapes, info, marks_smem, marks_ref, *refs):
    parts, kv_count, halves, mask_width = counts
    tok_rows, shard_rows, source_rows = shapes
    n = len(distances)
    token_hbm = [refs[k * parts : (k + 1) * parts] for k in range(n)]
    w_hbm = refs[n * parts]
    kv_hbm = refs[n * parts + 1 :][:kv_count]
    out_hbm = refs[n * parts + 1 + kv_count :][:n]
    scratch = refs[n * parts + 1 + kv_count + n :]
    token_ref, w_ref, key_ref, value_ref, total_ref, query_ref, doc_full, acc_ref, max_ref, sum_ref, out_ref = scratch[:11]
    token_sem, w_sem, kv_sem, out_sem = scratch[11:]
    columns = w_ref.shape[1]
    heads = columns // HD
    depth = w_ref.shape[0]
    blocks = depth // source_rows
    swap = info[1]
    chunk = depth // CHUNKS
    chunks_part = CHUNKS // parts
    doc_rows = tok_rows // TILE
    window_rows = halves * kv_count * shard_rows
    base = window_rows - kv_count * shard_rows

    def token_copy(ref, at, c, slot):
        return pltpu.make_async_copy(
            ref.at[:, at * chunk : (at + 1) * chunk],
            token_ref.at[slot, :, c * chunk : (c + 1) * chunk],
            token_sem.at[slot, c],
        )

    def fetch_tokens(k, c):
        token_copy(token_hbm[k][c // chunks_part], c % chunks_part, c, k % 2).start()

    def rows_of(c):
        return lax.bitwise_xor(info[2], c // chunks_part) * chunks_part + c % chunks_part

    def w_copy(at, place):
        target = pl.ds(pl.multiple_of(place * source_rows, 16), source_rows)
        return pltpu.make_async_copy(w_hbm.at[at], w_ref.at[target], w_sem.at[place])

    blocks_chunk = blocks // CHUNKS

    def kv_copy(ref, half, which, place):
        target = pl.ds(pl.multiple_of(KEYS + place * shard_rows, 16), shard_rows)
        return pltpu.make_async_copy(
            ref.at[pl.ds((half * 2 + which) * shard_rows, shard_rows), :],
            (key_ref, value_ref)[which].at[target],
            kv_sem.at[place, which],
        )

    def out_copy(k, slot):
        return pltpu.make_async_copy(out_ref.at[slot], out_hbm[k], out_sem.at[slot])

    for c in range(CHUNKS):
        fetch_tokens(0, c)
        for at in range(blocks_chunk):
            place = rows_of(c) * blocks_chunk + at
            w_copy(lax.bitwise_xor(swap, place), place).start()
    for at in range(kv_count):
        for half in range(halves):
            for which in range(2):
                kv_copy(kv_hbm[at], half, which, half * kv_count + lax.bitwise_xor(swap, at)).start()
    key_ref[0:KEYS, :] = jnp.zeros((KEYS, HD), jnp.bfloat16)
    value_ref[0:KEYS, :] = jnp.zeros((KEYS, HD), jnp.bfloat16)

    stacked = heads * QUERIES
    subs = QUERIES // TILE

    def one_rows(k, carry):
        slot = lax.rem(k, 2)
        for ahead in range(1, n):

            @pl.when(k == ahead - 1)
            def _():
                for c in range(CHUNKS):
                    fetch_tokens(ahead, c)

        for c in range(CHUNKS):
            token_copy(token_hbm[0][0], 0, c, slot).wait()

            @pl.when(k == 0)
            def _():
                for at in range(blocks_chunk):
                    w_copy(0, rows_of(c) * blocks_chunk + at).wait()

            for first in range(0, tok_rows, QUERIES):
                piece = jnp.dot(
                    token_ref[slot, first : first + QUERIES, c * chunk : (c + 1) * chunk],
                    w_ref[pl.ds(pl.multiple_of(rows_of(c) * chunk, 16), chunk), :],
                    preferred_element_type=jnp.float32,
                )
                if c == 0:
                    total_ref[first : first + QUERIES, :] = piece
                else:
                    total_ref[first : first + QUERIES, :] += piece
        for tile in range(tok_rows // QUERIES):
            for head in range(heads):
                at = (tile * heads + head) * QUERIES
                query_ref[at : at + QUERIES, :] = total_ref[
                    tile * QUERIES : (tile + 1) * QUERIES, head * HD : (head + 1) * HD
                ].astype(jnp.bfloat16)

        @pl.when(k == 0)
        def _():
            for place in range(kv_count * halves):
                for which in range(2):
                    kv_copy(kv_hbm[0], 0, which, place).wait()

        @pl.when(k >= 2)
        def _():
            out_copy(0, slot).wait()

        distance = jnp.int32(distances[0])
        for other in range(1, n):
            distance = jnp.where(k == other, distances[other], distance)
        rows_first = base + lax.bitwise_xor(swap, distance) * tok_rows

        def one_tile(tile, carry):
            query = query_ref[pl.ds(pl.multiple_of(tile * stacked, stacked), stacked), :]
            row_first = rows_first + tile * QUERIES
            end = row_first + QUERIES
            for sub in range(subs):
                docs_row = marks_ref[distance, pl.ds(tile * subs + sub, 1), :].astype(jnp.float32)
                doc_full[sub] = jnp.transpose(jnp.broadcast_to(docs_row, (TILE, TILE))).astype(jnp.int32)
            first_key = marks_smem[distance, tile * subs, 0] - info[0]
            count = (end - first_key + KEYS - 1) // KEYS

            def one_block(back, carry):
                start = end - (back + 1) * KEYS
                at = pl.multiple_of(start + KEYS, TILE)
                keys = key_ref[pl.ds(at, KEYS), :]
                values = value_ref[pl.ds(at, KEYS), :]
                key_tile = (info[0] + start) // TILE
                lane = lax.broadcasted_iota(jnp.int32, (TILE, TILE), 1)
                row = lax.broadcasted_iota(jnp.int32, (TILE, TILE), 0)
                bias_rows = []
                for sub in range(subs):
                    causal = row + (row_first + sub * TILE - start)
                    docs = doc_full[sub] - (info[0] + start)
                    pieces = []
                    for m in range(KEYS // TILE):
                        column = lax.min(lax.max(key_tile + m, 0), mask_width - 1)
                        flat = (tile * subs + sub) * mask_width + column
                        shut = jnp.where(marks_smem[distance, doc_rows + flat // TILE, lax.rem(flat, TILE)] == 1, 0, FAR)
                        seen = (lane <= causal - m * TILE) & (lane >= docs + (shut - m * TILE))
                        pieces.append(jnp.where(seen, 0.0, MASKED))
                    bias_rows.append(jnp.concatenate(pieces, axis=1))
                bias = jnp.concatenate(bias_rows, axis=0)
                spans = [slice(head * QUERIES, (head + 1) * QUERIES) for head in range(heads)]
                scores = [
                    bias
                    + lax.dot_general(
                        query[span], keys, (((1,), (1,)), ((), ())), preferred_element_type=jnp.float32
                    )
                    for span in spans
                ]
                olds = [max_ref[span, :] for span in spans]
                news = [jnp.maximum(old, jnp.max(x, axis=1, keepdims=True)) for old, x in zip(olds, scores)]
                for span, x, old, new in zip(spans, scores, olds, news):
                    alpha = jnp.exp2((old - new) * exp2_scale)
                    shift = jnp.concatenate([new * exp2_scale] * (KEYS // HD), axis=1)
                    weights = jnp.exp2(x * exp2_scale - shift)
                    max_ref[span, :] = new
                    folded = weights[:, :HD]
                    for m in range(1, KEYS // HD):
                        folded = folded + weights[:, m * HD : (m + 1) * HD]
                    sum_ref[span, :] = sum_ref[span, :] * alpha + folded
                    product = jnp.dot(weights.astype(jnp.bfloat16), values, preferred_element_type=jnp.float32)
                    acc_ref[span, :] = acc_ref[span, :] * alpha + product
                return carry

            max_ref[...] = jnp.full(max_ref.shape, MASKED, jnp.float32)
            sum_ref[...] = jnp.zeros(sum_ref.shape, jnp.float32)
            acc_ref[...] = jnp.zeros(acc_ref.shape, jnp.float32)
            lax.fori_loop(0, count, one_block, 0)
            result = acc_ref[...] / jnp.sum(sum_ref[...], axis=1, keepdims=True)
            for head in range(heads):
                out_ref[slot, pl.ds(pl.multiple_of(tile * QUERIES, QUERIES), QUERIES), head * HD : (head + 1) * HD] = (
                    result[head * QUERIES : (head + 1) * QUERIES].astype(out_ref.dtype)
                )
            return carry

        lax.fori_loop(0, tok_rows // QUERIES, one_tile, 0)
        for at in range(n):

            @pl.when(k == at)
            def _():
                out_copy(at, at % 2).start()

        return carry

    lax.fori_loop(0, n, one_rows, 0)
    for k in range(max(n - 2, 0), n):
        out_copy(k, k % 2).wait()


def attend(info, marks, distances, token_parts, w_blocks, kv_parts, halves, mask_width):
    n = len(distances)
    parts = len(token_parts[0])
    rows = token_parts[0][0].shape[0]
    source_rows, columns = w_blocks.shape[1:]
    depth = w_blocks.shape[0] * source_rows
    heads = columns // HD
    shard_rows = kv_parts[0].shape[0] // (2 * halves) // TILE * TILE
    shards = len(kv_parts) * halves
    vmem = pl.BlockSpec(memory_space=pltpu.VMEM)
    smem = pl.BlockSpec(memory_space=pltpu.SMEM)
    leave = pl.BlockSpec(memory_space=pl.ANY)
    arrays = [part for block in token_parts for part in block] + [w_blocks] + list(kv_parts)
    counts = (parts, len(kv_parts), halves, mask_width)
    tile_rows = heads * QUERIES

    def kernel(*refs):
        rows_kernel(counts, distances, (rows, shard_rows, source_rows), *refs)

    return pl.pallas_call(
        kernel,
        out_shape=[jax.ShapeDtypeStruct((rows, columns), jnp.bfloat16)] * n,
        in_specs=[smem, smem, vmem] + [leave] * len(arrays),
        out_specs=[leave] * n,
        scratch_shapes=[
            pltpu.VMEM((2, rows, depth), jnp.bfloat16),
            pltpu.VMEM((depth, columns), jnp.bfloat16),
            pltpu.VMEM((KEYS + shards * shard_rows, HD), jnp.bfloat16),
            pltpu.VMEM((KEYS + shards * shard_rows, HD), jnp.bfloat16),
            pltpu.VMEM((rows, columns), jnp.float32),
            pltpu.VMEM((rows * heads, HD), jnp.bfloat16),
            pltpu.VMEM((QUERIES // TILE, TILE, TILE), jnp.int32),
            pltpu.VMEM((tile_rows, HD), jnp.float32),
            pltpu.VMEM((tile_rows, HD), jnp.float32),
            pltpu.VMEM((tile_rows, HD), jnp.float32),
            pltpu.VMEM((2, rows, columns), jnp.bfloat16),
            pltpu.SemaphoreType.DMA((2, CHUNKS)),
            pltpu.SemaphoreType.DMA((w_blocks.shape[0],)),
            pltpu.SemaphoreType.DMA((shards, 2)),
            pltpu.SemaphoreType.DMA((2,)),
        ],
        compiler_params=pltpu.CompilerParams(vmem_limit_bytes=60 << 20),
        cost_estimate=pl.CostEstimate(
            flops=n * (2 * rows * depth * columns + 4 * rows * columns * 1024),
            bytes_accessed=2 * (n * rows * depth + depth * columns + shards * 2 * shard_rows * HD + n * rows * columns),
            transcendentals=n * rows * heads * 1024,
        ),
    )(info, marks, marks, *arrays)


def marks_of(doc_start, tile_mask):
    return jnp.concatenate([doc_start.reshape(-1, TILE), tile_mask.reshape(-1, TILE)])


def planar(tokens, norm_gain, w_query, cache_keys, cache_values, doc_start, tile_mask, group):
    devices = lax.axis_size("ctx")
    index = lax.axis_index("ctx")
    core = lax.axis_index("tp")
    place = lax.rem(index, group)
    tok_rows, width = tokens.shape
    kv_width = cache_keys.shape[1] // group
    q_width = w_query.shape[1] // group
    rows = group * tok_rows
    lines = [[first + k for first in range(0, devices, group)] for k in range(group)]
    far = range(1, group)

    def swapped(block, distance):
        return lax.ppermute(block, "ctx", [(i, i ^ distance) for i in range(devices)])

    def other_core(block):
        return lax.ppermute(block, "tp", [(0, 1), (1, 0)])

    def columns_for(array, distance, first, size, of, axis):
        at = lax.bitwise_xor(place, distance) * of + first
        return lax.dynamic_slice_in_dim(array, at, size, axis)

    def after(values, *earlier):
        flat = lax.optimization_barrier((tuple(values), tuple(earlier)))
        return list(flat[0])

    first_columns = (q_width // HD + 1) // 2 * HD
    cuts = ((0, first_columns), (first_columns, q_width))

    w_cut = [columns_for(w_query, d, 0, q_width, q_width, 1) for d in range(group)]
    kv_own = jnp.stack(after([cache_keys, cache_values], *w_cut))
    kv_before = lax.ppermute(kv_own, "ctx", [(i, i + group) for i in range(devices - group)])
    w_plane = w_cut[:1] + [swapped(w_cut[d], d) for d in far]
    float_tokens = tokens.astype(jnp.float32)
    squares = jnp.sum(float_tokens * float_tokens, axis=-1)
    squares = squares + other_core(squares)
    inverse = lax.rsqrt(squares / (2 * width) + epsilon)
    gain = lax.dynamic_slice_in_dim(norm_gain, core * width, width, 0)
    normed = (float_tokens * inverse[:, None] * gain).astype(jnp.bfloat16)

    w_plane = after(w_plane, kv_before, normed)
    w_stacks = [jnp.stack([block[:, low:high] for block in w_plane]) for low, high in cuts]
    w_chunks = [lax.all_gather(w_stacks[0], "ctx", axis=0, tiled=True, axis_index_groups=lines)]

    marks_own = marks_of(doc_start, tile_mask)
    marks_rows = marks_own.shape[0]
    bytes_own = jnp.concatenate([marks_own >> 16, (marks_own >> 8) & 255, marks_own & 255]).astype(jnp.bfloat16)
    bytes_own = jnp.pad(bytes_own, ((0, -bytes_own.shape[0] % 16), (0, 0)))

    def kv_for(d):
        cut = [columns_for(array, d, 0, kv_width, kv_width, 2).reshape(-1, kv_width) for array in (kv_before, kv_own)]
        return jnp.concatenate(cut + [bytes_own])

    kv_cut = after([kv_for(d) for d in range(group)], w_stacks[1])
    kv_parts = kv_cut[:1] + [swapped(kv_cut[d], d) for d in far]

    sent = jnp.stack([part[4 * tok_rows :] for part in kv_parts]).astype(jnp.int32)
    marks = sent[:, :marks_rows] * 65536 + sent[:, marks_rows : 2 * marks_rows] * 256
    marks = marks + sent[:, 2 * marks_rows : 3 * marks_rows]
    from_x, from_y = swapped(normed, 1), swapped(normed, 2)
    mine_other = other_core(normed)
    (w_after,) = after([w_stacks[1]], *kv_parts)
    w_chunks.append(lax.all_gather(w_after, "ctx", axis=0, tiled=True, axis_index_groups=lines))

    half = width // 2
    relay_y, relay_x = from_y[:, :half], from_x[:, half:]
    from_x, from_y, relay_y, relay_x = after([from_x, from_y, relay_y, relay_x], *kv_parts)
    corner_a, corner_b = swapped(relay_y, 1), swapped(relay_x, 2)
    token_parts = [[normed, mine_other]] + [[from_x, other_core(from_x)], [from_y, other_core(from_y)]]

    info = jnp.stack([(index // group - 1) * rows, place, core]).astype(jnp.int32)
    width_mask = tile_mask.shape[1]

    def call(distances, chunk, *earlier):
        chosen = [token_parts[d] for d in distances]
        (start,) = after([info], *earlier)
        return attend(start, marks, distances, chosen, chunk, kv_parts, 2, width_mask)

    pieces, last = {}, ()
    for chunk, distances in ((0, (2, 1, 0)), (0, (3,)), (1, (3, 2, 1)), (1, (0,))):
        if distances == (3,):
            corner = jnp.concatenate(after([corner_a, corner_b], *last), axis=1)
            token_parts.append([corner, other_core(corner)])
        outs = call(distances, w_chunks[chunk], *last)
        last = outs[:1]
        pieces.update({(d, chunk): swapped(out, d) if d else out for d, out in zip(distances, outs)})
    return joined(info, pieces, q_width, [low for low, _ in cuts], group * q_width)


def joined(info, pieces, q_width, lows, columns):
    keys = sorted(pieces)
    rows = pieces[keys[0]].shape[0]
    vmem = pl.BlockSpec(memory_space=pltpu.VMEM)

    def kernel(info_ref, *refs):
        out_ref = refs[-1]
        for k, (distance, chunk) in enumerate(keys):
            at = pl.multiple_of(lax.bitwise_xor(info_ref[1], distance) * q_width + lows[chunk], HD)
            out_ref[:, pl.ds(at, refs[k].shape[1])] = refs[k][...]

    return pl.pallas_call(
        kernel,
        out_shape=jax.ShapeDtypeStruct((rows, columns), jnp.bfloat16),
        in_specs=[pl.BlockSpec(memory_space=pltpu.SMEM)] + [vmem] * len(keys),
        out_specs=vmem,
        cost_estimate=pl.CostEstimate(flops=0, bytes_accessed=4 * rows * columns, transcendentals=0),
    )(info, *[pieces[key] for key in keys])


def plain(tokens, norm_gain, w_query, cache_keys, cache_values, doc_start, tile_mask):
    devices = lax.axis_size("ctx")
    index = lax.axis_index("ctx")
    tok_rows = tokens.shape[0]
    float_tokens = lax.all_gather(tokens, "tp", axis=1, tiled=True).astype(jnp.float32)
    inverse = lax.rsqrt(jnp.mean(float_tokens * float_tokens, axis=-1, keepdims=True) + epsilon)
    normed = (float_tokens * inverse * norm_gain).astype(jnp.bfloat16)
    kv_heads = cache_keys.shape[1] // HD
    q_width = w_query.shape[1] // kv_heads
    w_blocks = lax.all_gather(w_query, "ctx", axis=0)
    reach = (MAXDOC + tok_rows - 2) // tok_rows
    kv_own = jnp.stack([cache_keys, cache_values])
    shards = [
        lax.ppermute(kv_own, "ctx", [(i, i + distance) for i in range(devices - distance)])
        for distance in range(reach, 0, -1)
    ]
    kv_window = jnp.stack(shards + [kv_own])
    info = jnp.stack([(index - reach) * tok_rows, jnp.int32(0), jnp.int32(0)]).astype(jnp.int32)
    marks = marks_of(doc_start, tile_mask)[None]
    outs = [
        attend(
            info,
            marks,
            (0,),
            [[normed]],
            w_blocks[:, :, head * q_width : (head + 1) * q_width],
            [kv_window[:, :, :, head * HD : (head + 1) * HD].reshape(-1, HD)],
            reach + 1,
            tile_mask.shape[1],
        )[0]
        for head in range(kv_heads)
    ]
    return outs[0] if kv_heads == 1 else jnp.concatenate(outs, axis=1)


def on_device(*arrays):
    kv_heads = arrays[3].shape[1] // HD
    group = 4
    rows = group * arrays[0].shape[0]
    if kv_heads == group and lax.axis_size("ctx") % group == 0 and lax.axis_size("tp") == 2 and rows >= MAXDOC - 1:
        return planar(*arrays, group)
    return plain(*arrays)


def solution(mesh):
    return jax.shard_map(
        on_device,
        mesh=mesh,
        in_specs=(
            P("ctx", "tp"),
            P(),
            P("ctx", "tp"),
            P("ctx", "tp"),
            P("ctx", "tp"),
            P("ctx"),
            P("ctx", None),
        ),
        out_specs=P("ctx", "tp"),
        check_vma=False,
    )
```
